128 devices in a mesh: dp: 8 (over z_hi, x), fsdp: 16 (over z_lo, y, core).
Axes of the slice: x: 4, y: 4, z: 4 (z_hi: 2, z_lo: 2; z = z_hi * 2 + z_lo), core: 2. Of those that a mesh axis runs over, the one named last changes fastest.
Arguments:
- long_in: bfloat16 [65536, 768], P(('dp', 'fsdp')), may hold values from -6 to 6
- glob_in: bfloat16 [4096, 768], P(('dp', 'fsdp')), may hold values from -6 to 6
- cot_long: bfloat16 [65536, 768], P(('dp', 'fsdp')), may hold values from -6 to 6
- cot_glob: bfloat16 [4096, 768], P(('dp', 'fsdp')), may hold values from -6 to 6
- teacher: bfloat16 [65536, 768], P(('dp', 'fsdp')), may hold values from -12 to 12
- w_qkv: bfloat16 [768, 2304], P(('dp', 'fsdp')), may hold values from -0.21875 to 0.21875
- w_attn: bfloat16 [768, 768], P(('dp', 'fsdp')), may hold values from -0.875 to 0.875
- w_in: bfloat16 [768, 3072], P(('dp', 'fsdp')), may hold values from -0.21875 to 0.21875
- w_out: bfloat16 [3072, 768], P(('dp', 'fsdp')), may hold values from -0.109375 to 0.109375
- norm_gains: bfloat16 [768, 2], P(('dp', 'fsdp')), may hold values from 0.25 to 1.75
- norm_biases: bfloat16 [768, 2], P(('dp', 'fsdp')), may hold values from -1.5 to 1.5
- rel_bias: float32 [171, 12], replicated, may hold values from -5 to 5
- lengths: int32 [32], P('dp'), may hold values from 1024 to 2048, as said below
- block_order: int32 [8, 64], P('dp'), may hold values from 0 to 63, each once within a row
- global_pos: int32 [4096], P('dp'), may hold values from 0 to 2047, as said below
- rel_labels: int32 [169], replicated, may hold values from 0 to 168, each once
- loss_mask: int32 [65536], P(('dp', 'fsdp')), may hold values 0 or 1
Outputs:
- out_long: bfloat16 [65536, 768], P(('dp', 'fsdp'))
- out_glob: bfloat16 [4096, 768], P(('dp', 'fsdp'))
- loss: float32 [], replicated
- grad_long: float32 [65536, 768], P(('dp', 'fsdp'))
- grad_glob: float32 [4096, 768], P(('dp', 'fsdp'))
- grad_qkv: float32 [768, 2304], P(('dp', 'fsdp'))
- grad_attn: float32 [768, 768], P(('dp', 'fsdp'))
- grad_in: float32 [768, 3072], P(('dp', 'fsdp'))
- grad_out: float32 [3072, 768], P(('dp', 'fsdp'))
- grad_gains: float32 [768, 2], P(('dp', 'fsdp'))
- grad_biases: float32 [768, 2], P(('dp', 'fsdp'))
- grad_rel: float32 [171, 12], replicated
The draws below stay inside these ranges and needn't reach their ends.
Inputs may be any that keep to these rules, and one draw needn't show every extreme that they name: `lengths`: a sequence's real tokens fill its first slots; at least one sequence of all has 2048. `block_order`: each row is a permutation of the group's block numbers. `global_pos`: the k-th global token of a sequence is anchored at a position from k * 16 to k * 16 + 15. `rel_labels`: a permutation of the labels.
All inputs are finite; a program needn't handle non-finite values. No bound on the sum of `loss_mask` on one device may be relied on, other than what follows from the above.
Results may differ from the reference program's by a relative error of at most 0.018.
Values may be sent and summed in bfloat16 or wider, within the bound.
No kernel may reach another device: no remote copies, remote signals or barrier semaphores. Data moves between devices by JAX's collectives and lax.ppermute only.
A program may use at most 320 MiB of HBM per device.

```python
import math
import jax
import jax.numpy as jnp
from jax import lax

D = 768
HEADS = 12
HEAD = 64
FF = 3072
RADIUS = 84
LABELS = 169
BLOCK = 128
SEQ_BLOCKS = 16
GLOBAL_EVERY = 16
LSEQ = 2048
GSEQ = 128
GROUP_BLOCKS = 64
GROUPS = 8
SEQS_GROUP = 4
SEQS = 32
TOKENS = 65536
GROUP_GLOBALS = 512
GLOBALS = 4096


def draw_lengths(key, part):
    values = jax.random.randint(key, (SEQS,), LSEQ // 2, LSEQ + 1)
    chosen = jax.random.randint(jax.random.fold_in(key, 7), (), 0, SEQS)
    return jnp.where(jnp.arange(SEQS) == chosen, LSEQ, values).astype(jnp.int32)


def draw_global_pos(key, part):
    index = jnp.arange(GLOBALS)
    offset = jax.random.randint(key, (GLOBALS,), 0, GLOBAL_EVERY)
    offset = jnp.where(index == 0, 0, offset)
    offset = jnp.where(index == GSEQ - 1, GLOBAL_EVERY - 1, offset)
    return (index % GSEQ * GLOBAL_EVERY + offset).astype(jnp.int32)


def draw_teacher(key, part):
    place = jnp.arange(TOKENS, dtype=jnp.float32) / max(TOKENS - 1, 1)
    level = 0.5 + 2.0 * place
    noise = jax.random.normal(key, (TOKENS, D), jnp.float32)
    return jnp.clip(noise * level[:, None], -12.0, 12.0).astype(jnp.bfloat16)


def plant(array, rng, least, top_value):
    longest = array.shape.index(max(array.shape))
    spots = []
    for shift in (0, 1):
        where = [jax.random.randint(jax.random.fold_in(rng, axis), (), 0, length) for axis, length in enumerate(array.shape)]
        where[longest] = (where[longest] + shift) % array.shape[longest]
        spots.append(tuple(where))
    return array.at[spots[0]].set(least).at[spots[1]].set(top_value)


def block_levels(rng, extent, cuts, least, top_value):
    factor_of = 1.0
    for dim, blocks in cuts:
        draws = jax.random.uniform(jax.random.fold_in(jax.random.fold_in(rng, 6), dim), (blocks,), jnp.float32, least / len(cuts), top_value / len(cuts))
        factor_of = factor_of * jnp.repeat(jnp.exp(draws), extent[dim] // blocks).reshape((-1,) + (1,) * (len(extent) - 1 - dim))
    return factor_of


def bell_draw(own_key, dims, scale, most, cuts=(), kind=jnp.bfloat16):
    values = scale * jax.random.normal(own_key, dims, jnp.float32)
    if cuts:
        values = values * block_levels(own_key, dims, cuts, -0.22, 0.18)
    return jnp.clip(values, -most, most).astype(kind)


def setup_inputs(seed: int = 0) -> dict:
    seeds = jax.random.split(jax.random.key(seed), 18)
    return {
        "long_in": bell_draw(seeds[0], (TOKENS, D), 1.0, 6.0, ((0, 128),)),
        "glob_in": bell_draw(seeds[1], (GLOBALS, D), 1.0, 6.0, ((0, 128),)),
        "cot_long": bell_draw(seeds[2], (TOKENS, D), 1.0, 6.0, ((0, 128),)),
        "cot_glob": bell_draw(seeds[3], (GLOBALS, D), 1.0, 6.0, ((0, 128),)),
        "teacher": draw_teacher(jax.random.fold_in(seeds[17], 71), 0),
        "w_qkv": bell_draw(seeds[5], (D, 3 * D), D ** -0.5, 0.21875, ((0, 128),)),
        "w_attn": bell_draw(seeds[6], (D, D), (D // 16) ** -0.5, 0.875, ((0, 128),)),
        "w_in": bell_draw(seeds[7], (D, FF), D ** -0.5, 0.21875, ((0, 128),)),
        "w_out": bell_draw(seeds[8], (FF, D), FF ** -0.5, 0.109375, ((0, 128),)),
        "norm_gains": jnp.clip(1.0 + 0.15 * jax.random.normal(seeds[9], (D, 2), jnp.float32), 0.25, 1.75).astype(jnp.bfloat16),
        "norm_biases": bell_draw(seeds[10], (D, 2), 0.3, 1.5, ((0, 128),)),
        "rel_bias": bell_draw(seeds[11], (LABELS + 2, HEADS), 1.0, 5.0, (), jnp.float32),
        "lengths": draw_lengths(jax.random.fold_in(seeds[17], 71), 0),
        "block_order": jax.vmap(lambda own: jax.random.permutation(own, GROUP_BLOCKS))(jax.random.split(seeds[13], GROUPS)).reshape((GROUPS, GROUP_BLOCKS)).astype(jnp.int32),
        "global_pos": draw_global_pos(jax.random.fold_in(seeds[17], 71), 0),
        "rel_labels": jax.random.permutation(seeds[15], LABELS).astype(jnp.int32),
        "loss_mask": plant((jax.random.randint(seeds[16], (TOKENS,), 0, 4) < 3).astype(jnp.int32), jax.random.fold_in(seeds[16], 1), 0, 1),
    }


@jax.custom_vjp
def low(v):
    return lax.optimization_barrier(v.astype(jnp.bfloat16)).astype(jnp.float32)

@jax.custom_vjp
def low_back(v):
    return v

def low_keep(v):
    return (low(v), None)

def low_pass(kept, grad):
    return (grad,)

def back_keep(v):
    return (v, None)

def back_low(kept, grad):
    return (low(grad),)
low.defvjp(low_keep, low_pass)
low_back.defvjp(back_keep, back_low)
EPS = 1e-05
MASKED = -1e+30
HIGHEST = lax.Precision.HIGHEST

def norm_rows(values, gain, shift):
    centre = lax.optimization_barrier(jnp.mean(values, -1, keepdims=True))
    centred = values - centre
    spread = lax.optimization_barrier(jnp.mean(centred * centred, -1, keepdims=True))
    return centred * lax.rsqrt(spread + EPS) * gain + shift

def soft_rows(scores):
    summit = lax.optimization_barrier(jnp.max(scores, -1, keepdims=True))
    powers = jnp.exp(scores - summit)
    return powers / lax.optimization_barrier(jnp.sum(powers, -1, keepdims=True))

def sequence_attention(qkv_long, qkv_glob, length, anchors, band_bias, glob_table):
    scale = 1.0 / math.sqrt(HEAD)
    width = BLOCK + 2 * RADIUS
    query = qkv_long[:, :D].reshape(LSEQ, HEADS, HEAD)
    keys = qkv_long[:, D:2 * D].reshape(LSEQ, HEADS, HEAD)
    values = qkv_long[:, 2 * D:].reshape(LSEQ, HEADS, HEAD)
    glob_query = qkv_glob[:, :D].reshape(GSEQ, HEADS, HEAD)
    glob_keys = qkv_glob[:, D:2 * D].reshape(GSEQ, HEADS, HEAD)
    glob_values = qkv_glob[:, 2 * D:].reshape(GSEQ, HEADS, HEAD)
    position = jnp.arange(LSEQ, dtype=jnp.int32)
    valid = position < length
    glob_valid = anchors < length
    owning = position[:, None] // GLOBAL_EVERY == anchors[None, :] // GLOBAL_EVERY
    glob_bias = jnp.where(owning[None], glob_table[0][:, None, None], glob_table[1][:, None, None])
    padded_keys = jnp.pad(keys, ((RADIUS, RADIUS), (0, 0), (0, 0)))
    padded_values = jnp.pad(values, ((RADIUS, RADIUS), (0, 0), (0, 0)))
    padded_valid = jnp.pad(valid, (RADIUS, RADIUS))
    starts = jnp.arange(SEQ_BLOCKS, dtype=jnp.int32) * BLOCK
    window_index = starts[:, None] + jnp.arange(width, dtype=jnp.int32)[None, :]
    window_keys = padded_keys[window_index]
    window_values = padded_values[window_index]
    window_valid = padded_valid[window_index]
    block_query = query.reshape(SEQ_BLOCKS, BLOCK, HEADS, HEAD)
    offsets = jnp.arange(width, dtype=jnp.int32)[None, :] - jnp.arange(BLOCK, dtype=jnp.int32)[:, None]
    inside = (offsets >= 0) & (offsets <= 2 * RADIUS)
    local = jnp.einsum('bihd,bthd->bhit', block_query, window_keys, precision=HIGHEST) * scale + band_bias[None]
    remote_bias = jnp.transpose(glob_bias.reshape(HEADS, SEQ_BLOCKS, BLOCK, GSEQ), (1, 0, 2, 3))
    remote = jnp.einsum('bihd,ghd->bhig', block_query, glob_keys, precision=HIGHEST) * scale + remote_bias
    scores = low_back(jnp.concatenate([local, remote], -1))
    allowed = jnp.concatenate([jnp.broadcast_to(inside[None, None] & window_valid[:, None, None, :], local.shape), jnp.broadcast_to(glob_valid[None, None, None, :], remote.shape)], -1)
    probs = low(soft_rows(jnp.where(allowed, scores, MASKED)))
    long_out = jnp.einsum('bhit,bthd->bihd', probs[..., :width], window_values, precision=HIGHEST) + jnp.einsum('bhig,ghd->bihd', probs[..., width:], glob_values, precision=HIGHEST)
    long_out = low_back(low(long_out.reshape(LSEQ, D)))
    self_part = jnp.einsum('ihd,jhd->hij', glob_query, glob_keys, precision=HIGHEST) * scale
    cross_part = jnp.einsum('ihd,jhd->hij', glob_query, keys, precision=HIGHEST) * scale + jnp.transpose(glob_bias, (0, 2, 1))
    glob_scores = low_back(jnp.concatenate([self_part, cross_part], -1))
    glob_allowed = jnp.concatenate([jnp.broadcast_to(glob_valid[None, None, :], self_part.shape), jnp.broadcast_to(valid[None, None, :], cross_part.shape)], -1)
    glob_probs = low(soft_rows(jnp.where(glob_allowed, glob_scores, MASKED)))
    glob_out = jnp.einsum('hij,jhd->ihd', glob_probs[..., :GSEQ], glob_values, precision=HIGHEST) + jnp.einsum('hij,jhd->ihd', glob_probs[..., GSEQ:], values, precision=HIGHEST)
    glob_out = low_back(low(glob_out.reshape(GSEQ, D)))
    return (long_out, glob_out)

def group_forward(weights, band_bias, glob_table, long_group, glob_group, order_group, length_group, anchor_group):
    qkv_weight, attn_weight, in_weight, out_weight, gain_table, shift_table = weights
    split = GROUP_BLOCKS * BLOCK
    inverse = jnp.zeros((GROUP_BLOCKS,), jnp.int32).at[order_group].set(jnp.arange(GROUP_BLOCKS, dtype=jnp.int32))
    natural = long_group.reshape(GROUP_BLOCKS, BLOCK, D)[inverse].reshape(split, D)
    stacked = jnp.concatenate([natural, glob_group], 0)
    acts = low(norm_rows(stacked, gain_table[:, 0], shift_table[:, 0]))
    projected = low_back(low(jnp.dot(acts, qkv_weight, precision=HIGHEST)))
    long_proj = projected[:split].reshape(SEQS_GROUP, LSEQ, 3 * D)
    glob_proj = projected[split:].reshape(SEQS_GROUP, GSEQ, 3 * D)

    def attend(item):
        return sequence_attention(item[0], item[1], item[2], item[3], band_bias, glob_table)
    long_out, glob_out = lax.map(jax.checkpoint(attend), (long_proj, glob_proj, length_group, anchor_group.reshape(SEQS_GROUP, GSEQ)))
    mixed = jnp.concatenate([long_out.reshape(split, D), glob_out.reshape(SEQS_GROUP * GSEQ, D)], 0)
    middle = stacked + low_back(jnp.dot(mixed, attn_weight, precision=HIGHEST))
    normed = low(norm_rows(middle, gain_table[:, 1], shift_table[:, 1]))
    inner = low_back(jnp.dot(normed, in_weight, precision=HIGHEST))
    hidden = low(jax.nn.gelu(inner, approximate=False))
    result = middle + low_back(jnp.dot(hidden, out_weight, precision=HIGHEST))
    long_result = result[:split].reshape(GROUP_BLOCKS, BLOCK, D)[order_group].reshape(split, D)
    return (long_result, result[split:])

def reference(long_in, glob_in, cot_long, cot_glob, teacher, w_qkv, w_attn, w_in, w_out, norm_gains, norm_biases, rel_bias, lengths, block_order, global_pos, rel_labels, loss_mask):
    group_count = block_order.shape[0]
    split = GROUP_BLOCKS * BLOCK
    width = BLOCK + 2 * RADIUS
    length_table = lengths.reshape(group_count, SEQS_GROUP)
    block_length = jnp.take_along_axis(length_table, block_order // SEQ_BLOCKS, 1)
    positions = (block_order % SEQ_BLOCKS)[:, :, None] * BLOCK + jnp.arange(BLOCK, dtype=jnp.int32)[None, None, :]
    weighting = ((positions < block_length[:, :, None]) & (loss_mask.reshape(group_count, GROUP_BLOCKS, BLOCK) == 1)).astype(jnp.float32).reshape(group_count, split)
    count = jnp.sum(weighting)
    teacher_groups = teacher.astype(jnp.float32).reshape(group_count, split, D)
    anchors = global_pos.reshape(group_count, GROUP_GLOBALS)
    offsets = jnp.arange(width, dtype=jnp.int32)[None, :] - jnp.arange(BLOCK, dtype=jnp.int32)[:, None]
    clipped = jnp.clip(offsets, 0, 2 * RADIUS)

    def forward(long_state, glob_state, qkv_weight, attn_weight, in_weight, out_weight, gain_table, shift_table, rel_table):
        label_table = rel_table[rel_labels]
        band_bias = jnp.transpose(label_table[clipped], (2, 0, 1))
        glob_table = rel_table[LABELS:]
        weights = (qkv_weight, attn_weight, in_weight, out_weight, gain_table, shift_table)

        def step(total, item):
            long_group, glob_group, order_group, length_group, anchor_group, teach_group, weight_group = item
            long_result, glob_result = jax.checkpoint(group_forward)(weights, band_bias, glob_table, long_group, glob_group, order_group, length_group, anchor_group)
            error = long_result - teach_group
            return (total + jnp.sum(weight_group[:, None] * error * error), (long_result, glob_result))
        total, (long_all, glob_all) = lax.scan(step, jnp.zeros((), jnp.float32), (long_state.reshape(group_count, split, D), glob_state.reshape(group_count, GROUP_GLOBALS, D), block_order, length_table, anchors, teacher_groups, weighting))
        return (long_all.reshape(TOKENS, D), glob_all.reshape(GLOBALS, D), total / count)
    primals = (long_in.astype(jnp.float32), glob_in.astype(jnp.float32), w_qkv.astype(jnp.float32), w_attn.astype(jnp.float32), w_in.astype(jnp.float32), w_out.astype(jnp.float32), norm_gains.astype(jnp.float32), norm_biases.astype(jnp.float32), rel_bias.astype(jnp.float32))
    outputs, pullback = jax.vjp(forward, *primals)
    grads = pullback((cot_long.astype(jnp.float32), cot_glob.astype(jnp.float32), jnp.ones((), jnp.float32)))
    return (outputs[0].astype(jnp.bfloat16), outputs[1].astype(jnp.bfloat16), outputs[2], grads[0], grads[1], grads[2], grads[3], grads[4], grads[5], grads[6], grads[7], grads[8])
```

```python
import math

import jax
import jax.numpy as jnp
from jax import lax
from jax.sharding import PartitionSpec as P

D = 768
HEADS = 12
HEAD = 64
RADIUS = 84
LABELS = 169
BLOCK = 128
SEQ_BLOCKS = 16
GLOBAL_EVERY = 16
GSEQ = 128
ROWS = 512
EXT = 896
EPS = 1e-05
MASKED = -1e30
HIGHEST = lax.Precision.HIGHEST
BOTH = ("dp", "fsdp")
f32 = jnp.float32
bf16 = jnp.bfloat16

QUADS = [[4 * i + j for j in range(4)] for i in range(4)]
SAME_CORE = [[4 * g + 2 * p + c for p in range(2) for g in range(32)] for c in range(2)]
SWAP = [(i, i ^ 1) for i in range(16)]
TO_RIGHT = [(i, i + 1) for i in range(16) if i % 4 < 3]
TO_LEFT = [(i, i - 1) for i in range(16) if i % 4 > 0]


def exchange(value, axis, groups=None):
    return lax.all_to_all(value, axis, 0, 0, axis_index_groups=groups, tiled=True)


def swap(value):
    return lax.ppermute(value, "fsdp", SWAP)


def pieces(rows):
    width = rows.shape[-1]
    return rows.reshape(4, 16, 8, width).transpose(1, 0, 2, 3).reshape(64, 8, width)


def unpieces(value):
    width = value.shape[-1]
    return value.reshape(16, 4, 8, width).transpose(1, 0, 2, 3).reshape(ROWS, width)


def reorder(rows, index):
    spread = exchange(pieces(rows), "fsdp")
    return unpieces(exchange(spread[index], "fsdp"))


def norm_rows(values, gain, shift):
    centre = jnp.mean(values, -1, keepdims=True)
    centred = values - centre
    spread = jnp.mean(centred * centred, -1, keepdims=True)
    factor = lax.rsqrt(spread + EPS)
    normal = centred * factor
    return (normal * gain + shift, normal, factor)


def norm_back(grad, normal, factor, gain):
    scaled = grad * gain
    first = jnp.mean(scaled, -1, keepdims=True)
    second = jnp.mean(scaled * normal, -1, keepdims=True)
    return factor * (scaled - first - normal * second)


def split3(value):
    high = value.astype(bf16)
    rest = value - high.astype(f32)
    mid = rest.astype(bf16)
    low = (rest - mid.astype(f32)).astype(bf16)
    return jnp.concatenate([high, mid, low], -1)


def join3(value, count):
    value = value.astype(f32)
    return value[..., :count] + value[..., count : 2 * count] + value[..., 2 * count : 3 * count]


def dot(a, b):
    return jnp.dot(a, b, preferred_element_type=f32)


def reduce_columns(grad, core):
    keep = lax.dynamic_index_in_dim(grad, core, 1, keepdims=False)
    send = lax.dynamic_index_in_dim(grad, 1 - core, 1, keepdims=False)
    total = keep + swap(send.astype(bf16)).astype(f32)
    parts = exchange(total.astype(bf16).reshape(64, 24, D), BOTH, SAME_CORE)
    mine = jnp.sum(parts.astype(f32), 0)
    return exchange(mine.reshape(4, 6, D), "fsdp", QUADS)


def shards(
    long_in,
    glob_in,
    cot_long,
    cot_glob,
    teacher,
    w_qkv,
    w_attn,
    w_in,
    w_out,
    norm_gains,
    norm_biases,
    rel_bias,
    lengths,
    block_order,
    global_pos,
    rel_labels,
    loss_mask,
):
    scale = 1.0 / math.sqrt(HEAD)
    member = lax.axis_index("fsdp")
    core = member % 2
    quarter = member % 4
    seq = member // 4
    order = block_order[0]
    slots = jnp.arange(64)
    inverse = jnp.sum(jnp.where(order[None, :] == slots[:, None], slots[None, :], 0), 1)
    length = jnp.sum(jnp.where(jnp.arange(4) == seq, lengths, 0))
    anchors = lax.dynamic_slice_in_dim(global_pos, seq * GSEQ, GSEQ)

    my_ids = lax.dynamic_slice_in_dim(order, member * 4, 4)
    my_lens = jnp.sum(
        jnp.where(my_ids[:, None] // SEQ_BLOCKS == jnp.arange(4)[None, :], lengths[None, :], 0), 1
    )
    slot_pos = (my_ids % SEQ_BLOCKS)[:, None] * BLOCK + jnp.arange(BLOCK)[None, :]
    slot_weight = ((slot_pos < my_lens[:, None]).reshape(ROWS) & (loss_mask == 1)).astype(jnp.int32)
    my_count = jnp.sum(slot_weight)

    high = (my_count // 16).astype(bf16)
    low = (my_count % 16).astype(bf16)
    extra = jnp.concatenate(
        [
            norm_gains,
            norm_biases,
            jnp.broadcast_to(jnp.stack([high, low]), (6, 2)),
            jnp.zeros((6, 122), bf16),
        ],
        1,
    )
    first = lax.all_gather(
        jnp.concatenate([w_qkv, w_attn, extra], 1), "fsdp", axis_index_groups=QUADS, axis=0, tiled=True
    )
    second = lax.all_gather(w_in, "fsdp", axis_index_groups=QUADS, axis=0, tiled=True)
    first_part = jnp.concatenate(
        [lax.dynamic_slice_in_dim(first, quarter * D, D, 1), first[:, 4 * D :]], 1
    )
    second_part = lax.dynamic_slice_in_dim(second, quarter * D, D, 1)
    mine_one = exchange(
        jnp.broadcast_to(first_part[None], (64, 24, EXT)), BOTH, SAME_CORE
    ).reshape(2, D, EXT)
    other_one = swap(mine_one[..., :D])
    extras = mine_one[..., D:].reshape(2, 32, 24, 128)[0].reshape(D, 128)
    del extras
    side = mine_one[0, :, D:].astype(f32)
    even = jnp.where(core == 0, mine_one[..., :D], other_one)
    odd = jnp.where(core == 0, other_one, mine_one[..., :D])
    wq, wv = even[0], even[1]
    wk, wa = odd[0], odd[1]
    gain1, gain2, shift1, shift2 = side[:, 0], side[:, 1], side[:, 2], side[:, 3]
    count = jnp.sum(
        jnp.where(jnp.arange(D) % 6 == 0, side[:, 4] * 16.0 + side[:, 5], 0.0)
    )
    mine_two = exchange(
        jnp.broadcast_to(second_part[None], (64, 24, D)), BOTH, SAME_CORE
    ).reshape(2, D, D)
    other_two = swap(mine_two)
    even = jnp.where(core == 0, mine_two, other_two)
    odd = jnp.where(core == 0, other_two, mine_two)
    win = jnp.concatenate([even[0], odd[0], even[1], odd[1]], 1)
    half_keep = lax.dynamic_slice_in_dim(w_out, core * 384, 384, 1)
    half_send = lax.dynamic_slice_in_dim(w_out, (1 - core) * 384, 384, 1)
    half_got = swap(half_send)
    pair_rows = jnp.where(
        core == 0,
        jnp.concatenate([half_keep, half_got], 0),
        jnp.concatenate([half_got, half_keep], 0),
    )
    mine_three = exchange(jnp.broadcast_to(pair_rows[None], (64, 48, 384)), BOTH, SAME_CORE)
    mine_three = mine_three.reshape(2, 32, 48, 384).transpose(1, 0, 2, 3).reshape(4 * D, 384)
    other_three = swap(mine_three)
    wout = jnp.where(
        core == 0,
        jnp.concatenate([mine_three, other_three], 1),
        jnp.concatenate([other_three, mine_three], 1),
    )

    natural = reorder(long_in, inverse)
    packed = jnp.concatenate(
        [
            cot_long,
            teacher,
            jnp.broadcast_to(slot_weight[:, None], (ROWS, 128)).astype(bf16),
        ],
        1,
    )
    packed = reorder(packed, inverse)
    cot_nat = packed[:, :D].astype(f32)
    teach_nat = packed[:, D : 2 * D].astype(f32)
    weighting = packed[:, 2 * D].astype(f32)
    globs = lax.all_gather(
        jnp.concatenate([glob_in, cot_glob], 1), "fsdp", axis_index_groups=QUADS, axis=0, tiled=True
    )
    left = lax.ppermute(natural[ROWS - BLOCK :], "fsdp", TO_RIGHT)
    right = lax.ppermute(natural[:BLOCK], "fsdp", TO_LEFT)
    inputs = jnp.concatenate([left, natural, right, globs[:, :D]], 0).astype(f32)
    normed_one, base_one, factor_one = norm_rows(inputs, gain1, shift1)
    acts_one = normed_one.astype(bf16)
    wqkv = jnp.concatenate([wq, wk, wv], 1)
    proj = dot(acts_one, wqkv).astype(bf16)

    def heads(value):
        return value.reshape(value.shape[0], HEADS, HEAD)

    query = heads(proj[128:640, :D]).reshape(4, BLOCK, HEADS, HEAD)
    keys = heads(proj[:768, D : 2 * D])
    values = heads(proj[:768, 2 * D :])
    gquery = heads(proj[768:, :D])
    gkey = heads(proj[768:, D : 2 * D])
    gvalue = heads(proj[768:, 2 * D :])
    start = quarter * ROWS
    key_pos = start - BLOCK + jnp.arange(768)
    key_ok = (key_pos >= 0) & (key_pos < length)
    glob_ok = anchors < length
    window_key = jnp.stack([keys[128 * j : 128 * j + 384] for j in range(4)])
    window_value = jnp.stack([values[128 * j : 128 * j + 384] for j in range(4)])
    window_ok = jnp.stack([key_ok[128 * j : 128 * j + 384] for j in range(4)])
    picker = (rel_labels[:, None] == jnp.arange(LABELS)[None, :]).astype(f32)
    label_table = jnp.dot(picker, rel_bias[:LABELS], precision=HIGHEST)
    line = jnp.full((HEADS, 512), MASKED, f32)
    line = lax.dynamic_update_slice(line, label_table.T, (0, 44))
    band = jnp.stack([jnp.roll(line, r, 1)[:, :384] for r in range(BLOCK)], 1)
    query_run = (start + jnp.arange(ROWS)) // GLOBAL_EVERY
    owning = (query_run[:, None] == jnp.arange(GSEQ)[None, :]).reshape(4, BLOCK, GSEQ)
    own_bias = rel_bias[LABELS]
    other_bias = rel_bias[LABELS + 1]
    remote_bias = jnp.where(
        owning[:, None], own_bias[None, :, None, None], other_bias[None, :, None, None]
    )

    def long_scores():
        local = (
            jnp.einsum("bihd,bthd->bhit", query, window_key, preferred_element_type=f32) * scale
            + band[None]
        )
        remote = (
            jnp.einsum("bihd,ghd->bhig", query, gkey, preferred_element_type=f32) * scale
            + remote_bias
        )
        return jnp.concatenate(
            [
                jnp.where(window_ok[:, None, None, :], local, MASKED),
                jnp.where(glob_ok[None, None, None, :], remote, MASKED),
            ],
            -1,
        )

    scores = long_scores()
    summit = jnp.max(scores, -1, keepdims=True)
    powers = jnp.exp(scores - summit)
    total = jnp.sum(powers, -1, keepdims=True)
    long_lse = summit + jnp.log(total)
    probs = (powers / total).astype(bf16)
    long_out = jnp.einsum(
        "bhit,bthd->bihd", probs[..., :384], window_value, preferred_element_type=f32
    ) + jnp.einsum("bhig,ghd->bihd", probs[..., 384:], gvalue, preferred_element_type=f32)
    long_out = long_out.reshape(ROWS, D).astype(bf16)

    cross_key = jnp.concatenate([keys[128:640], gkey], 0)
    cross_value = jnp.concatenate([values[128:640], gvalue], 0)
    own_glob = jnp.arange(GSEQ) // 32 == quarter
    cross_ok = jnp.concatenate([key_ok[128:640], glob_ok & own_glob])
    cross_own = query_run[None, :] == jnp.arange(GSEQ)[:, None]
    cross_bias = jnp.concatenate(
        [
            jnp.where(cross_own[None], own_bias[:, None, None], other_bias[:, None, None]),
            jnp.zeros((HEADS, GSEQ, GSEQ), f32),
        ],
        -1,
    )

    def cross_scores():
        return jnp.where(
            cross_ok[None, None, :],
            jnp.einsum("ihd,jhd->hij", gquery, cross_key, preferred_element_type=f32) * scale
            + cross_bias,
            MASKED,
        )

    scores = cross_scores()
    top = jnp.max(scores, -1, keepdims=True)
    powers = jnp.exp(scores - top)
    total = jnp.sum(powers, -1, keepdims=True)
    part_lse = (top + jnp.log(total))[..., 0].T
    part_out = jnp.einsum(
        "hij,jhd->ihd", (powers / total).astype(bf16), cross_value, preferred_element_type=f32
    ).reshape(GSEQ, D)
    sent = jnp.concatenate(
        [part_out.astype(bf16), split3(part_lse), jnp.zeros((GSEQ, 92), bf16)], 1
    )
    got = exchange(jnp.broadcast_to(sent[None], (4, GSEQ, EXT)).reshape(4 * GSEQ, EXT), "fsdp", QUADS)
    got = got.reshape(4, GSEQ, EXT)
    lses = join3(got[..., D:], HEADS)
    high = jnp.max(lses, 0)
    glob_lse = high + jnp.log(jnp.sum(jnp.exp(lses - high), 0))
    shares = jnp.exp(lses - glob_lse)
    glob_out = jnp.sum(
        got[..., :D].astype(f32) * jnp.repeat(shares, HEAD, axis=-1), 0
    ).astype(bf16)

    mixed = jnp.concatenate([long_out, glob_out], 0)
    middle = inputs[jnp.r_[128:640, 768:896]] + dot(mixed, wa)
    normed_two, base_two, factor_two = norm_rows(middle, gain2, shift2)
    acts_two = normed_two.astype(bf16)
    inner = dot(acts_two, win)
    hidden_full, gelu_back = jax.vjp(lambda v: jax.nn.gelu(v, approximate=False), inner)
    hidden = hidden_full.astype(bf16)
    result = middle + dot(hidden, wout)
    error = result[:ROWS] - teach_nat
    loss_sum = jnp.sum(weighting[:, None] * error * error)
    grad_result = jnp.concatenate(
        [cot_nat + 2.0 * weighting[:, None] * error / count, globs[:, D:].astype(f32)], 0
    )
    owned = jnp.concatenate([jnp.ones((ROWS,), f32), own_glob.astype(f32)])[:, None]
    owned_bf = owned.astype(bf16)
    grad_z = grad_result.astype(bf16)
    grad_wout = dot(hidden.T, grad_z * owned_bf)
    grad_hidden = dot(grad_z, wout.T)
    grad_inner = gelu_back(grad_hidden)[0].astype(bf16)
    grad_win = dot(acts_two.T, grad_inner * owned_bf)
    grad_acts = dot(grad_inner, win.T)
    gain_grad_two = jnp.sum(grad_acts * base_two * owned, 0)
    shift_grad_two = jnp.sum(grad_acts * owned, 0)
    grad_middle = grad_result + norm_back(grad_acts, base_two, factor_two, gain2)
    grad_branch = grad_middle.astype(bf16)
    grad_wattn = dot(mixed.T, grad_branch * owned_bf)
    grad_mixed = dot(grad_branch, wa.T).astype(bf16)

    grad_long_out = heads(grad_mixed[:ROWS]).reshape(4, BLOCK, HEADS, HEAD)
    grad_glob_out = heads(grad_mixed[ROWS:])
    probs = jnp.exp(long_scores() - long_lse)
    dp = jnp.concatenate(
        [
            jnp.einsum("bihd,bthd->bhit", grad_long_out, window_value, preferred_element_type=f32),
            jnp.einsum("bihd,ghd->bhig", grad_long_out, gvalue, preferred_element_type=f32),
        ],
        -1,
    )
    delta = jnp.sum(probs * dp, -1, keepdims=True)
    ds = (probs * (dp - delta)).astype(bf16)
    probs = probs.astype(bf16)
    grad_query = (
        jnp.einsum("bhit,bthd->bihd", ds[..., :384], window_key, preferred_element_type=f32)
        + jnp.einsum("bhig,ghd->bihd", ds[..., 384:], gkey, preferred_element_type=f32)
    ) * scale
    win_dk = jnp.einsum("bhit,bihd->bthd", ds[..., :384], query, preferred_element_type=f32) * scale
    win_dv = jnp.einsum(
        "bhit,bihd->bthd", probs[..., :384], grad_long_out, preferred_element_type=f32
    )
    dgk = jnp.einsum("bhig,bihd->ghd", ds[..., 384:], query, preferred_element_type=f32) * scale
    dgv = jnp.einsum("bhig,bihd->ghd", probs[..., 384:], grad_long_out, preferred_element_type=f32)
    band_grad = jnp.sum(ds[..., :384].astype(f32), 0)
    skewed = jnp.pad(band_grad.reshape(HEADS, BLOCK * 384), ((0, 0), (0, BLOCK))).reshape(
        HEADS, BLOCK, 385
    )
    grad_table = jnp.sum(skewed, 1)[:, 44 : 44 + LABELS]
    remote = ds[..., 384:].astype(f32)
    grad_own = jnp.sum(jnp.where(owning[:, None], remote, 0.0), (0, 2, 3))
    grad_other = jnp.sum(jnp.where(owning[:, None], 0.0, remote), (0, 2, 3))
    gdelta = jnp.sum(
        heads(grad_mixed[ROWS:]).astype(f32) * heads(glob_out).astype(f32), -1
    )
    probs = jnp.exp(cross_scores() - glob_lse.T[..., None])
    dp = jnp.einsum("ihd,jhd->hij", grad_glob_out, cross_value, preferred_element_type=f32)
    ds = (probs * (dp - gdelta.T[..., None])).astype(bf16)
    probs = probs.astype(bf16)
    dgq = jnp.einsum("hij,jhd->ihd", ds, cross_key, preferred_element_type=f32) * scale
    cross_dk = jnp.einsum("hij,ihd->jhd", ds, gquery, preferred_element_type=f32) * scale
    cross_dv = jnp.einsum("hij,ihd->jhd", probs, grad_glob_out, preferred_element_type=f32)
    remote = ds[..., :ROWS].astype(f32)
    grad_own = grad_own + jnp.sum(jnp.where(cross_own[None], remote, 0.0), (1, 2))
    grad_other = grad_other + jnp.sum(jnp.where(cross_own[None], 0.0, remote), (1, 2))

    def gather_rows(windows, cross):
        rows = jnp.zeros((768, HEADS, HEAD), f32)
        for j in range(4):
            rows = rows.at[128 * j : 128 * j + 384].add(windows[j])
        return rows.at[128:640].add(cross[:ROWS]).reshape(768, D)

    dk = jnp.concatenate([gather_rows(win_dk, cross_dk), (dgk + cross_dk[ROWS:]).reshape(GSEQ, D)])
    dv = jnp.concatenate([gather_rows(win_dv, cross_dv), (dgv + cross_dv[ROWS:]).reshape(GSEQ, D)])
    dq = jnp.concatenate(
        [
            jnp.zeros((BLOCK, D), f32),
            grad_query.reshape(ROWS, D),
            jnp.zeros((BLOCK, D), f32),
            dgq.reshape(GSEQ, D),
        ]
    )
    grad_proj = jnp.concatenate([dq, dk, dv], 1).astype(bf16)
    grad_wqkv = dot(acts_one.T, grad_proj)
    grad_acts = dot(grad_proj, wqkv.T)
    gain_grad_one = jnp.sum(grad_acts * base_one, 0)
    shift_grad_one = jnp.sum(grad_acts, 0)
    back = norm_back(grad_acts, base_one, factor_one, gain1)
    from_left = lax.ppermute(back[640:768].astype(bf16), "fsdp", TO_RIGHT).astype(f32)
    from_right = lax.ppermute(back[:128].astype(bf16), "fsdp", TO_LEFT).astype(f32)
    grad_nat = grad_middle[:ROWS] + back[128:640]
    grad_nat = grad_nat.at[:128].add(from_left).at[384:].add(from_right)
    grad_long = reorder(grad_nat.astype(bf16), order).astype(f32)
    glob_parts = exchange(back[768:].reshape(4 * 32, D), "fsdp", QUADS).reshape(4, 32, D)
    grad_glob = lax.dynamic_slice_in_dim(grad_middle, ROWS + quarter * 32, 32, 0) + jnp.sum(
        glob_parts, 0
    )
    out_long = reorder(result[:ROWS].astype(bf16), order)
    out_glob = lax.dynamic_slice_in_dim(result, ROWS + quarter * 32, 32, 0).astype(bf16)

    one = jnp.concatenate([grad_wqkv, grad_wattn], 1).reshape(D, 2, 2, D).transpose(1, 2, 0, 3)
    one = reduce_columns(one, core)
    two = reduce_columns(grad_win.reshape(D, 2, 2, D).transpose(1, 2, 0, 3), core)
    qkv_grad = one[:3].transpose(1, 0, 2).reshape(6, 3 * D)
    attn_grad = one[3]
    in_grad = two.transpose(1, 0, 2).reshape(6, 4 * D)
    keep = lax.dynamic_slice_in_dim(grad_wout, core * 384, 384, 1)
    send = lax.dynamic_slice_in_dim(grad_wout, (1 - core) * 384, 384, 1)
    total = (keep + swap(send.astype(bf16)).astype(f32)).astype(bf16)
    total = total.reshape(32, 2, 48, 384).transpose(1, 0, 2, 3).reshape(64, 48, 384)
    mine = jnp.sum(exchange(total, BOTH, SAME_CORE).astype(f32), 0)
    other = swap(mine)
    halves = jnp.where(
        core == 0, jnp.concatenate([mine, other], 1), jnp.concatenate([other, mine], 1)
    )
    out_grad = lax.dynamic_slice_in_dim(halves, core * 24, 24, 0)
    label_grad = jnp.dot(picker.T, grad_table.T, precision=HIGHEST)
    rel_grad = jnp.concatenate([label_grad, grad_own[None], grad_other[None]], 0)
    norm_grads = jnp.stack([gain_grad_one, gain_grad_two, shift_grad_one, shift_grad_two], 1)
    rel_total, norm_total, loss_total = lax.psum((rel_grad, norm_grads, loss_sum), BOTH)
    mine_norm = lax.dynamic_slice_in_dim(
        norm_total, (lax.axis_index("dp") * 16 + member) * 6, 6, 0
    )
    return (
        out_long,
        out_glob,
        loss_total / count,
        grad_long,
        grad_glob,
        qkv_grad,
        attn_grad,
        in_grad,
        out_grad,
        mine_norm[:, :2],
        mine_norm[:, 2:],
        rel_total,
    )


def solution(mesh):
    rows = P(BOTH, None)
    in_specs = (rows,) * 11 + (P(), P("dp"), P("dp", None), P("dp"), P(), P(BOTH))
    out_specs = (rows, rows, P(), rows, rows, rows, rows, rows, rows, rows, rows, P())
    return jax.shard_map(shards, mesh=mesh, in_specs=in_specs, out_specs=out_specs, check_vma=False)
```

```python
import jax
import jax.numpy as jnp
from jax import lax
from jax.experimental import pallas as pl
from jax.experimental.pallas import tpu as pltpu
from jax.sharding import PartitionSpec as P

D = 768
HEADS = 12
HEAD = 64
RADIUS = 84
LABELS = 169
BLOCK = 128
SEQ_BLOCKS = 16
GLOBAL_EVERY = 16
GSEQ = 128
ROWS = 512
EXT = 896
EPS = 1e-05
MASKED = -1e30
HIGHEST = lax.Precision.HIGHEST
BOTH = ("dp", "fsdp")
f32 = jnp.float32
bf16 = jnp.bfloat16

QUADS = [[4 * i + j for j in range(4)] for i in range(4)]
SAME_CORE = [[4 * g + 2 * p + c for p in range(2) for g in range(32)] for c in range(2)]
SWAP = [(i, i ^ 1) for i in range(16)]
TO_RIGHT = [(i, i + 1) for i in range(16) if i % 4 < 3]
TO_LEFT = [(i, i - 1) for i in range(16) if i % 4 > 0]


def exchange(value, axis, groups=None):
    return lax.all_to_all(value, axis, 0, 0, axis_index_groups=groups, tiled=True)


def swap(value):
    return lax.ppermute(value, "fsdp", SWAP)


def pieces(rows):
    width = rows.shape[-1]
    return rows.reshape(4, 16, 8, width).transpose(1, 0, 2, 3).reshape(64, 8, width)


def unpieces(value):
    width = value.shape[-1]
    return value.reshape(16, 4, 8, width).transpose(1, 0, 2, 3).reshape(ROWS, width)


def reorder(rows, index):
    spread = exchange(pieces(rows), "fsdp")
    return unpieces(exchange(spread[index], "fsdp"))


def split3(value):
    high = value.astype(bf16)
    rest = value - high.astype(f32)
    mid = rest.astype(bf16)
    low = (rest - mid.astype(f32)).astype(bf16)
    return jnp.concatenate([high, mid, low], 0)


def join3(value):
    value = value.astype(f32)
    return value[:, :HEADS] + value[:, HEADS : 2 * HEADS] + value[:, 2 * HEADS : 3 * HEADS]


def reduce_columns(keep, send):
    total = keep.astype(f32) + swap(send).astype(f32)
    parts = exchange(total.astype(bf16).reshape(64, 24, D), BOTH, SAME_CORE)
    mine = jnp.sum(parts.astype(f32), 0)
    return exchange(mine.reshape(4, 6, D), "fsdp", QUADS)


def dot_nn(a, b):
    return lax.dot_general(a, b, (((1,), (0,)), ((), ())), preferred_element_type=f32)


def dot_nt(a, b):
    return lax.dot_general(a, b, (((1,), (1,)), ((), ())), preferred_element_type=f32)


def dot_tn(a, b):
    return lax.dot_general(a, b, (((0,), (0,)), ((), ())), preferred_element_type=f32)


def whole(shape):
    zeros = (0,) * len(shape)
    return pl.BlockSpec(shape, lambda *_: zeros, pipeline_mode=pl.Buffered(1))


SCALARS = pl.BlockSpec(memory_space=pltpu.SMEM)


def params(megabytes):
    return pltpu.CompilerParams(vmem_limit_bytes=megabytes << 20)


def normalise(values):
    centre = jnp.mean(values, -1, keepdims=True)
    centred = values - centre
    spread = jnp.mean(centred * centred, -1, keepdims=True)
    factor = lax.rsqrt(spread + EPS)
    return centred * factor, factor


def project_kernel(left, nat, right, globs, norms, even, odd, rows_out, acts_out, proj_out):
    rows_out[:128] = left[...]
    rows_out[128:640] = nat[...]
    rows_out[640:768] = right[...]
    rows_out[768:] = globs[:, :D]
    normal, _ = normalise(rows_out[...].astype(f32))
    acts = (normal * norms[0:1] + norms[2:3]).astype(bf16)
    acts_out[...] = acts
    proj_out[:, :D] = dot_nn(acts, even[0]).astype(bf16)
    proj_out[:, D : 2 * D] = dot_nn(acts, odd[0]).astype(bf16)
    proj_out[:, 2 * D :] = dot_nn(acts, even[1]).astype(bf16)


def project(left, nat, right, globs, norms, even, odd):
    return pl.pallas_call(
        project_kernel,
        out_shape=(
            jax.ShapeDtypeStruct((EXT, D), bf16),
            jax.ShapeDtypeStruct((EXT, D), bf16),
            jax.ShapeDtypeStruct((EXT, 3 * D), bf16),
        ),
        compiler_params=params(50),
        name="project",
    )(left, nat, right, globs, norms, even, odd)


def stack_heads(rows):
    first = lax.broadcasted_iota(jnp.int32, rows.shape, 1) < HEAD
    zero = jnp.zeros_like(rows)
    return jnp.concatenate([jnp.where(first, rows, zero), jnp.where(first, zero, rows)], 0)


def merge_heads(value):
    first = lax.broadcasted_iota(jnp.int32, (128, 128), 0) < HEAD
    return jnp.where(first, value[:, :128], value[:, 128:]).T


def band_tile(line):
    tiles = []
    for head in range(2):
        spread = jnp.broadcast_to(line[head : head + 1], (BLOCK, 512))
        rolled = pltpu.roll(spread, 0, 1, stride=1, stride_axis=0)
        tiles.append(
            jnp.concatenate([rolled[:, 128 * i : 128 * i + 128].T for i in range(3)], 0)
        )
    return jnp.concatenate(tiles, 1)


def pair_row(first, second):
    lane = lax.broadcasted_iota(jnp.int32, (1, 256), 1)
    return jnp.where(lane < 128, first, second)


def long_owned(run):
    key = lax.broadcasted_iota(jnp.int32, (128, 256), 0)
    lane = lax.broadcasted_iota(jnp.int32, (128, 256), 1)
    return key == run + lax.shift_right_logical(lane & 127, 4)


def cross_owned(run):
    key = lax.broadcasted_iota(jnp.int32, (ROWS, 256), 0)
    lane = lax.broadcasted_iota(jnp.int32, (ROWS, 256), 1)
    return run + lax.shift_right_logical(key, 4) == (lane & 127)


def attend_kernel(
    place, table, line, key_mask, self_mask, q, k, v, out, lse, glob_out, glob_lse, band
):
    pair = pl.program_id(0)
    run = place[0] * 32
    own = pair_row(table[0, 2 * pair], table[0, 2 * pair + 1])
    other = pair_row(table[1, 2 * pair], table[1, 2 * pair + 1])
    band[...] = band_tile(line[0])
    values = v[...].T
    for j in range(4):
        low = 128 * j
        query = stack_heads(q[128 + low : 256 + low, :] * 0.125)
        near = dot_nt(k[low : low + 384, :], query) + (band[...] + key_mask[low : low + 384, :])
        far = dot_nt(k[768:, :], query) + (
            jnp.where(long_owned(run + 8 * j), own, other) + key_mask[768:, :]
        )
        top = jnp.maximum(jnp.max(near, 0, keepdims=True), jnp.max(far, 0, keepdims=True))
        near = jnp.exp(near - top)
        far = jnp.exp(far - top)
        total = jnp.sum(near, 0, keepdims=True) + jnp.sum(far, 0, keepdims=True)
        share = 1.0 / total
        got = dot_nn(values[:, low : low + 384], (near * share).astype(bf16)) + dot_nn(
            values[:, 768:], (far * share).astype(bf16)
        )
        out[low : low + 128, :] = merge_heads(got).astype(bf16)
        lse[0, j : j + 1, :] = top + jnp.log(total)
    query = stack_heads(q[768:, :] * 0.125)
    near = dot_nt(k[128:640, :], query) + (
        jnp.where(cross_owned(run), own, other) + key_mask[128:640, :]
    )
    far = dot_nt(k[768:, :], query) + self_mask[...]
    top = jnp.maximum(jnp.max(near, 0, keepdims=True), jnp.max(far, 0, keepdims=True))
    near = jnp.exp(near - top)
    far = jnp.exp(far - top)
    total = jnp.sum(near, 0, keepdims=True) + jnp.sum(far, 0, keepdims=True)
    share = 1.0 / total
    got = dot_nn(values[:, 128:640], (near * share).astype(bf16)) + dot_nn(
        values[:, 768:], (far * share).astype(bf16)
    )
    first = lax.broadcasted_iota(jnp.int32, (128, 128), 0) < HEAD
    glob_out[...] = jnp.where(first, got[:, :128], got[:, 128:]).astype(bf16)
    glob_lse[0] = top + jnp.log(total)


def column(width, offset):
    return pl.BlockSpec((width, 128), lambda h: (0, h + offset))


def attend(place, table, line, key_mask, self_mask, proj):
    return pl.pallas_call(
        attend_kernel,
        grid=(6,),
        in_specs=[
            SCALARS,
            SCALARS,
            pl.BlockSpec((1, 2, 512), lambda h: (h, 0, 0)),
            whole((EXT, 256)),
            whole((128, 256)),
            column(EXT, 0),
            column(EXT, 6),
            column(EXT, 12),
        ],
        out_specs=[
            column(ROWS, 0),
            pl.BlockSpec((1, 4, 256), lambda h: (h, 0, 0)),
            pl.BlockSpec((128, 128), lambda h: (h, 0)),
            pl.BlockSpec((1, 1, 256), lambda h: (h, 0, 0)),
        ],
        out_shape=(
            jax.ShapeDtypeStruct((ROWS, D), bf16),
            jax.ShapeDtypeStruct((6, 4, 256), f32),
            jax.ShapeDtypeStruct((D, 128), bf16),
            jax.ShapeDtypeStruct((6, 1, 256), f32),
        ),
        scratch_shapes=[pltpu.VMEM((384, 256), f32)],
        compiler_params=params(40),
        name="attend",
    )(place, table, line, key_mask, self_mask, proj, proj, proj)


def fold_band(tile):
    rows = jnp.concatenate([tile[128 * i : 128 * i + 128].T for i in range(3)], 1)
    rows = jnp.concatenate([rows, jnp.zeros((BLOCK, 128), f32)], 1)
    total = rows[:8]
    for a in range(1, 16):
        total = total + pltpu.roll(rows[8 * a : 8 * a + 8], 512 - 8 * a, 1)
    row = lax.broadcasted_iota(jnp.int32, (8, 512), 0)
    for bit in (1, 2, 4):
        total = jnp.where((row & bit) != 0, pltpu.roll(total, 512 - bit, 1), total)
    return jnp.sum(total, 0, keepdims=True)


def attend_back_kernel(
    place,
    table,
    line,
    key_mask,
    self_mask,
    q,
    k,
    v,
    grad,
    lse,
    glob_out,
    glob_lse,
    dq,
    dk,
    dv,
    rel,
    band,
    band_sum,
    key_sum,
    value_sum,
):
    pair = pl.program_id(0)
    run = place[0] * 32
    own = pair_row(table[0, 2 * pair], table[0, 2 * pair + 1])
    other = pair_row(table[1, 2 * pair], table[1, 2 * pair + 1])
    band[...] = band_tile(line[0])
    keys = k[...].T
    band_sum[...] = jnp.zeros_like(band_sum)
    key_sum[...] = jnp.zeros_like(key_sum)
    value_sum[...] = jnp.zeros_like(value_sum)
    owned_sum = jnp.zeros((1, 256), f32)
    other_sum = jnp.zeros((1, 256), f32)
    dq[:128] = jnp.zeros((128, 128), bf16)
    dq[640:768] = jnp.zeros((128, 128), bf16)
    for j in range(4):
        low = 128 * j
        query = stack_heads(q[128 + low : 256 + low, :] * 0.125)
        back = stack_heads(grad[low : low + 128, :])
        near = dot_nt(k[low : low + 384, :], query) + (band[...] + key_mask[low : low + 384, :])
        owned = long_owned(run + 8 * j)
        far = dot_nt(k[768:, :], query) + (jnp.where(owned, own, other) + key_mask[768:, :])
        top = lse[0, j : j + 1, :]
        near = jnp.exp(near - top)
        far = jnp.exp(far - top)
        near_d = dot_nt(v[low : low + 384, :], back)
        far_d = dot_nt(v[768:, :], back)
        delta = jnp.sum(near * near_d, 0, keepdims=True) + jnp.sum(far * far_d, 0, keepdims=True)
        near_d = (near * (near_d - delta)).astype(bf16)
        far_d = (far * (far_d - delta)).astype(bf16)
        key_sum[low : low + 384, :] += dot_nn(near_d, query)
        value_sum[low : low + 384, :] += dot_nn(near.astype(bf16), back)
        key_sum[768:, :] += dot_nn(far_d, query)
        value_sum[768:, :] += dot_nn(far.astype(bf16), back)
        got = dot_nn(keys[:, low : low + 384], near_d) + dot_nn(keys[:, 768:], far_d)
        dq[128 + low : 256 + low, :] = (merge_heads(got) * 0.125).astype(bf16)
        band_sum[...] += near_d.astype(f32)
        far_d = far_d.astype(f32)
        owned_sum += jnp.sum(jnp.where(owned, far_d, 0.0), 0, keepdims=True)
        other_sum += jnp.sum(jnp.where(owned, 0.0, far_d), 0, keepdims=True)
    query = stack_heads(q[768:, :] * 0.125)
    back = stack_heads(grad[ROWS:, :])
    owned = cross_owned(run)
    near = dot_nt(k[128:640, :], query) + (jnp.where(owned, own, other) + key_mask[128:640, :])
    far = dot_nt(k[768:, :], query) + self_mask[...]
    top = glob_lse[0]
    near = jnp.exp(near - top)
    far = jnp.exp(far - top)
    near_d = dot_nt(v[128:640, :], back)
    far_d = dot_nt(v[768:, :], back)
    product = grad[ROWS:, :].astype(f32).T * glob_out[...].astype(f32)
    delta = jnp.concatenate(
        [
            jnp.sum(product[:HEAD], 0, keepdims=True),
            jnp.sum(product[HEAD:], 0, keepdims=True),
        ],
        1,
    )
    near_d = (near * (near_d - delta)).astype(bf16)
    far_d = (far * (far_d - delta)).astype(bf16)
    key_sum[128:640, :] += dot_nn(near_d, query)
    value_sum[128:640, :] += dot_nn(near.astype(bf16), back)
    key_sum[768:, :] += dot_nn(far_d, query)
    value_sum[768:, :] += dot_nn(far.astype(bf16), back)
    got = dot_nn(keys[:, 128:640], near_d) + dot_nn(keys[:, 768:], far_d)
    dq[768:, :] = (merge_heads(got) * 0.125).astype(bf16)
    near_d = near_d.astype(f32)
    owned_sum += jnp.sum(jnp.where(owned, near_d, 0.0), 0, keepdims=True)
    other_sum += jnp.sum(jnp.where(owned, 0.0, near_d), 0, keepdims=True)
    dk[...] = key_sum[...].astype(bf16)
    dv[...] = value_sum[...].astype(bf16)
    rel[0] = jnp.zeros((8, 512), f32)
    for head in range(2):
        lanes = slice(128 * head, 128 * head + 128)
        rel[0, head : head + 1, :] = fold_band(band_sum[:, lanes])
        rel[0, 2 + head : 3 + head, :128] = owned_sum[:, lanes]
        rel[0, 4 + head : 5 + head, :128] = other_sum[:, lanes]


def attend_back(place, table, line, key_mask, self_mask, proj, grad, lse, glob_out, glob_lse):
    return pl.pallas_call(
        attend_back_kernel,
        grid=(6,),
        in_specs=[
            SCALARS,
            SCALARS,
            pl.BlockSpec((1, 2, 512), lambda h: (h, 0, 0)),
            whole((EXT, 256)),
            whole((128, 256)),
            column(EXT, 0),
            column(EXT, 6),
            column(EXT, 12),
            column(640, 0),
            pl.BlockSpec((1, 4, 256), lambda h: (h, 0, 0)),
            pl.BlockSpec((128, 128), lambda h: (h, 0)),
            pl.BlockSpec((1, 1, 256), lambda h: (h, 0, 0)),
        ],
        out_specs=[
            column(EXT, 0),
            column(EXT, 0),
            column(EXT, 0),
            pl.BlockSpec((1, 8, 512), lambda h: (h, 0, 0)),
        ],
        out_shape=(
            jax.ShapeDtypeStruct((EXT, D), bf16),
            jax.ShapeDtypeStruct((EXT, D), bf16),
            jax.ShapeDtypeStruct((EXT, D), bf16),
            jax.ShapeDtypeStruct((6, 8, 512), f32),
        ),
        scratch_shapes=[
            pltpu.VMEM((384, 256), f32),
            pltpu.VMEM((384, 256), f32),
            pltpu.VMEM((EXT, 128), f32),
            pltpu.VMEM((EXT, 128), f32),
        ],
        compiler_params=params(48),
        name="attend_back",
    )(place, table, line, key_mask, self_mask, proj, proj, proj, grad, lse, glob_out, glob_lse)


def feed_kernel(
    place,
    coef,
    rows,
    long_out,
    parts,
    shares,
    packed,
    globs,
    norms,
    wa,
    win,
    wout,
    result_out,
    loss_out,
    glob_out,
    middle_grad_out,
    mixed_grad_out,
    wattn_grad,
    win_send,
    win_keep,
    wout_send,
    wout_keep,
    norm_grads,
    mixed,
    acts,
    normal,
    total,
    hidden,
    slope,
    grad_z,
    grad_acts,
    factor,
):
    step = pl.program_id(0)
    core = place[1]
    quarter = place[0]
    forward = step < 4
    late = jnp.maximum(step - 4, 0)
    chunk = jnp.where(
        forward, step, jnp.where(late < 2, 2 * late + 1 - core, 2 * (late - 2) + core)
    )

    def owned():
        row = lax.broadcasted_iota(jnp.int32, (640, 1), 0)
        first = ROWS + quarter * 32
        return (row < ROWS) | ((row >= first) & (row < first + 32))

    @pl.when(step == 0)
    def _():
        mixed[:ROWS] = long_out[...]
        for pair in range(6):
            sums = jnp.zeros((128, 128), f32)
            top = lax.broadcasted_iota(jnp.int32, (128, 128), 0) < HEAD
            for source in range(4):
                share = jnp.where(
                    top,
                    shares[source, 2 * pair : 2 * pair + 1, :],
                    shares[source, 2 * pair + 1 : 2 * pair + 2, :],
                )
                sums = sums + parts[source, 128 * pair : 128 * pair + 128, :].astype(f32) * share
            glob_out[128 * pair : 128 * pair + 128, :] = sums.astype(bf16)
            mixed[ROWS:, 128 * pair : 128 * pair + 128] = sums.T.astype(bf16)
        middle = dot_nn(mixed[...], wa[...])
        middle = middle + jnp.concatenate(
            [rows[128:640].astype(f32), rows[768:].astype(f32)], 0
        )
        total[...] = middle
        base, scale = normalise(middle)
        normal[...] = base
        factor[...] = scale
        acts[...] = (base * norms[1:2] + norms[3:4]).astype(bf16)

    @pl.when(forward)
    def _():
        inner = dot_nn(acts[...], win[0])
        half = 0.5 + 0.5 * lax.erf(inner * 0.7071067811865476)
        slope[chunk] = half + inner * (jnp.exp(-0.5 * inner * inner) * 0.3989422804014327)
        bits = (inner * half).astype(bf16)
        hidden[chunk] = bits
        total[...] += dot_nn(bits, wout[...])

    @pl.when(step == 3)
    def _():
        result = total[...]
        result_out[...] = result.astype(bf16)
        weight = packed[:, 2 * D : 2 * D + 1].astype(f32)
        error = result[:ROWS] - packed[:, D : 2 * D].astype(f32)
        masked = weight * error
        loss_out[...] = jnp.broadcast_to(
            jnp.sum(jnp.sum(masked * error, 0, keepdims=True), 1, keepdims=True), (8, 128)
        )
        grad = jnp.concatenate(
            [packed[:, :D].astype(f32) + coef[0] * masked, globs[:, D:].astype(f32)], 0
        )
        total[...] = grad
        grad_z[...] = grad.astype(bf16)
        grad_acts[...] = jnp.zeros_like(grad_acts)

    @pl.when(step >= 4)
    def _():
        keep_rows = owned()
        grad_inner = (dot_nt(grad_z[...], wout[...]) * slope[chunk]).astype(bf16)
        zeros = jnp.zeros_like(grad_inner)
        grad_acts[...] += dot_nt(grad_inner, win[0])
        part = dot_tn(acts[...], jnp.where(keep_rows, grad_inner, zeros)).astype(bf16)

        @pl.when(late < 2)
        def _():
            win_send[0] = part

        @pl.when(late >= 2)
        def _():
            win_keep[0] = part

        part = dot_tn(hidden[chunk], jnp.where(keep_rows, grad_z[...], zeros)).astype(bf16)
        first = core == 0
        wout_keep[...] = jnp.where(first, part[:, :384], part[:, 384:])
        wout_send[...] = jnp.where(first, part[:, 384:], part[:, :384])

    @pl.when(step == 7)
    def _():
        keep_rows = owned()
        grad = grad_acts[...]
        base = normal[...]
        mine = jnp.where(keep_rows, grad, 0.0)
        norm_grads[0:1, :] = jnp.sum(mine * base, 0, keepdims=True)
        norm_grads[1:2, :] = jnp.sum(mine, 0, keepdims=True)
        scaled = grad * norms[1:2]
        first = jnp.mean(scaled, -1, keepdims=True)
        second = jnp.mean(scaled * base, -1, keepdims=True)
        middle = total[...] + factor[...] * (scaled - first - base * second)
        middle_grad_out[...] = middle
        branch = middle.astype(bf16)
        mixed_grad_out[...] = dot_nt(branch, wa[...]).astype(bf16)
        wattn_grad[...] = dot_tn(
            mixed[...], jnp.where(keep_rows, branch, jnp.zeros_like(branch))
        ).astype(bf16)


def feed(place, coef, rows, long_out, parts, shares, packed, globs, norms, wa, win, wout):
    def chunk(t, place):
        late = jnp.maximum(t - 4, 0)
        core = place[1]
        back = jnp.where(late < 2, 2 * late + 1 - core, 2 * (late - 2) + core)
        return jnp.where(t < 4, t, back)

    def back_chunk(t, place):
        return chunk(jnp.maximum(t, 4), place)

    def fixed(shape):
        zeros = (0,) * len(shape)
        return pl.BlockSpec(shape, lambda t, place: zeros, pipeline_mode=pl.Buffered(1))

    return pl.pallas_call(
        feed_kernel,
        grid_spec=pltpu.PrefetchScalarGridSpec(
            num_scalar_prefetch=1,
            grid=(8,),
            in_specs=[
                SCALARS,
                fixed((EXT, D)),
                fixed((ROWS, D)),
                fixed((4, 816, 128)),
                fixed((4, 16, 128)),
                fixed((ROWS, 2 * D + 128)),
                fixed((128, 2 * D)),
                fixed((8, D)),
                fixed((D, D)),
                pl.BlockSpec((1, D, D), lambda t, place: (chunk(t, place), 0, 0)),
                pl.BlockSpec((D, D), lambda t, place: (chunk(t, place), 0)),
            ],
            out_specs=[
                fixed((640, D)),
                fixed((8, 128)),
                fixed((D, 128)),
                fixed((640, D)),
                fixed((640, D)),
                fixed((D, D)),
                pl.BlockSpec((1, D, D), lambda t, place: (jnp.clip(t - 4, 0, 1), 0, 0)),
                pl.BlockSpec((1, D, D), lambda t, place: (jnp.clip(t - 6, 0, 1), 0, 0)),
                pl.BlockSpec((D, 384), lambda t, place: (back_chunk(t, place), 0)),
                pl.BlockSpec((D, 384), lambda t, place: (back_chunk(t, place), 0)),
                fixed((8, D)),
            ],
            scratch_shapes=[
                pltpu.VMEM((640, D), bf16),
                pltpu.VMEM((640, D), bf16),
                pltpu.VMEM((640, D), f32),
                pltpu.VMEM((640, D), f32),
                pltpu.VMEM((4, 640, D), bf16),
                pltpu.VMEM((4, 640, D), f32),
                pltpu.VMEM((640, D), bf16),
                pltpu.VMEM((640, D), f32),
                pltpu.VMEM((640, 1), f32),
            ],
        ),
        out_shape=(
            jax.ShapeDtypeStruct((640, D), bf16),
            jax.ShapeDtypeStruct((8, 128), f32),
            jax.ShapeDtypeStruct((D, 128), bf16),
            jax.ShapeDtypeStruct((640, D), f32),
            jax.ShapeDtypeStruct((640, D), bf16),
            jax.ShapeDtypeStruct((D, D), bf16),
            jax.ShapeDtypeStruct((2, D, D), bf16),
            jax.ShapeDtypeStruct((2, D, D), bf16),
            jax.ShapeDtypeStruct((4 * D, 384), bf16),
            jax.ShapeDtypeStruct((4 * D, 384), bf16),
            jax.ShapeDtypeStruct((8, D), f32),
        ),
        compiler_params=params(60),
        name="feed",
    )(place, coef, rows, long_out, parts, shares, packed, globs, norms, wa, win, wout)


def project_back_kernel(
    place, rows, acts, dq, dk, dv, norms, even, odd, middle_grad, wattn_grad,
    send, keep, nat, left, right, globs, norm_grads,
):
    core = place[1]
    both = acts[...]
    grads = (dot_tn(both, dq[...]), dot_tn(both, dk[...]), dot_tn(both, dv[...]))
    parts = [part.astype(bf16) for part in grads] + [wattn_grad[...]]

    @pl.when(core == 0)
    def _():
        keep[0], keep[1], send[0], send[1] = parts[0], parts[2], parts[1], parts[3]

    @pl.when(core == 1)
    def _():
        keep[0], keep[1], send[0], send[1] = parts[1], parts[3], parts[0], parts[2]

    grad = dot_nt(dq[...], even[0]) + dot_nt(dk[...], odd[0]) + dot_nt(dv[...], even[1])
    base, factor = normalise(rows[...].astype(f32))
    norm_grads[0:1, :] = jnp.sum(grad * base, 0, keepdims=True)
    norm_grads[1:2, :] = jnp.sum(grad, 0, keepdims=True)
    scaled = grad * norms[0:1]
    first = jnp.mean(scaled, -1, keepdims=True)
    second = jnp.mean(scaled * base, -1, keepdims=True)
    back = factor * (scaled - first - base * second)
    nat[...] = back[128:640] + middle_grad[:ROWS]
    left[...] = back[:128].astype(bf16)
    right[...] = back[640:768].astype(bf16)
    globs[...] = back[768:]


def project_back(place, rows, acts, dq, dk, dv, norms, even, odd, middle_grad, wattn_grad):
    vm = pl.BlockSpec(memory_space=pltpu.VMEM)
    return pl.pallas_call(
        project_back_kernel,
        in_specs=[SCALARS] + [vm] * 10,
        out_shape=(
            jax.ShapeDtypeStruct((2, D, D), bf16),
            jax.ShapeDtypeStruct((2, D, D), bf16),
            jax.ShapeDtypeStruct((ROWS, D), f32),
            jax.ShapeDtypeStruct((128, D), bf16),
            jax.ShapeDtypeStruct((128, D), bf16),
            jax.ShapeDtypeStruct((128, D), f32),
            jax.ShapeDtypeStruct((8, D), f32),
        ),
        compiler_params=params(56),
        name="project_back",
    )(place, rows, acts, dq, dk, dv, norms, even, odd, middle_grad, wattn_grad)


def shards(
    long_in,
    glob_in,
    cot_long,
    cot_glob,
    teacher,
    w_qkv,
    w_attn,
    w_in,
    w_out,
    norm_gains,
    norm_biases,
    rel_bias,
    lengths,
    block_order,
    global_pos,
    rel_labels,
    loss_mask,
):
    member = lax.axis_index("fsdp")
    core = member % 2
    quarter = member % 4
    seq = member // 4
    order = block_order[0]
    slots = jnp.arange(64)
    inverse = jnp.sum(jnp.where(order[None, :] == slots[:, None], slots[None, :], 0), 1)
    length = jnp.sum(jnp.where(jnp.arange(4) == seq, lengths, 0))
    anchors = lax.dynamic_slice_in_dim(global_pos, seq * GSEQ, GSEQ)

    my_ids = lax.dynamic_slice_in_dim(order, member * 4, 4)
    my_lens = jnp.sum(
        jnp.where(my_ids[:, None] // SEQ_BLOCKS == jnp.arange(4)[None, :], lengths[None, :], 0), 1
    )
    slot_pos = (my_ids % SEQ_BLOCKS)[:, None] * BLOCK + jnp.arange(BLOCK)[None, :]
    slot_weight = ((slot_pos < my_lens[:, None]).reshape(ROWS) & (loss_mask == 1)).astype(jnp.int32)
    my_count = jnp.sum(slot_weight)

    high = (my_count // 16).astype(bf16)
    low = (my_count % 16).astype(bf16)
    extra = jnp.concatenate(
        [
            norm_gains,
            norm_biases,
            jnp.broadcast_to(jnp.stack([high, low]), (6, 2)),
            jnp.zeros((6, 122), bf16),
        ],
        1,
    )
    first = lax.all_gather(
        jnp.concatenate([w_qkv, w_attn, extra], 1), "fsdp", axis_index_groups=QUADS, axis=0, tiled=True
    )
    second = lax.all_gather(w_in, "fsdp", axis_index_groups=QUADS, axis=0, tiled=True)
    first_part = jnp.concatenate(
        [lax.dynamic_slice_in_dim(first, quarter * D, D, 1), first[:, 4 * D :]], 1
    )
    second_part = lax.dynamic_slice_in_dim(second, quarter * D, D, 1)
    mine_one = exchange(
        jnp.broadcast_to(first_part[None], (64, 24, EXT)), BOTH, SAME_CORE
    ).reshape(2, D, EXT)
    other_one = swap(mine_one[..., :D])
    side = mine_one[0, :, D:].astype(f32)
    even = jnp.where(core == 0, mine_one[..., :D], other_one)
    odd = jnp.where(core == 0, other_one, mine_one[..., :D])
    wa = odd[1]
    count = jnp.sum(
        jnp.where(jnp.arange(D) % 6 == 0, side[:, 4] * 16.0 + side[:, 5], 0.0)
    )
    mine_two = exchange(
        jnp.broadcast_to(second_part[None], (64, 24, D)), BOTH, SAME_CORE
    ).reshape(2, D, D)
    other_two = swap(mine_two)
    even2 = jnp.where(core == 0, mine_two, other_two)
    odd2 = jnp.where(core == 0, other_two, mine_two)
    win = jnp.stack([even2[0], odd2[0], even2[1], odd2[1]])
    half_keep = lax.dynamic_slice_in_dim(w_out, core * 384, 384, 1)
    half_send = lax.dynamic_slice_in_dim(w_out, (1 - core) * 384, 384, 1)
    half_got = swap(half_send)
    pair_rows = jnp.where(
        core == 0,
        jnp.concatenate([half_keep, half_got], 0),
        jnp.concatenate([half_got, half_keep], 0),
    )
    mine_three = exchange(jnp.broadcast_to(pair_rows[None], (64, 48, 384)), BOTH, SAME_CORE)
    mine_three = mine_three.reshape(2, 32, 48, 384).transpose(1, 0, 2, 3).reshape(4 * D, 384)
    other_three = swap(mine_three)
    wout = jnp.where(
        core == 0,
        jnp.concatenate([mine_three, other_three], 1),
        jnp.concatenate([other_three, mine_three], 1),
    )

    natural = reorder(long_in, inverse)
    packed = jnp.concatenate(
        [
            cot_long,
            teacher,
            jnp.broadcast_to(slot_weight[:, None], (ROWS, 128)).astype(bf16),
        ],
        1,
    )
    packed = reorder(packed, inverse)
    globs = lax.all_gather(
        jnp.concatenate([glob_in, cot_glob], 1), "fsdp", axis_index_groups=QUADS, axis=0, tiled=True
    )
    left = lax.ppermute(natural[ROWS - BLOCK :], "fsdp", TO_RIGHT)
    right = lax.ppermute(natural[:BLOCK], "fsdp", TO_LEFT)
    norms = jnp.concatenate([side[:, :4].T, jnp.zeros((4, D), f32)], 0)
    rows, acts, proj = project(left, natural, right, globs, norms, even, odd)

    start = quarter * ROWS
    place = jnp.stack([quarter, core]).astype(jnp.int32)
    key_pos = start - BLOCK + jnp.arange(768)
    key_ok = (key_pos >= 0) & (key_pos < length)
    glob_ok = anchors < length
    own_glob = jnp.arange(GSEQ) // 32 == quarter
    key_mask = jnp.broadcast_to(
        jnp.where(jnp.concatenate([key_ok, glob_ok]), 0.0, MASKED)[:, None], (EXT, 256)
    )
    self_mask = jnp.broadcast_to(jnp.where(glob_ok & own_glob, 0.0, MASKED)[:, None], (GSEQ, 256))
    picker = (rel_labels[:, None] == jnp.arange(LABELS)[None, :]).astype(f32)
    label_table = jnp.dot(picker, rel_bias[:LABELS], precision=HIGHEST)
    line = jnp.full((HEADS, 512), MASKED, f32)
    line = lax.dynamic_update_slice(line, label_table.T, (0, 44)).reshape(6, 2, 512)
    table = rel_bias[LABELS:]
    long_out, long_lse, part_out, part_lse = attend(place, table, line, key_mask, self_mask, proj)

    sent = jnp.concatenate(
        [part_out, split3(part_lse.reshape(HEADS, 128)), jnp.zeros((12, 128), bf16)], 0
    )
    got = exchange(jnp.broadcast_to(sent[None], (4, 816, 128)), "fsdp", QUADS)
    lses = join3(got[:, D:])
    high = jnp.max(lses, 0)
    glob_lse = high + jnp.log(jnp.sum(jnp.exp(lses - high), 0))
    shares = jnp.pad(jnp.exp(lses - glob_lse), ((0, 0), (0, 4), (0, 0)))
    glob_lse = glob_lse.reshape(6, 1, 256)

    (
        result,
        loss_sum,
        glob_out,
        grad_middle,
        grad_mixed,
        wattn_grad,
        win_send,
        win_keep,
        wout_send,
        wout_keep,
        norm_two,
    ) = feed(
        place, (2.0 / count)[None], rows, long_out, got, shares, packed, globs, norms, wa, win, wout
    )
    loss_sum = loss_sum[0, 0]
    dq, dk, dv, rel = attend_back(
        place, table, line, key_mask, self_mask, proj, grad_mixed, long_lse, glob_out, glob_lse
    )
    one_send, one_keep, grad_nat, back_left, back_right, back_glob, norm_one = project_back(
        place, rows, acts, dq, dk, dv, norms, even, odd, grad_middle, wattn_grad
    )
    grad_table = rel[:, :2, 44 : 44 + LABELS].reshape(HEADS, LABELS)
    grad_own = jnp.sum(rel[:, 2:4, :128], -1).reshape(HEADS)
    grad_other = jnp.sum(rel[:, 4:6, :128], -1).reshape(HEADS)
    from_left = lax.ppermute(back_right, "fsdp", TO_RIGHT).astype(f32)
    from_right = lax.ppermute(back_left, "fsdp", TO_LEFT).astype(f32)
    grad_nat = grad_nat.at[:128].add(from_left).at[384:].add(from_right)
    grad_long = reorder(grad_nat.astype(bf16), order).astype(f32)
    glob_parts = exchange(back_glob.reshape(4 * 32, D), "fsdp", QUADS).reshape(4, 32, D)
    grad_glob = lax.dynamic_slice_in_dim(grad_middle, ROWS + quarter * 32, 32, 0) + jnp.sum(
        glob_parts, 0
    )
    out_long = reorder(result[:ROWS], order)
    out_glob = lax.dynamic_slice_in_dim(result, ROWS + quarter * 32, 32, 0)

    one = reduce_columns(one_keep, one_send)
    two = reduce_columns(win_keep, win_send)
    qkv_grad = one[:3].transpose(1, 0, 2).reshape(6, 3 * D)
    attn_grad = one[3]
    in_grad = two.transpose(1, 0, 2).reshape(6, 4 * D)
    total = (wout_keep.astype(f32) + swap(wout_send).astype(f32)).astype(bf16)
    total = total.reshape(32, 2, 48, 384).transpose(1, 0, 2, 3).reshape(64, 48, 384)
    mine = jnp.sum(exchange(total, BOTH, SAME_CORE).astype(f32), 0)
    other = swap(mine)
    halves = jnp.where(
        core == 0, jnp.concatenate([mine, other], 1), jnp.concatenate([other, mine], 1)
    )
    out_grad = lax.dynamic_slice_in_dim(halves, core * 24, 24, 0)
    label_grad = jnp.dot(picker.T, grad_table.T, precision=HIGHEST)
    rel_grad = jnp.concatenate([label_grad, grad_own[None], grad_other[None]], 0)
    norm_grads = jnp.stack([norm_one[0], norm_two[0], norm_one[1], norm_two[1]], 1)
    rel_total, norm_total, loss_total = lax.psum((rel_grad, norm_grads, loss_sum), BOTH)
    mine_norm = lax.dynamic_slice_in_dim(
        norm_total, (lax.axis_index("dp") * 16 + member) * 6, 6, 0
    )
    return (
        out_long,
        out_glob,
        loss_total / count,
        grad_long,
        grad_glob,
        qkv_grad,
        attn_grad,
        in_grad,
        out_grad,
        mine_norm[:, :2],
        mine_norm[:, 2:],
        rel_total,
    )


def solution(mesh):
    rows = P(BOTH, None)
    in_specs = (rows,) * 11 + (P(), P("dp"), P("dp", None), P("dp"), P(), P(BOTH))
    out_specs = (rows, rows, P(), rows, rows, rows, rows, rows, rows, rows, rows, P())
    return jax.shard_map(shards, mesh=mesh, in_specs=in_specs, out_specs=out_specs, check_vma=False)
```

```python
import jax
import jax.numpy as jnp
from jax import lax
from jax.experimental import pallas as pl
from jax.experimental.pallas import tpu as pltpu
from jax.sharding import PartitionSpec as P

D = 768
HEADS = 12
HEAD = 64
RADIUS = 84
LABELS = 169
BLOCK = 128
SEQ_BLOCKS = 16
GLOBAL_EVERY = 16
GSEQ = 128
ROWS = 512
EXT = 896
EPS = 1e-05
MASKED = -1e30
HIGHEST = lax.Precision.HIGHEST
BOTH = ("dp", "fsdp")
f32 = jnp.float32
bf16 = jnp.bfloat16

QUADS = [[4 * i + j for j in range(4)] for i in range(4)]
SAME_CORE = [[4 * g + 2 * p + c for p in range(2) for g in range(32)] for c in range(2)]
SWAP = [(i, i ^ 1) for i in range(16)]
TO_RIGHT = [(i, i + 1) for i in range(16) if i % 4 < 3]
TO_LEFT = [(i, i - 1) for i in range(16) if i % 4 > 0]


def flip(device, axis, step):
    if axis == "x":
        return device ^ (step << 4)
    if axis == "y":
        return device ^ (step << 1)
    return device ^ ((step >> 1) << 6) ^ ((step & 1) << 3)


PARTNERS = {
    axis: [[(i, flip(i, axis, step)) for i in range(128)] for step in (1, 2, 3)] for axis in "xyz"
}


def exchange(value, axis, groups=None):
    return lax.all_to_all(value, axis, 0, 0, axis_index_groups=groups, tiled=True)


def swap(value):
    return lax.ppermute(value, "fsdp", SWAP)


def relay(values, axis):
    return [lax.ppermute(value, BOTH, pairs) for value, pairs in zip(values, PARTNERS[axis])]


def after(value, *others):
    return lax.optimization_barrier((value,) + others)[0]


ANY = pl.BlockSpec(memory_space=pl.ANY)
SCALARS = pl.BlockSpec(memory_space=pltpu.SMEM)


def cost(microseconds):
    return pl.CostEstimate(
        flops=int(microseconds * 1.1e9),
        bytes_accessed=int(microseconds * 3.6e6),
        transcendentals=0,
    )


def place_parts(spot, parts, shapes, moves, name):
    def kernel(spot_ref, *refs):
        ins, outs = refs[:4], refs[4:]
        for k in range(4):
            for source, which, target in moves(spot_ref[0] ^ k):
                outs[which][target] = ins[k][source]

    vm = pl.BlockSpec(memory_space=pltpu.VMEM)
    return pl.pallas_call(
        kernel,
        in_specs=[SCALARS] + [vm] * 4,
        out_specs=[vm] * len(shapes),
        out_shape=[jax.ShapeDtypeStruct(shape, bf16) for shape in shapes],
        compiler_params=params(32),
        cost_estimate=cost(2),
        name=name,
    )(spot, *parts)


def gather_axis(spot, value, axis, shapes, moves, name):
    return place_parts(spot, [value] + relay([value] * 3, axis), shapes, moves, name)


def encode(value):
    high = value.astype(bf16)
    return high, (value - high.astype(f32)).astype(bf16)


def fold_parts(spot, parts, starts, length, name):
    count = parts[0].shape[0] // 4 * 4
    extra = parts[0].shape[0] - count
    size = count // 4

    def kernel(spot_ref, *refs):
        ins, outs = refs[: len(parts)], refs[len(parts) :]
        for k in range(4):
            for i, start in enumerate(starts(spot_ref[0] ^ k)):
                total = ins[0][pl.ds(start, length)].astype(f32)
                for other in ins[1:]:
                    total = total + other[pl.ds(start, length)].astype(f32)
                outs[k][i * length : (i + 1) * length] = total.astype(bf16)
        if extra:
            small = [ref[count, :8].astype(f32) + ref[count, 8:16].astype(f32) for ref in ins]
            small = [small[i] + small[i + 1] for i in range(0, len(ins), 2)]
            high, low = encode(small[0] if len(small) == 1 else small[0] + small[1])
            for out in outs:
                out[size, :8] = high
                out[size, 8:16] = low
                out[size, 16:] = jnp.zeros((8, D), bf16)

    vm = pl.BlockSpec(memory_space=pltpu.VMEM)
    return pl.pallas_call(
        kernel,
        in_specs=[SCALARS] + [vm] * len(parts),
        out_specs=[vm] * 4,
        out_shape=[jax.ShapeDtypeStruct((size + extra, 24, D), bf16)] * 4,
        compiler_params=params(32),
        cost_estimate=cost(2),
        name=name,
    )(spot, *parts)


def add_pairs(pairs, name):
    def kernel(*refs):
        for i in range(len(pairs)):
            ours, theirs = refs[2 * i][...].astype(f32), refs[2 * i + 1][...].astype(f32)
            refs[2 * len(pairs) + i][...] = (ours + theirs).astype(bf16)

    block = pl.BlockSpec((384, D), lambda i: (i, 0))
    return pl.pallas_call(
        kernel,
        grid=(4,),
        in_specs=[block] * (2 * len(pairs)),
        out_specs=[block] * len(pairs),
        out_shape=[jax.ShapeDtypeStruct((2 * D, D), bf16)] * len(pairs),
        compiler_params=params(32),
        cost_estimate=cost(4),
        name=name,
    )(*[part.reshape(2 * D, D) for pair in pairs for part in pair])


def scatter_axis(spot, parts, axis, starts, length, name):
    cut = fold_parts(spot, parts, starts, length, name)
    return [cut[0]] + relay(cut[1:], axis)


def pack_rows(result, nat, from_left, from_right):
    def kernel(result_ref, nat_ref, left_ref, right_ref, out):
        for block in range(4):
            rows = slice(128 * block, 128 * block + 128)
            grad = nat_ref[rows]
            if block == 0:
                grad = grad + left_ref[...].astype(f32)
            if block == 3:
                grad = grad + right_ref[...].astype(f32)
            for piece in range(16):
                low = 8 * piece
                out[4 * piece + block, :, D:] = grad[low : low + 8].astype(bf16)
                out[4 * piece + block, :, :D] = result_ref[
                    128 * block + low : 128 * block + low + 8
                ]

    vm = pl.BlockSpec(memory_space=pltpu.VMEM)
    return pl.pallas_call(
        kernel,
        in_specs=[vm] * 4,
        out_specs=vm,
        out_shape=jax.ShapeDtypeStruct((64, 8, 2 * D), bf16),
        compiler_params=params(32),
        cost_estimate=cost(3),
        name="pack_rows",
    )(result, nat, from_left, from_right)


def unpack_rows(value):
    def kernel(value_ref, long_ref, grad_ref):
        for block in range(4):
            for piece in range(16):
                low = 128 * block + 8 * piece
                long_ref[low : low + 8] = value_ref[4 * piece + block, :, :D]
                grad_ref[low : low + 8] = value_ref[4 * piece + block, :, D:].astype(f32)

    vm = pl.BlockSpec(memory_space=pltpu.VMEM)
    return pl.pallas_call(
        kernel,
        in_specs=[vm],
        out_specs=[vm] * 2,
        out_shape=[jax.ShapeDtypeStruct((ROWS, D), bf16), jax.ShapeDtypeStruct((ROWS, D), f32)],
        compiler_params=params(32),
        cost_estimate=cost(3),
        name="unpack_rows",
    )(value)


def total_of(parts):
    total = parts[0].astype(f32)
    for part in parts[1:]:
        total = total + part.astype(f32)
    return total


def pieces(rows):
    width = rows.shape[-1]
    return rows.reshape(4, 16, 8, width).transpose(1, 0, 2, 3).reshape(64, 8, width)


def unpieces(value):
    width = value.shape[-1]
    return value.reshape(16, 4, 8, width).transpose(1, 0, 2, 3).reshape(ROWS, width)


def reorder(rows, index):
    spread = exchange(pieces(rows), "fsdp")
    return unpieces(exchange(spread[index], "fsdp"))


def split3(value):
    high = value.astype(bf16)
    rest = value - high.astype(f32)
    mid = rest.astype(bf16)
    low = (rest - mid.astype(f32)).astype(bf16)
    return jnp.concatenate([high, mid, low], 0)


def join3(value):
    value = value.astype(f32)
    return value[:, :HEADS] + value[:, HEADS : 2 * HEADS] + value[:, 2 * HEADS : 3 * HEADS]


def dot_nn(a, b):
    return lax.dot_general(a, b, (((1,), (0,)), ((), ())), preferred_element_type=f32)


def dot_nt(a, b):
    return lax.dot_general(a, b, (((1,), (1,)), ((), ())), preferred_element_type=f32)


def dot_tn(a, b):
    return lax.dot_general(a, b, (((0,), (0,)), ((), ())), preferred_element_type=f32)


def whole(shape):
    zeros = (0,) * len(shape)
    return pl.BlockSpec(shape, lambda *_: zeros, pipeline_mode=pl.Buffered(1))


def params(megabytes):
    return pltpu.CompilerParams(vmem_limit_bytes=megabytes << 20)


def normalise(values):
    centre = jnp.mean(values, -1, keepdims=True)
    centred = values - centre
    spread = jnp.mean(centred * centred, -1, keepdims=True)
    factor = lax.rsqrt(spread + EPS)
    return centred * factor, factor


def load_quarters(core, mine, other, target, sems, count):
    copies = []
    for p in range(2):
        copies.append(pltpu.make_async_copy(mine.at[p, :, pl.ds(0, D)], target.at[2 * p + core], sems.at[2 * p]))
        copies.append(
            pltpu.make_async_copy(
                other.at[p, :, pl.ds(0, D)], target.at[2 * p + 1 - core], sems.at[2 * p + 1]
            )
        )
    for copy in copies:
        copy.start()
    return copies


def project_kernel(
    place, left, nat, right, globs, norms, mine, other, rows_out, acts_out, proj_out, w, sems
):
    copies = load_quarters(place[1], mine, other, w, sems, 4)
    rows_out[:128] = left[...]
    rows_out[128:640] = nat[...]
    rows_out[640:768] = right[...]
    rows_out[768:] = globs[:, :D]
    normal, _ = normalise(rows_out[...].astype(f32))
    acts = (normal * norms[0:1] + norms[2:3]).astype(bf16)
    acts_out[...] = acts
    for copy in copies:
        copy.wait()
    for i in range(3):
        proj_out[:, i * D : i * D + D] = dot_nn(acts, w[i]).astype(bf16)


def project(place, left, nat, right, globs, norms, mine, other):
    vm = pl.BlockSpec(memory_space=pltpu.VMEM)
    return pl.pallas_call(
        project_kernel,
        in_specs=[SCALARS] + [vm] * 5 + [ANY] * 2,
        scratch_shapes=[pltpu.VMEM((4, D, D), bf16), pltpu.SemaphoreType.DMA((4,))],
        out_shape=(
            jax.ShapeDtypeStruct((EXT, D), bf16),
            jax.ShapeDtypeStruct((EXT, D), bf16),
            jax.ShapeDtypeStruct((EXT, 3 * D), bf16),
        ),
        compiler_params=params(50),
        cost_estimate=cost(9),
        name="project",
    )(place, left, nat, right, globs, norms, mine, other)


def stack_heads(rows):
    first = lax.broadcasted_iota(jnp.int32, rows.shape, 1) < HEAD
    zero = jnp.zeros_like(rows)
    return jnp.concatenate([jnp.where(first, rows, zero), jnp.where(first, zero, rows)], 0)


def merge_heads(value):
    first = lax.broadcasted_iota(jnp.int32, (128, 128), 0) < HEAD
    return jnp.where(first, value[:, :128], value[:, 128:]).T


def band_tile(line):
    tiles = []
    for head in range(2):
        spread = jnp.broadcast_to(line[head : head + 1], (BLOCK, 512))
        rolled = pltpu.roll(spread, 0, 1, stride=1, stride_axis=0)
        tiles.append(
            jnp.concatenate([rolled[:, 128 * i : 128 * i + 128].T for i in range(3)], 0)
        )
    return jnp.concatenate(tiles, 1)


def pair_row(first, second):
    lane = lax.broadcasted_iota(jnp.int32, (1, 256), 1)
    return jnp.where(lane < 128, first, second)


def long_owned(run):
    key = lax.broadcasted_iota(jnp.int32, (128, 256), 0)
    lane = lax.broadcasted_iota(jnp.int32, (128, 256), 1)
    return key == run + lax.shift_right_logical(lane & 127, 4)


def cross_owned(run):
    key = lax.broadcasted_iota(jnp.int32, (ROWS, 256), 0)
    lane = lax.broadcasted_iota(jnp.int32, (ROWS, 256), 1)
    return run + lax.shift_right_logical(key, 4) == (lane & 127)


def attend_kernel(
    place, table, line, key_mask, self_mask, q, k, v, out, lse, glob_out, glob_lse, band
):
    pair = pl.program_id(0)
    run = place[0] * 32
    own = pair_row(table[0, 2 * pair], table[0, 2 * pair + 1])
    other = pair_row(table[1, 2 * pair], table[1, 2 * pair + 1])
    band[...] = band_tile(line[0])
    values = v[...].T
    for j in range(4):
        low = 128 * j
        query = stack_heads(q[128 + low : 256 + low, :] * 0.125)
        near = dot_nt(k[low : low + 384, :], query) + (band[...] + key_mask[low : low + 384, :])
        far = dot_nt(k[768:, :], query) + (
            jnp.where(long_owned(run + 8 * j), own, other) + key_mask[768:, :]
        )
        top = jnp.maximum(jnp.max(near, 0, keepdims=True), jnp.max(far, 0, keepdims=True))
        near = jnp.exp(near - top)
        far = jnp.exp(far - top)
        total = jnp.sum(near, 0, keepdims=True) + jnp.sum(far, 0, keepdims=True)
        share = 1.0 / total
        got = dot_nn(values[:, low : low + 384], (near * share).astype(bf16)) + dot_nn(
            values[:, 768:], (far * share).astype(bf16)
        )
        out[low : low + 128, :] = merge_heads(got).astype(bf16)
        lse[0, j : j + 1, :] = top + jnp.log(total)
    query = stack_heads(q[768:, :] * 0.125)
    near = dot_nt(k[128:640, :], query) + (
        jnp.where(cross_owned(run), own, other) + key_mask[128:640, :]
    )
    far = dot_nt(k[768:, :], query) + self_mask[...]
    top = jnp.maximum(jnp.max(near, 0, keepdims=True), jnp.max(far, 0, keepdims=True))
    near = jnp.exp(near - top)
    far = jnp.exp(far - top)
    total = jnp.sum(near, 0, keepdims=True) + jnp.sum(far, 0, keepdims=True)
    share = 1.0 / total
    got = dot_nn(values[:, 128:640], (near * share).astype(bf16)) + dot_nn(
        values[:, 768:], (far * share).astype(bf16)
    )
    first = lax.broadcasted_iota(jnp.int32, (128, 128), 0) < HEAD
    glob_out[...] = jnp.where(first, got[:, :128], got[:, 128:]).astype(bf16)
    glob_lse[0] = top + jnp.log(total)


def column(width, offset):
    return pl.BlockSpec((width, 128), lambda h: (0, h + offset))


def attend(place, table, line, key_mask, self_mask, proj):
    return pl.pallas_call(
        attend_kernel,
        grid=(6,),
        in_specs=[
            SCALARS,
            SCALARS,
            pl.BlockSpec((1, 2, 512), lambda h: (h, 0, 0)),
            whole((EXT, 256)),
            whole((128, 256)),
            column(EXT, 0),
            column(EXT, 6),
            column(EXT, 12),
        ],
        out_specs=[
            column(ROWS, 0),
            pl.BlockSpec((1, 4, 256), lambda h: (h, 0, 0)),
            pl.BlockSpec((128, 128), lambda h: (h, 0)),
            pl.BlockSpec((1, 1, 256), lambda h: (h, 0, 0)),
        ],
        out_shape=(
            jax.ShapeDtypeStruct((ROWS, D), bf16),
            jax.ShapeDtypeStruct((6, 4, 256), f32),
            jax.ShapeDtypeStruct((D, 128), bf16),
            jax.ShapeDtypeStruct((6, 1, 256), f32),
        ),
        scratch_shapes=[pltpu.VMEM((384, 256), f32)],
        compiler_params=params(40),
        cost_estimate=cost(15),
        name="attend",
    )(place, table, line, key_mask, self_mask, proj, proj, proj)


def fold_band(tile):
    rows = jnp.concatenate([tile[128 * i : 128 * i + 128].T for i in range(3)], 1)
    rows = jnp.concatenate([rows, jnp.zeros((BLOCK, 128), f32)], 1)
    total = rows[:8]
    for a in range(1, 16):
        total = total + pltpu.roll(rows[8 * a : 8 * a + 8], 512 - 8 * a, 1)
    row = lax.broadcasted_iota(jnp.int32, (8, 512), 0)
    for bit in (1, 2, 4):
        total = jnp.where((row & bit) != 0, pltpu.roll(total, 512 - bit, 1), total)
    return jnp.sum(total, 0, keepdims=True)


def attend_back_kernel(
    place,
    table,
    line,
    key_mask,
    self_mask,
    q,
    k,
    v,
    grad,
    lse,
    glob_out,
    glob_lse,
    dq,
    dk,
    dv,
    rel,
    band,
    band_sum,
    key_sum,
    value_sum,
):
    pair = pl.program_id(0)
    run = place[0] * 32
    own = pair_row(table[0, 2 * pair], table[0, 2 * pair + 1])
    other = pair_row(table[1, 2 * pair], table[1, 2 * pair + 1])
    band[...] = band_tile(line[0])
    keys = k[...].T
    band_sum[...] = jnp.zeros_like(band_sum)
    key_sum[...] = jnp.zeros_like(key_sum)
    value_sum[...] = jnp.zeros_like(value_sum)
    owned_sum = jnp.zeros((1, 256), f32)
    other_sum = jnp.zeros((1, 256), f32)
    dq[:128] = jnp.zeros((128, 128), bf16)
    dq[640:768] = jnp.zeros((128, 128), bf16)
    for j in range(4):
        low = 128 * j
        query = stack_heads(q[128 + low : 256 + low, :] * 0.125)
        back = stack_heads(grad[low : low + 128, :])
        near = dot_nt(k[low : low + 384, :], query) + (band[...] + key_mask[low : low + 384, :])
        owned = long_owned(run + 8 * j)
        far = dot_nt(k[768:, :], query) + (jnp.where(owned, own, other) + key_mask[768:, :])
        top = lse[0, j : j + 1, :]
        near = jnp.exp(near - top)
        far = jnp.exp(far - top)
        near_d = dot_nt(v[low : low + 384, :], back)
        far_d = dot_nt(v[768:, :], back)
        delta = jnp.sum(near * near_d, 0, keepdims=True) + jnp.sum(far * far_d, 0, keepdims=True)
        near_d = (near * (near_d - delta)).astype(bf16)
        far_d = (far * (far_d - delta)).astype(bf16)
        key_sum[low : low + 384, :] += dot_nn(near_d, query)
        value_sum[low : low + 384, :] += dot_nn(near.astype(bf16), back)
        key_sum[768:, :] += dot_nn(far_d, query)
        value_sum[768:, :] += dot_nn(far.astype(bf16), back)
        got = dot_nn(keys[:, low : low + 384], near_d) + dot_nn(keys[:, 768:], far_d)
        dq[128 + low : 256 + low, :] = (merge_heads(got) * 0.125).astype(bf16)
        band_sum[...] += near_d.astype(f32)
        far_d = far_d.astype(f32)
        owned_sum += jnp.sum(jnp.where(owned, far_d, 0.0), 0, keepdims=True)
        other_sum += jnp.sum(jnp.where(owned, 0.0, far_d), 0, keepdims=True)
    query = stack_heads(q[768:, :] * 0.125)
    back = stack_heads(grad[ROWS:, :])
    owned = cross_owned(run)
    near = dot_nt(k[128:640, :], query) + (jnp.where(owned, own, other) + key_mask[128:640, :])
    far = dot_nt(k[768:, :], query) + self_mask[...]
    top = glob_lse[0]
    near = jnp.exp(near - top)
    far = jnp.exp(far - top)
    near_d = dot_nt(v[128:640, :], back)
    far_d = dot_nt(v[768:, :], back)
    product = grad[ROWS:, :].astype(f32).T * glob_out[...].astype(f32)
    delta = jnp.concatenate(
        [
            jnp.sum(product[:HEAD], 0, keepdims=True),
            jnp.sum(product[HEAD:], 0, keepdims=True),
        ],
        1,
    )
    near_d = (near * (near_d - delta)).astype(bf16)
    far_d = (far * (far_d - delta)).astype(bf16)
    key_sum[128:640, :] += dot_nn(near_d, query)
    value_sum[128:640, :] += dot_nn(near.astype(bf16), back)
    key_sum[768:, :] += dot_nn(far_d, query)
    value_sum[768:, :] += dot_nn(far.astype(bf16), back)
    got = dot_nn(keys[:, 128:640], near_d) + dot_nn(keys[:, 768:], far_d)
    dq[768:, :] = (merge_heads(got) * 0.125).astype(bf16)
    near_d = near_d.astype(f32)
    owned_sum += jnp.sum(jnp.where(owned, near_d, 0.0), 0, keepdims=True)
    other_sum += jnp.sum(jnp.where(owned, 0.0, near_d), 0, keepdims=True)
    dk[...] = key_sum[...].astype(bf16)
    dv[...] = value_sum[...].astype(bf16)
    rel[0] = jnp.zeros((8, 512), f32)
    for head in range(2):
        lanes = slice(128 * head, 128 * head + 128)
        rel[0, head : head + 1, :] = fold_band(band_sum[:, lanes])
        rel[0, 2 + head : 3 + head, :128] = owned_sum[:, lanes]
        rel[0, 4 + head : 5 + head, :128] = other_sum[:, lanes]


def attend_back(place, table, line, key_mask, self_mask, proj, grad, lse, glob_out, glob_lse):
    return pl.pallas_call(
        attend_back_kernel,
        grid=(6,),
        in_specs=[
            SCALARS,
            SCALARS,
            pl.BlockSpec((1, 2, 512), lambda h: (h, 0, 0)),
            whole((EXT, 256)),
            whole((128, 256)),
            column(EXT, 0),
            column(EXT, 6),
            column(EXT, 12),
            column(640, 0),
            pl.BlockSpec((1, 4, 256), lambda h: (h, 0, 0)),
            pl.BlockSpec((128, 128), lambda h: (h, 0)),
            pl.BlockSpec((1, 1, 256), lambda h: (h, 0, 0)),
        ],
        out_specs=[
            column(EXT, 0),
            column(EXT, 0),
            column(EXT, 0),
            pl.BlockSpec((1, 8, 512), lambda h: (h, 0, 0)),
        ],
        out_shape=(
            jax.ShapeDtypeStruct((EXT, D), bf16),
            jax.ShapeDtypeStruct((EXT, D), bf16),
            jax.ShapeDtypeStruct((EXT, D), bf16),
            jax.ShapeDtypeStruct((6, 8, 512), f32),
        ),
        scratch_shapes=[
            pltpu.VMEM((384, 256), f32),
            pltpu.VMEM((384, 256), f32),
            pltpu.VMEM((EXT, 128), f32),
            pltpu.VMEM((EXT, 128), f32),
        ],
        compiler_params=params(48),
        cost_estimate=cost(21),
        name="attend_back",
    )(place, table, line, key_mask, self_mask, proj, proj, proj, grad, lse, glob_out, glob_lse)


def feed_kernel(
    place,
    coef,
    rows,
    long_out,
    parts,
    shares,
    packed,
    globs,
    norms,
    wout,
    first_mine,
    first_other,
    in_mine,
    in_other,
    result_out,
    loss_out,
    glob_out,
    middle_grad_out,
    mixed_grad_out,
    wattn_grad,
    win_send,
    win_keep,
    wout_send,
    wout_keep,
    norm_grads,
    mixed,
    acts,
    normal,
    total,
    hidden,
    slope,
    grad_z,
    grad_acts,
    factor,
    wa,
    win,
    sem,
    sems,
):
    step = pl.program_id(0)
    core = place[1]


    def attn_copy(source):
        return pltpu.make_async_copy(source.at[1, :, pl.ds(0, D)], wa, sem)

    quarter = place[0]
    forward = step < 4
    late = jnp.maximum(step - 4, 0)
    chunk = jnp.where(
        forward, step, jnp.where(late < 2, 2 * late + 1 - core, 2 * (late - 2) + core)
    )

    def owned():
        row = lax.broadcasted_iota(jnp.int32, (640, 1), 0)
        first = ROWS + quarter * 32
        return (row < ROWS) | ((row >= first) & (row < first + 32))

    @pl.when(step == 0)
    def _():
        @pl.when(core == 1)
        def _():
            attn_copy(first_mine).start()

        @pl.when(core == 0)
        def _():
            attn_copy(first_other).start()

        load_quarters(core, in_mine, in_other, win, sems, 4)
        mixed[:ROWS] = long_out[...]
        for pair in range(6):
            sums = jnp.zeros((128, 128), f32)
            top = lax.broadcasted_iota(jnp.int32, (128, 128), 0) < HEAD
            for source in range(4):
                share = jnp.where(
                    top,
                    shares[source, 2 * pair : 2 * pair + 1, :],
                    shares[source, 2 * pair + 1 : 2 * pair + 2, :],
                )
                sums = sums + parts[source, 128 * pair : 128 * pair + 128, :].astype(f32) * share
            glob_out[128 * pair : 128 * pair + 128, :] = sums.astype(bf16)
            mixed[ROWS:, 128 * pair : 128 * pair + 128] = sums.T.astype(bf16)
        attn_copy(first_mine).wait()
        middle = dot_nn(mixed[...], wa[...])
        middle = middle + jnp.concatenate(
            [rows[128:640].astype(f32), rows[768:].astype(f32)], 0
        )
        total[...] = middle
        base, scale = normalise(middle)
        normal[...] = base
        factor[...] = scale
        acts[...] = (base * norms[1:2] + norms[3:4]).astype(bf16)
        for p in range(4):
            pltpu.make_async_copy(in_mine.at[0, :, pl.ds(0, D)], win.at[0], sems.at[p]).wait()

    @pl.when(forward)
    def _():
        inner = dot_nn(acts[...], win[chunk])
        half = 0.5 + 0.5 * lax.erf(inner * 0.7071067811865476)
        slope[chunk] = half + inner * (jnp.exp(-0.5 * inner * inner) * 0.3989422804014327)
        bits = (inner * half).astype(bf16)
        hidden[chunk] = bits
        total[...] += dot_nn(bits, wout[...])

    @pl.when(step == 3)
    def _():
        result = total[...]
        result_out[...] = result.astype(bf16)
        weight = packed[:, 2 * D : 2 * D + 1].astype(f32)
        error = result[:ROWS] - packed[:, D : 2 * D].astype(f32)
        masked = weight * error
        loss_out[...] = jnp.broadcast_to(
            jnp.sum(jnp.sum(masked * error, 0, keepdims=True), 1, keepdims=True), (8, 128)
        )
        grad = jnp.concatenate(
            [packed[:, :D].astype(f32) + coef[0] * masked, globs[:, D:].astype(f32)], 0
        )
        total[...] = grad
        grad_z[...] = grad.astype(bf16)
        grad_acts[...] = jnp.zeros_like(grad_acts)

    @pl.when(step >= 4)
    def _():
        keep_rows = owned()
        grad_inner = (dot_nt(grad_z[...], wout[...]) * slope[chunk]).astype(bf16)
        zeros = jnp.zeros_like(grad_inner)
        grad_acts[...] += dot_nt(grad_inner, win[chunk])
        part = dot_tn(acts[...], jnp.where(keep_rows, grad_inner, zeros)).astype(bf16)

        @pl.when(late < 2)
        def _():
            win_send[0] = part

        @pl.when(late >= 2)
        def _():
            win_keep[0] = part

        part = dot_tn(hidden[chunk], jnp.where(keep_rows, grad_z[...], zeros))
        part = part.reshape(8, 2, 2, 24, D)
        for p in range(2):
            even, odd = part[:, p, 0], part[:, p, 1]
            wout_keep[p] = jnp.where(core == 0, even, odd).astype(bf16)
            wout_send[p] = jnp.where(core == 0, odd, even).astype(bf16)

    @pl.when(step == 7)
    def _():
        keep_rows = owned()
        grad = grad_acts[...]
        base = normal[...]
        mine = jnp.where(keep_rows, grad, 0.0)
        norm_grads[0:1, :] = jnp.sum(mine * base, 0, keepdims=True)
        norm_grads[1:2, :] = jnp.sum(mine, 0, keepdims=True)
        scaled = grad * norms[1:2]
        first = jnp.mean(scaled, -1, keepdims=True)
        second = jnp.mean(scaled * base, -1, keepdims=True)
        middle = total[...] + factor[...] * (scaled - first - base * second)
        middle_grad_out[...] = middle
        branch = middle.astype(bf16)
        mixed_grad_out[...] = dot_nt(branch, wa[...]).astype(bf16)
        wattn_grad[...] = dot_tn(
            mixed[...], jnp.where(keep_rows, branch, jnp.zeros_like(branch))
        ).astype(bf16)


def feed(place, coef, rows, long_out, parts, shares, packed, globs, norms, *weights):
    def chunk(t, place):
        late = jnp.maximum(t - 4, 0)
        core = place[1]
        back = jnp.where(late < 2, 2 * late + 1 - core, 2 * (late - 2) + core)
        return jnp.where(t < 4, t, back)

    def back_chunk(t, place):
        return chunk(jnp.maximum(t, 4), place)

    def fixed(shape):
        zeros = (0,) * len(shape)
        return pl.BlockSpec(shape, lambda t, place: zeros, pipeline_mode=pl.Buffered(1))

    return pl.pallas_call(
        feed_kernel,
        grid_spec=pltpu.PrefetchScalarGridSpec(
            num_scalar_prefetch=1,
            grid=(8,),
            in_specs=[
                SCALARS,
                fixed((EXT, D)),
                fixed((ROWS, D)),
                fixed((4, 816, 128)),
                fixed((4, 16, 128)),
                fixed((ROWS, 2 * D + 128)),
                fixed((128, 2 * D)),
                fixed((8, D)),
                pl.BlockSpec((D, D), lambda t, place: (chunk(t, place), 0)),
                ANY,
                ANY,
                ANY,
                ANY,
            ],
            out_specs=[
                fixed((640, D)),
                fixed((8, 128)),
                fixed((D, 128)),
                fixed((640, D)),
                fixed((640, D)),
                fixed((D, D)),
                pl.BlockSpec((1, D, D), lambda t, place: (jnp.clip(t - 4, 0, 1), 0, 0)),
                pl.BlockSpec((1, D, D), lambda t, place: (jnp.clip(t - 6, 0, 1), 0, 0)),
                pl.BlockSpec((2, 8, 24, D), lambda t, place: (0, back_chunk(t, place), 0, 0)),
                pl.BlockSpec((2, 8, 24, D), lambda t, place: (0, back_chunk(t, place), 0, 0)),
                fixed((8, D)),
            ],
            scratch_shapes=[
                pltpu.VMEM((640, D), bf16),
                pltpu.VMEM((640, D), bf16),
                pltpu.VMEM((640, D), f32),
                pltpu.VMEM((640, D), f32),
                pltpu.VMEM((4, 640, D), bf16),
                pltpu.VMEM((4, 640, D), f32),
                pltpu.VMEM((640, D), bf16),
                pltpu.VMEM((640, D), f32),
                pltpu.VMEM((640, 1), f32),
                pltpu.VMEM((D, D), bf16),
                pltpu.VMEM((4, D, D), bf16),
                pltpu.SemaphoreType.DMA,
                pltpu.SemaphoreType.DMA((4,)),
            ],
        ),
        out_shape=(
            jax.ShapeDtypeStruct((640, D), bf16),
            jax.ShapeDtypeStruct((8, 128), f32),
            jax.ShapeDtypeStruct((D, 128), bf16),
            jax.ShapeDtypeStruct((640, D), f32),
            jax.ShapeDtypeStruct((640, D), bf16),
            jax.ShapeDtypeStruct((D, D), bf16),
            jax.ShapeDtypeStruct((2, D, D), bf16),
            jax.ShapeDtypeStruct((2, D, D), bf16),
            jax.ShapeDtypeStruct((2, 32, 24, D), bf16),
            jax.ShapeDtypeStruct((2, 32, 24, D), bf16),
            jax.ShapeDtypeStruct((8, D), f32),
        ),
        compiler_params=params(60),
        cost_estimate=cost(43),
        name="feed",
    )(place, coef, rows, long_out, parts, shares, packed, globs, norms, *weights)


def project_back_kernel(
    place, rows, acts, dq, dk, dv, norms, middle_grad, wattn_grad, rel, norm_two, loss,
    mine, other, send, keep, nat, left, right, globs, w, sems, small,
):
    core = place[1]
    copies = load_quarters(core, mine, other, w, sems, 4)
    both = acts[...]
    grads = [dot_tn(both, ref[...]).reshape(32, 24, D).astype(bf16) for ref in (dq, dk, dv)]
    grads.append(wattn_grad[...].astype(f32).reshape(32, 24, D).astype(bf16))
    first, second = slice(0, 32), slice(32, 64)

    @pl.when(core == 0)
    def _():
        keep[first], keep[second], send[first], send[second] = grads[0], grads[2], grads[1], grads[3]

    @pl.when(core == 1)
    def _():
        keep[first], keep[second], send[first], send[second] = grads[1], grads[3], grads[0], grads[2]

    for copy in copies:
        copy.wait()
    grad = dot_nt(dq[...], w[0]) + dot_nt(dk[...], w[1]) + dot_nt(dv[...], w[2])
    base, factor = normalise(rows[...].astype(f32))
    small[0:1, :] = jnp.sum(grad * base, 0, keepdims=True)
    small[1:2, :] = jnp.sum(grad, 0, keepdims=True)
    small[2:4, :] = norm_two[0:2, :]
    for n in range(HEADS):
        low = 256 * (n % 3)
        small[4 + n // 3 : 5 + n // 3, low : low + 256] = rel[n // 2, n % 2 : n % 2 + 1, :256]
    lane = lax.broadcasted_iota(jnp.int32, (1, 128), 1)
    line = jnp.where(lane == 24, loss[0:1, :], small[4:5, :128])
    for n in range(2 * HEADS):
        head, row = n % HEADS, 2 + 2 * (n // HEADS)
        part = rel[head // 2, row + head % 2 : row + head % 2 + 1, :128]
        line = jnp.where(lane == n, jnp.sum(part, 1, keepdims=True), line)
    small[4:5, :128] = line
    high, low = encode(small[...])
    for ref in (keep, send):
        ref[64, :8] = high
        ref[64, 8:16] = low
        ref[64, 16:] = jnp.zeros((8, D), bf16)
    scaled = grad * norms[0:1]
    first = jnp.mean(scaled, -1, keepdims=True)
    second = jnp.mean(scaled * base, -1, keepdims=True)
    back = factor * (scaled - first - base * second)
    nat[...] = back[128:640] + middle_grad[:ROWS]
    left[...] = back[:128].astype(bf16)
    right[...] = back[640:768].astype(bf16)
    globs[...] = back[768:]


def project_back(*operands):
    vm = pl.BlockSpec(memory_space=pltpu.VMEM)
    return pl.pallas_call(
        project_back_kernel,
        in_specs=[SCALARS] + [vm] * 11 + [ANY] * 2,
        scratch_shapes=[
            pltpu.VMEM((4, D, D), bf16),
            pltpu.SemaphoreType.DMA((4,)),
            pltpu.VMEM((8, D), f32),
        ],
        out_shape=(
            jax.ShapeDtypeStruct((65, 24, D), bf16),
            jax.ShapeDtypeStruct((65, 24, D), bf16),
            jax.ShapeDtypeStruct((ROWS, D), f32),
            jax.ShapeDtypeStruct((128, D), bf16),
            jax.ShapeDtypeStruct((128, D), bf16),
            jax.ShapeDtypeStruct((128, D), f32),
        ),
        compiler_params=params(56),
        cost_estimate=cost(15),
        name="project_back",
    )(*operands)


def shards(
    long_in,
    glob_in,
    cot_long,
    cot_glob,
    teacher,
    w_qkv,
    w_attn,
    w_in,
    w_out,
    norm_gains,
    norm_biases,
    rel_bias,
    lengths,
    block_order,
    global_pos,
    rel_labels,
    loss_mask,
):
    member = lax.axis_index("fsdp")
    core = member % 2
    quarter = member % 4
    seq = member // 4
    order = block_order[0]
    slots = jnp.arange(64)
    inverse = jnp.sum(jnp.where(order[None, :] == slots[:, None], slots[None, :], 0), 1)
    length = jnp.sum(jnp.where(jnp.arange(4) == seq, lengths, 0))
    anchors = lax.dynamic_slice_in_dim(global_pos, seq * GSEQ, GSEQ)

    my_ids = lax.dynamic_slice_in_dim(order, member * 4, 4)
    my_lens = jnp.sum(
        jnp.where(my_ids[:, None] // SEQ_BLOCKS == jnp.arange(4)[None, :], lengths[None, :], 0), 1
    )
    slot_pos = (my_ids % SEQ_BLOCKS)[:, None] * BLOCK + jnp.arange(BLOCK)[None, :]
    slot_weight = ((slot_pos < my_lens[:, None]).reshape(ROWS) & (loss_mask == 1)).astype(jnp.int32)
    my_count = jnp.sum(slot_weight)

    device = lax.axis_index("dp") * 16 + member
    spot = {
        "x": ((device >> 4) & 3)[None],
        "y": ((device >> 1) & 3)[None],
        "z": (((device >> 6) & 1) * 2 + ((device >> 3) & 1))[None],
    }
    counted = jnp.stack([my_count // 16, my_count % 16]).astype(bf16)
    extra = jnp.concatenate([norm_gains, norm_biases, jnp.broadcast_to(counted, (6, 2))], 1)
    extra = jnp.broadcast_to(jnp.pad(extra, ((0, 6), (0, D - 6))), (4, 12, D))
    opening = jnp.concatenate(
        [
            jnp.concatenate([w_qkv, w_attn], 1).reshape(6, 4, D).transpose(1, 0, 2),
            w_in.reshape(6, 4, D).transpose(1, 0, 2),
            extra,
            jnp.broadcast_to(jnp.concatenate([glob_in, cot_glob])[None], (4, 64, D)),
        ],
        1,
    )
    opening = exchange(opening, "fsdp", QUADS)
    spread_long = exchange(pieces(after(long_in, opening)), "fsdp")
    first = jnp.concatenate([opening[:, :6].reshape(24, D), opening[:, 12:18, :128].reshape(24, 128)], 1)
    globs = jnp.concatenate([opening[:, 24:56], opening[:, 56:]], 2).reshape(GSEQ, 2 * D)
    wout = jnp.concatenate([w_out, jnp.zeros((24, D), bf16)], 0)
    wout = lax.all_gather(wout, "fsdp", axis=0, tiled=True)
    wout = wout.reshape(16, 48, D)[:, :24].reshape(384, D)
    natural = unpieces(exchange(spread_long[inverse], "fsdp"))
    every = slice(None)
    start = quarter * ROWS
    place = jnp.stack([quarter, core]).astype(jnp.int32)
    key_pos = start - BLOCK + jnp.arange(768)
    key_ok = (key_pos >= 0) & (key_pos < length)
    glob_ok = anchors < length
    own_glob = jnp.arange(GSEQ) // 32 == quarter
    key_mask = jnp.broadcast_to(
        jnp.where(jnp.concatenate([key_ok, glob_ok]), 0.0, MASKED)[:, None], (EXT, 256)
    )
    self_mask = jnp.broadcast_to(jnp.where(glob_ok & own_glob, 0.0, MASKED)[:, None], (GSEQ, 256))
    picker = (rel_labels[:, None] == jnp.arange(LABELS)[None, :]).astype(f32)
    label_table = jnp.dot(picker, rel_bias[:LABELS], precision=HIGHEST)
    line = jnp.full((HEADS, 512), MASKED, f32)
    line = lax.dynamic_update_slice(line, label_table.T, (0, 44)).reshape(6, 2, 512)
    table = rel_bias[LABELS:]
    second = opening[:, 6:12].reshape(24, D)
    (first,) = gather_axis(
        spot["y"], first, "y", [(2, 2, 24, EXT)], lambda s: [(..., 0, (s & 1, s >> 1))], "first_y"
    )
    (second,) = gather_axis(
        spot["z"], second, "z", [(2, 2, 24, D)], lambda s: [(..., 0, (s >> 1, s & 1))], "second_z"
    )
    first, second = lax.optimization_barrier((first, second))
    (first,) = gather_axis(
        spot["z"],
        first,
        "z",
        [(2, 2, 2, 2, 24, EXT)],
        lambda s: [(..., 0, (every, s >> 1, s & 1))],
        "first_z",
    )
    (second,) = gather_axis(
        spot["x"],
        second,
        "x",
        [(2, 4, 2, 24, D)],
        lambda s: [(..., 0, (every, s))],
        "second_x",
    )
    first, second, natural, key_mask, self_mask, line = lax.optimization_barrier(
        (first, second, natural, key_mask, self_mask, line)
    )
    left = lax.ppermute(natural[ROWS - BLOCK :], "fsdp", TO_RIGHT)
    right = lax.ppermute(natural[:BLOCK], "fsdp", TO_LEFT)
    first = first.reshape(2, 2, 4, 24, EXT)
    parts = [first] + relay([first] * 3, "x")
    packed = jnp.concatenate(
        [
            cot_long,
            teacher,
            jnp.broadcast_to(slot_weight[:, None], (ROWS, 128)).astype(bf16),
        ],
        1,
    )
    packed = exchange(pieces(after(packed, natural)), "fsdp")
    *parts, left, right, packed = lax.optimization_barrier((*parts, left, right, packed))
    (first,) = place_parts(
        spot["x"],
        parts,
        [(2, 2, 4, 4, 24, EXT)],
        lambda s: [(..., 0, (every, every, s))],
        "first_x",
    )
    first = first.reshape(2, D, EXT)
    first_other = swap(first)
    wout = lax.all_gather(after(wout, first), "dp", axis=0, tiled=True)
    second = after(second.reshape(16, 24, D), first_other)
    second_parts = [second] + relay([second] * 3, "y")
    side = first[0, :, D:].astype(f32)
    whole_count = side[:, 4] * 16.0 + side[:, 5]
    count = jnp.sum(jnp.where(jnp.arange(D) % 6 == 0, whole_count, 0.0))
    norms = jnp.pad(side[:, :4].T, ((0, 4), (0, 0)))

    packed = exchange(packed[inverse], "fsdp")
    rows, acts, proj = project(place, left, natural, right, globs, norms, first, first_other)
    long_out, long_lse, part_out, part_lse = attend(place, table, line, key_mask, self_mask, proj)

    sent = jnp.concatenate(
        [part_out, split3(part_lse.reshape(HEADS, 128)), jnp.zeros((12, 128), bf16)], 0
    )
    packed = after(packed, long_out)
    got = exchange(jnp.broadcast_to(after(sent, packed)[None], (4, 816, 128)), "fsdp", QUADS)
    *second_parts, _ = lax.optimization_barrier((*second_parts, long_out))
    (second,) = place_parts(
        spot["y"],
        second_parts,
        [(2, 16, 2, 24, D)],
        lambda s: [(..., 0, (s & 1, every, s >> 1))],
        "second_y",
    )
    second = second.reshape(2, D, D)
    second_other = swap(second)

    packed = unpieces(packed)
    lses = join3(got[:, D:])
    high = jnp.max(lses, 0)
    glob_lse = high + jnp.log(jnp.sum(jnp.exp(lses - high), 0))
    shares = jnp.pad(jnp.exp(lses - glob_lse), ((0, 0), (0, 4), (0, 0)))
    glob_lse = glob_lse.reshape(6, 1, 256)

    (
        result,
        loss_sum,
        glob_out,
        grad_middle,
        grad_mixed,
        wattn_grad,
        win_send,
        win_keep,
        wout_send,
        wout_keep,
        norm_two,
    ) = feed(
        place,
        (2.0 / count)[None],
        rows,
        long_out,
        got,
        shares,
        packed,
        globs,
        norms,
        wout,
        first,
        first_other,
        second,
        second_other,
    )
    dq, dk, dv, rel = attend_back(
        place, table, line, key_mask, self_mask, proj, grad_mixed, long_lse, glob_out, glob_lse
    )
    (two,) = add_pairs([(win_keep, swap(win_send))], "add_cores")
    three = fold_parts(
        spot["z"],
        [wout_keep.reshape(64, 24, D), swap(wout_send).reshape(64, 24, D)],
        lambda s: [((g // 4 * 2 + (s >> 1)) * 4 + g % 4) * 4 + (s & 1) * 2 for g in range(8)],
        2,
        "three_z",
    )
    dq, two, *three = lax.optimization_barrier((dq, two, *three))
    two = exchange(two.reshape(64, 24, D), BOTH, SAME_CORE)
    one_send, one_keep, grad_nat, back_left, back_right, back_glob = project_back(
        place,
        rows,
        acts,
        dq,
        dk,
        dv,
        norms,
        grad_middle,
        wattn_grad,
        rel,
        norm_two,
        loss_sum,
        first,
        first_other,
    )
    one = scatter_axis(
        spot["x"],
        [one_keep, swap(one_send)],
        "x",
        lambda s: [(g * 4 + s) * 4 for g in range(4)],
        4,
        "one_x",
    )
    *three, _ = lax.optimization_barrier((*three, one[0]))
    three = [three[0]] + relay(three[1:], "z")
    three = scatter_axis(spot["x"], three, "x", lambda s: [s * 2, (4 + s) * 2], 2, "three_x")
    three = scatter_axis(spot["y"], three, "y", lambda s: [(s & 1) * 2 + (s >> 1)], 1, "three_y")
    out_grad = total_of(three)[0]
    from_left = lax.ppermute(back_right, "fsdp", TO_RIGHT)
    from_right = lax.ppermute(back_left, "fsdp", TO_LEFT)
    both = pack_rows(result, grad_nat, from_left, from_right)
    both = exchange(after(both, two), "fsdp")
    out_long, grad_long = unpack_rows(exchange(both[order], "fsdp"))
    two = jnp.sum(two.astype(f32), 0)
    out_glob = lax.dynamic_slice_in_dim(result, ROWS + quarter * 32, 32, 0)
    one = scatter_axis(
        spot["z"], one, "z", lambda s: [s * 2, (4 + s) * 2], 2, "one_z"
    )
    one = scatter_axis(spot["y"], one, "y", lambda s: [(s & 1) * 2 + (s >> 1)], 1, "one_y")
    small = [part[1, :8].astype(f32) + part[1, 8:16].astype(f32) for part in one]
    small = (small[0] + small[1]) + (small[2] + small[3])
    one = [part[0] for part in one]
    closing = jnp.concatenate(
        [
            back_glob.reshape(4, 32, D),
            total_of(one).reshape(4, 6, D),
            two.reshape(4, 6, D),
            jnp.zeros((4, 4, D), f32),
        ],
        1,
    )
    closing = exchange(after(closing, out_long), "fsdp", QUADS)
    grad_glob = lax.dynamic_slice_in_dim(grad_middle, ROWS + quarter * 32, 32, 0) + jnp.sum(
        closing[:, :32], 0
    )
    one, two = closing[:, 32:38], closing[:, 38:44]
    qkv_grad = one[:3].transpose(1, 0, 2).reshape(6, 3 * D)
    attn_grad = one[3]
    in_grad = two.transpose(1, 0, 2).reshape(6, 4 * D)
    bands = small[4:].reshape(HEADS, 256)[:, 44 : 44 + LABELS]
    label_grad = jnp.dot(picker.T, bands.T, precision=HIGHEST)
    rel_total = jnp.concatenate([label_grad, small[4:5, :HEADS], small[4:5, HEADS : 2 * HEADS]], 0)
    loss_total = small[4, 24]
    mine_norm = lax.dynamic_slice_in_dim(small[:4], device * 6, 6, 1).T
    return (
        out_long,
        out_glob,
        loss_total / count,
        grad_long,
        grad_glob,
        qkv_grad,
        attn_grad,
        in_grad,
        out_grad,
        mine_norm[:, 0::2],
        mine_norm[:, 1::2],
        rel_total,
    )


def solution(mesh):
    rows = P(BOTH, None)
    in_specs = (rows,) * 11 + (P(), P("dp"), P("dp", None), P("dp"), P(), P(BOTH))
    out_specs = (rows, rows, P(), rows, rows, rows, rows, rows, rows, rows, rows, P())
    return jax.shard_map(shards, mesh=mesh, in_specs=in_specs, out_specs=out_specs, check_vma=False)
```

```python
import jax
import jax.numpy as jnp
from jax import lax
from jax.experimental import pallas as pl
from jax.experimental.pallas import tpu as pltpu
from jax.sharding import PartitionSpec as P

D = 768
HEADS = 12
HEAD = 64
RADIUS = 84
LABELS = 169
BLOCK = 128
SEQ_BLOCKS = 16
GLOBAL_EVERY = 16
GSEQ = 128
ROWS = 512
EXT = 896
EPS = 1e-05
MASKED = -1e30
HIGHEST = lax.Precision.HIGHEST
BOTH = ("dp", "fsdp")
f32 = jnp.float32
bf16 = jnp.bfloat16

QUADS = [[4 * i + j for j in range(4)] for i in range(4)]
SAME_CORE = [[4 * g + 2 * p + c for p in range(2) for g in range(32)] for c in range(2)]
SWAP = [(i, i ^ 1) for i in range(16)]
TO_RIGHT = [(i, i + 1) for i in range(16) if i % 4 < 3]
TO_LEFT = [(i, i - 1) for i in range(16) if i % 4 > 0]


def flip(device, axis, step):
    if axis == "x":
        return device ^ (step << 4)
    if axis == "y":
        return device ^ (step << 1)
    return device ^ ((step >> 1) << 6) ^ ((step & 1) << 3)


PARTNERS = {
    axis: [[(i, flip(i, axis, step)) for i in range(128)] for step in (1, 2, 3)] for axis in "xyz"
}


def exchange(value, axis, groups=None):
    return lax.all_to_all(value, axis, 0, 0, axis_index_groups=groups, tiled=True)


def swap(value):
    return lax.ppermute(value, "fsdp", SWAP)


def relay(values, axis):
    return [lax.ppermute(value, BOTH, pairs) for value, pairs in zip(values, PARTNERS[axis])]


def after(value, *others):
    return lax.optimization_barrier((value,) + others)[0]


ANY = pl.BlockSpec(memory_space=pl.ANY)
SCALARS = pl.BlockSpec(memory_space=pltpu.SMEM)


def cost(microseconds):
    return pl.CostEstimate(
        flops=int(microseconds * 1.1e9),
        bytes_accessed=int(microseconds * 3.6e6),
        transcendentals=0,
    )


def place_parts(spot, parts, shapes, moves, name):
    def kernel(spot_ref, *refs):
        ins, outs = refs[:4], refs[4:]
        for k in range(4):
            for source, which, target in moves(spot_ref[0] ^ k):
                outs[which][target] = ins[k][source]

    vm = pl.BlockSpec(memory_space=pltpu.VMEM)
    return pl.pallas_call(
        kernel,
        in_specs=[SCALARS] + [vm] * 4,
        out_specs=[vm] * len(shapes),
        out_shape=[jax.ShapeDtypeStruct(shape, bf16) for shape in shapes],
        compiler_params=params(32),
        cost_estimate=cost(2),
        name=name,
    )(spot, *parts)


def gather_axis(spot, value, axis, shapes, moves, name):
    return place_parts(spot, [value] + relay([value] * 3, axis), shapes, moves, name)


def encode(value):
    high = value.astype(bf16)
    return high, (value - high.astype(f32)).astype(bf16)


def fold_parts(spot, parts, starts, length, name):
    count = parts[0].shape[0] // 4 * 4
    extra = parts[0].shape[0] - count
    size = count // 4

    def kernel(spot_ref, *refs):
        ins, outs = refs[: len(parts)], refs[len(parts) :]
        for k in range(4):
            for i, start in enumerate(starts(spot_ref[0] ^ k)):
                total = ins[0][pl.ds(start, length)].astype(f32)
                for other in ins[1:]:
                    total = total + other[pl.ds(start, length)].astype(f32)
                outs[k][i * length : (i + 1) * length] = total.astype(bf16)
        if extra:
            small = [ref[count, :8].astype(f32) + ref[count, 8:16].astype(f32) for ref in ins]
            small = [small[i] + small[i + 1] for i in range(0, len(ins), 2)]
            high, low = encode(small[0] if len(small) == 1 else small[0] + small[1])
            for out in outs:
                out[size, :8] = high
                out[size, 8:16] = low
                out[size, 16:] = jnp.zeros((8, D), bf16)

    vm = pl.BlockSpec(memory_space=pltpu.VMEM)
    return pl.pallas_call(
        kernel,
        in_specs=[SCALARS] + [vm] * len(parts),
        out_specs=[vm] * 4,
        out_shape=[jax.ShapeDtypeStruct((size + extra, 24, D), bf16)] * 4,
        compiler_params=params(32),
        cost_estimate=cost(2),
        name=name,
    )(spot, *parts)


def add_pairs(pairs, name):
    def kernel(*refs):
        for i in range(len(pairs)):
            ours, theirs = refs[2 * i][...].astype(f32), refs[2 * i + 1][...].astype(f32)
            refs[2 * len(pairs) + i][...] = (ours + theirs).astype(bf16)

    block = pl.BlockSpec((384, D), lambda i: (i, 0))
    return pl.pallas_call(
        kernel,
        grid=(4,),
        in_specs=[block] * (2 * len(pairs)),
        out_specs=[block] * len(pairs),
        out_shape=[jax.ShapeDtypeStruct((2 * D, D), bf16)] * len(pairs),
        compiler_params=params(32),
        cost_estimate=cost(4),
        name=name,
    )(*[part.reshape(2 * D, D) for pair in pairs for part in pair])


def scatter_axis(spot, parts, axis, starts, length, name):
    cut = fold_parts(spot, parts, starts, length, name)
    return [cut[0]] + relay(cut[1:], axis)


def pack_rows(result, nat, from_left, from_right):
    def kernel(result_ref, nat_ref, left_ref, right_ref, out):
        for block in range(4):
            rows = slice(128 * block, 128 * block + 128)
            grad = nat_ref[rows]
            if block == 0:
                grad = grad + left_ref[...].astype(f32)
            if block == 3:
                grad = grad + right_ref[...].astype(f32)
            for piece in range(16):
                low = 8 * piece
                out[4 * piece + block, :, D:] = grad[low : low + 8].astype(bf16)
                out[4 * piece + block, :, :D] = result_ref[
                    128 * block + low : 128 * block + low + 8
                ]

    vm = pl.BlockSpec(memory_space=pltpu.VMEM)
    return pl.pallas_call(
        kernel,
        in_specs=[vm] * 4,
        out_specs=vm,
        out_shape=jax.ShapeDtypeStruct((64, 8, 2 * D), bf16),
        compiler_params=params(32),
        cost_estimate=cost(3),
        name="pack_rows",
    )(result, nat, from_left, from_right)


def unpack_rows(value):
    def kernel(value_ref, long_ref, grad_ref):
        for block in range(4):
            for piece in range(16):
                low = 128 * block + 8 * piece
                long_ref[low : low + 8] = value_ref[4 * piece + block, :, :D]
                grad_ref[low : low + 8] = value_ref[4 * piece + block, :, D:].astype(f32)

    vm = pl.BlockSpec(memory_space=pltpu.VMEM)
    return pl.pallas_call(
        kernel,
        in_specs=[vm],
        out_specs=[vm] * 2,
        out_shape=[jax.ShapeDtypeStruct((ROWS, D), bf16), jax.ShapeDtypeStruct((ROWS, D), f32)],
        compiler_params=params(32),
        cost_estimate=cost(3),
        name="unpack_rows",
    )(value)


def total_of(parts):
    total = parts[0].astype(f32)
    for part in parts[1:]:
        total = total + part.astype(f32)
    return total


def pieces(rows):
    width = rows.shape[-1]
    return rows.reshape(4, 16, 8, width).transpose(1, 0, 2, 3).reshape(64, 8, width)


def unpieces(value):
    width = value.shape[-1]
    return value.reshape(16, 4, 8, width).transpose(1, 0, 2, 3).reshape(ROWS, width)


def reorder(rows, index):
    spread = exchange(pieces(rows), "fsdp")
    return unpieces(exchange(spread[index], "fsdp"))


def split3(value):
    high = value.astype(bf16)
    rest = value - high.astype(f32)
    mid = rest.astype(bf16)
    low = (rest - mid.astype(f32)).astype(bf16)
    return jnp.concatenate([high, mid, low], 0)


def join3(value):
    value = value.astype(f32)
    return value[:, :HEADS] + value[:, HEADS : 2 * HEADS] + value[:, 2 * HEADS : 3 * HEADS]


def dot_nn(a, b):
    return lax.dot_general(a, b, (((1,), (0,)), ((), ())), preferred_element_type=f32)


def dot_nt(a, b):
    return lax.dot_general(a, b, (((1,), (1,)), ((), ())), preferred_element_type=f32)


def dot_tn(a, b):
    return lax.dot_general(a, b, (((0,), (0,)), ((), ())), preferred_element_type=f32)


def whole(shape):
    zeros = (0,) * len(shape)
    return pl.BlockSpec(shape, lambda *_: zeros, pipeline_mode=pl.Buffered(1))


def params(megabytes):
    return pltpu.CompilerParams(vmem_limit_bytes=megabytes << 20)


def normalise(values):
    centre = jnp.mean(values, -1, keepdims=True)
    centred = values - centre
    spread = jnp.mean(centred * centred, -1, keepdims=True)
    factor = lax.rsqrt(spread + EPS)
    return centred * factor, factor


def load_quarters(core, mine, other, target, sems, count):
    copies = []
    for p in range(2):
        copies.append(pltpu.make_async_copy(mine.at[p, :, pl.ds(0, D)], target.at[2 * p + core], sems.at[2 * p]))
        copies.append(
            pltpu.make_async_copy(
                other.at[p, :, pl.ds(0, D)], target.at[2 * p + 1 - core], sems.at[2 * p + 1]
            )
        )
    for copy in copies:
        copy.start()
    return copies


def quarter_copy(step, core, mine, target, sems):
    slot = 2 * (step // 2) + jnp.where(step % 2 == core, 0, 1)
    return pltpu.make_async_copy(mine.at[0, :, pl.ds(0, D)], target.at[step], sems.at[slot])


def project_kernel(
    place, left, nat, right, globs, norms, mine, other, rows_out, acts_out, proj_out, w, sems
):
    step = pl.program_id(0)
    core = place[1]

    @pl.when(step == 0)
    def _():
        load_quarters(core, mine, other, w, sems, 4)
        rows_out[:128] = left[...]
        rows_out[128:640] = nat[...]
        rows_out[640:768] = right[...]
        rows_out[768:] = globs[:, :D]
        normal, _ = normalise(rows_out[...].astype(f32))
        acts_out[...] = (normal * norms[0:1] + norms[2:3]).astype(bf16)

    quarter_copy(step, core, mine, w, sems).wait()
    proj_out[...] = dot_nn(acts_out[...], w[step]).astype(bf16)

    @pl.when(step == 2)
    def _():
        quarter_copy(step + 1, core, mine, w, sems).wait()


def project(place, left, nat, right, globs, norms, mine, other):
    return pl.pallas_call(
        project_kernel,
        grid=(3,),
        in_specs=[
            SCALARS,
            whole((128, D)),
            whole((ROWS, D)),
            whole((128, D)),
            whole((128, 2 * D)),
            whole((8, D)),
            ANY,
            ANY,
        ],
        out_specs=[
            whole((EXT, D)),
            whole((EXT, D)),
            pl.BlockSpec((EXT, D), lambda i: (0, i)),
        ],
        scratch_shapes=[pltpu.VMEM((4, D, D), bf16), pltpu.SemaphoreType.DMA((4,))],
        out_shape=(
            jax.ShapeDtypeStruct((EXT, D), bf16),
            jax.ShapeDtypeStruct((EXT, D), bf16),
            jax.ShapeDtypeStruct((EXT, 3 * D), bf16),
        ),
        compiler_params=params(50),
        cost_estimate=cost(9),
        name="project",
    )(place, left, nat, right, globs, norms, mine, other)


def stack_heads(rows):
    first = lax.broadcasted_iota(jnp.int32, rows.shape, 1) < HEAD
    zero = jnp.zeros_like(rows)
    return jnp.concatenate([jnp.where(first, rows, zero), jnp.where(first, zero, rows)], 0)


def merge_heads(value):
    first = lax.broadcasted_iota(jnp.int32, (128, 128), 0) < HEAD
    return jnp.where(first, value[:, :128], value[:, 128:]).T


def band_tile(line):
    tiles = []
    for head in range(2):
        spread = jnp.broadcast_to(line[head : head + 1], (BLOCK, 512))
        rolled = pltpu.roll(spread, 0, 1, stride=1, stride_axis=0)
        tiles.append(
            jnp.concatenate([rolled[:, 128 * i : 128 * i + 128].T for i in range(3)], 0)
        )
    return jnp.concatenate(tiles, 1)


def pair_row(first, second):
    lane = lax.broadcasted_iota(jnp.int32, (1, 256), 1)
    return jnp.where(lane < 128, first, second)


def long_owned(run):
    key = lax.broadcasted_iota(jnp.int32, (128, 256), 0)
    lane = lax.broadcasted_iota(jnp.int32, (128, 256), 1)
    return key == run + lax.shift_right_logical(lane & 127, 4)


def cross_owned(run):
    key = lax.broadcasted_iota(jnp.int32, (ROWS, 256), 0)
    lane = lax.broadcasted_iota(jnp.int32, (ROWS, 256), 1)
    return run + lax.shift_right_logical(key, 4) == (lane & 127)


def attend_kernel(
    place, table, line, key_mask, self_mask, q, k, v, out, lse, glob_out, glob_lse, band
):
    pair = pl.program_id(0)
    run = place[0] * 32
    own = pair_row(table[0, 2 * pair], table[0, 2 * pair + 1])
    other = pair_row(table[1, 2 * pair], table[1, 2 * pair + 1])
    band[...] = band_tile(line[0])
    values = v[...].T
    for j in range(4):
        low = 128 * j
        query = stack_heads(q[128 + low : 256 + low, :] * 0.125)
        near = dot_nt(k[low : low + 384, :], query) + (band[...] + key_mask[low : low + 384, :])
        far = dot_nt(k[768:, :], query) + (
            jnp.where(long_owned(run + 8 * j), own, other) + key_mask[768:, :]
        )
        top = jnp.maximum(jnp.max(near, 0, keepdims=True), jnp.max(far, 0, keepdims=True))
        near = jnp.exp(near - top)
        far = jnp.exp(far - top)
        total = jnp.sum(near, 0, keepdims=True) + jnp.sum(far, 0, keepdims=True)
        share = 1.0 / total
        got = dot_nn(values[:, low : low + 384], (near * share).astype(bf16)) + dot_nn(
            values[:, 768:], (far * share).astype(bf16)
        )
        out[low : low + 128, :] = merge_heads(got).astype(bf16)
        lse[0, j : j + 1, :] = top + jnp.log(total)
    query = stack_heads(q[768:, :] * 0.125)
    near = dot_nt(k[128:640, :], query) + (
        jnp.where(cross_owned(run), own, other) + key_mask[128:640, :]
    )
    far = dot_nt(k[768:, :], query) + self_mask[...]
    top = jnp.maximum(jnp.max(near, 0, keepdims=True), jnp.max(far, 0, keepdims=True))
    near = jnp.exp(near - top)
    far = jnp.exp(far - top)
    total = jnp.sum(near, 0, keepdims=True) + jnp.sum(far, 0, keepdims=True)
    share = 1.0 / total
    got = dot_nn(values[:, 128:640], (near * share).astype(bf16)) + dot_nn(
        values[:, 768:], (far * share).astype(bf16)
    )
    first = lax.broadcasted_iota(jnp.int32, (128, 128), 0) < HEAD
    glob_out[...] = jnp.where(first, got[:, :128], got[:, 128:]).astype(bf16)
    glob_lse[0] = top + jnp.log(total)


def column(width, offset):
    return pl.BlockSpec((width, 128), lambda h: (0, h + offset))


def attend(place, table, line, key_mask, self_mask, proj):
    return pl.pallas_call(
        attend_kernel,
        grid=(6,),
        in_specs=[
            SCALARS,
            SCALARS,
            pl.BlockSpec((1, 2, 512), lambda h: (h, 0, 0)),
            whole((EXT, 256)),
            whole((128, 256)),
            column(EXT, 0),
            column(EXT, 6),
            column(EXT, 12),
        ],
        out_specs=[
            column(ROWS, 0),
            pl.BlockSpec((1, 4, 256), lambda h: (h, 0, 0)),
            pl.BlockSpec((128, 128), lambda h: (h, 0)),
            pl.BlockSpec((1, 1, 256), lambda h: (h, 0, 0)),
        ],
        out_shape=(
            jax.ShapeDtypeStruct((ROWS, D), bf16),
            jax.ShapeDtypeStruct((6, 4, 256), f32),
            jax.ShapeDtypeStruct((D, 128), bf16),
            jax.ShapeDtypeStruct((6, 1, 256), f32),
        ),
        scratch_shapes=[pltpu.VMEM((384, 256), f32)],
        compiler_params=params(40),
        cost_estimate=cost(15),
        name="attend",
    )(place, table, line, key_mask, self_mask, proj, proj, proj)


def fold_band(tile):
    rows = jnp.concatenate([tile[128 * i : 128 * i + 128].T for i in range(3)], 1)
    rows = jnp.concatenate([rows, jnp.zeros((BLOCK, 128), f32)], 1)
    total = rows[:8]
    for a in range(1, 16):
        total = total + pltpu.roll(rows[8 * a : 8 * a + 8], 512 - 8 * a, 1)
    row = lax.broadcasted_iota(jnp.int32, (8, 512), 0)
    for bit in (1, 2, 4):
        total = jnp.where((row & bit) != 0, pltpu.roll(total, 512 - bit, 1), total)
    return jnp.sum(total, 0, keepdims=True)


def attend_back_kernel(
    place,
    table,
    line,
    key_mask,
    self_mask,
    q,
    k,
    v,
    grad,
    lse,
    glob_out,
    glob_lse,
    grads,
    rel,
    band,
    band_sum,
    key_sum,
    value_sum,
):
    pair = pl.program_id(0)
    run = place[0] * 32
    own = pair_row(table[0, 2 * pair], table[0, 2 * pair + 1])
    other = pair_row(table[1, 2 * pair], table[1, 2 * pair + 1])
    band[...] = band_tile(line[0])
    keys = k[...].T
    band_sum[...] = jnp.zeros_like(band_sum)
    key_sum[...] = jnp.zeros_like(key_sum)
    value_sum[...] = jnp.zeros_like(value_sum)
    owned_sum = jnp.zeros((1, 256), f32)
    other_sum = jnp.zeros((1, 256), f32)
    grads[0, :128] = jnp.zeros((128, 128), bf16)
    grads[0, 640:768] = jnp.zeros((128, 128), bf16)
    for j in range(4):
        low = 128 * j
        query = stack_heads(q[128 + low : 256 + low, :] * 0.125)
        back = stack_heads(grad[low : low + 128, :])
        near = dot_nt(k[low : low + 384, :], query) + (band[...] + key_mask[low : low + 384, :])
        owned = long_owned(run + 8 * j)
        far = dot_nt(k[768:, :], query) + (jnp.where(owned, own, other) + key_mask[768:, :])
        top = lse[0, j : j + 1, :]
        near = jnp.exp(near - top)
        far = jnp.exp(far - top)
        near_d = dot_nt(v[low : low + 384, :], back)
        far_d = dot_nt(v[768:, :], back)
        delta = jnp.sum(near * near_d, 0, keepdims=True) + jnp.sum(far * far_d, 0, keepdims=True)
        near_d = (near * (near_d - delta)).astype(bf16)
        far_d = (far * (far_d - delta)).astype(bf16)
        key_sum[low : low + 384, :] += dot_nn(near_d, query)
        value_sum[low : low + 384, :] += dot_nn(near.astype(bf16), back)
        key_sum[768:, :] += dot_nn(far_d, query)
        value_sum[768:, :] += dot_nn(far.astype(bf16), back)
        got = dot_nn(keys[:, low : low + 384], near_d) + dot_nn(keys[:, 768:], far_d)
        grads[0, 128 + low : 256 + low, :] = (merge_heads(got) * 0.125).astype(bf16)
        band_sum[...] += near_d.astype(f32)
        far_d = far_d.astype(f32)
        owned_sum += jnp.sum(jnp.where(owned, far_d, 0.0), 0, keepdims=True)
        other_sum += jnp.sum(jnp.where(owned, 0.0, far_d), 0, keepdims=True)
    query = stack_heads(q[768:, :] * 0.125)
    back = stack_heads(grad[ROWS:, :])
    owned = cross_owned(run)
    near = dot_nt(k[128:640, :], query) + (jnp.where(owned, own, other) + key_mask[128:640, :])
    far = dot_nt(k[768:, :], query) + self_mask[...]
    top = glob_lse[0]
    near = jnp.exp(near - top)
    far = jnp.exp(far - top)
    near_d = dot_nt(v[128:640, :], back)
    far_d = dot_nt(v[768:, :], back)
    product = grad[ROWS:, :].astype(f32).T * glob_out[...].astype(f32)
    delta = jnp.concatenate(
        [
            jnp.sum(product[:HEAD], 0, keepdims=True),
            jnp.sum(product[HEAD:], 0, keepdims=True),
        ],
        1,
    )
    near_d = (near * (near_d - delta)).astype(bf16)
    far_d = (far * (far_d - delta)).astype(bf16)
    key_sum[128:640, :] += dot_nn(near_d, query)
    value_sum[128:640, :] += dot_nn(near.astype(bf16), back)
    key_sum[768:, :] += dot_nn(far_d, query)
    value_sum[768:, :] += dot_nn(far.astype(bf16), back)
    got = dot_nn(keys[:, 128:640], near_d) + dot_nn(keys[:, 768:], far_d)
    grads[0, 768:, :] = (merge_heads(got) * 0.125).astype(bf16)
    near_d = near_d.astype(f32)
    owned_sum += jnp.sum(jnp.where(owned, near_d, 0.0), 0, keepdims=True)
    other_sum += jnp.sum(jnp.where(owned, 0.0, near_d), 0, keepdims=True)
    grads[1] = key_sum[...].astype(bf16)
    grads[2] = value_sum[...].astype(bf16)
    rel[0] = jnp.zeros((8, 512), f32)
    for head in range(2):
        lanes = slice(128 * head, 128 * head + 128)
        rel[0, head : head + 1, :] = fold_band(band_sum[:, lanes])
        rel[0, 2 + head : 3 + head, :128] = owned_sum[:, lanes]
        rel[0, 4 + head : 5 + head, :128] = other_sum[:, lanes]


def attend_back(place, table, line, key_mask, self_mask, proj, grad, lse, glob_out, glob_lse):
    return pl.pallas_call(
        attend_back_kernel,
        grid=(6,),
        in_specs=[
            SCALARS,
            SCALARS,
            pl.BlockSpec((1, 2, 512), lambda h: (h, 0, 0)),
            whole((EXT, 256)),
            whole((128, 256)),
            column(EXT, 0),
            column(EXT, 6),
            column(EXT, 12),
            column(640, 0),
            pl.BlockSpec((1, 4, 256), lambda h: (h, 0, 0)),
            pl.BlockSpec((128, 128), lambda h: (h, 0)),
            pl.BlockSpec((1, 1, 256), lambda h: (h, 0, 0)),
        ],
        out_specs=[
            pl.BlockSpec((3, EXT, 128), lambda h: (0, 0, h)),
            pl.BlockSpec((1, 8, 512), lambda h: (h, 0, 0)),
        ],
        out_shape=(
            jax.ShapeDtypeStruct((3, EXT, D), bf16),
            jax.ShapeDtypeStruct((6, 8, 512), f32),
        ),
        scratch_shapes=[
            pltpu.VMEM((384, 256), f32),
            pltpu.VMEM((384, 256), f32),
            pltpu.VMEM((EXT, 128), f32),
            pltpu.VMEM((EXT, 128), f32),
        ],
        compiler_params=params(48),
        cost_estimate=cost(21),
        name="attend_back",
    )(place, table, line, key_mask, self_mask, proj, proj, proj, grad, lse, glob_out, glob_lse)


def feed_kernel(
    place,
    coef,
    rows,
    long_out,
    parts,
    shares,
    packed,
    globs,
    norms,
    wout,
    first_mine,
    first_other,
    in_mine,
    in_other,
    result_out,
    loss_out,
    glob_out,
    middle_grad_out,
    mixed_grad_out,
    wattn_grad,
    win_send,
    win_keep,
    wout_grad,
    norm_grads,
    mixed,
    acts,
    normal,
    total,
    hidden,
    slope,
    grad_z,
    grad_acts,
    factor,
    wa,
    win,
    sem,
    sems,
):
    step = pl.program_id(0)
    core = place[1]


    def attn_copy(source):
        return pltpu.make_async_copy(source.at[1, :, pl.ds(0, D)], wa, sem)

    quarter = place[0]
    forward = step < 4
    late = jnp.maximum(step - 4, 0)
    chunk = jnp.where(
        forward, step, jnp.where(late < 2, 2 * late + 1 - core, 2 * (late - 2) + core)
    )

    def owned():
        row = lax.broadcasted_iota(jnp.int32, (640, 1), 0)
        first = ROWS + quarter * 32
        return (row < ROWS) | ((row >= first) & (row < first + 32))

    @pl.when(step == 0)
    def _():
        @pl.when(core == 1)
        def _():
            attn_copy(first_mine).start()

        @pl.when(core == 0)
        def _():
            attn_copy(first_other).start()

        load_quarters(core, in_mine, in_other, win, sems, 4)
        mixed[:ROWS] = long_out[...]
        for pair in range(6):
            sums = jnp.zeros((128, 128), f32)
            top = lax.broadcasted_iota(jnp.int32, (128, 128), 0) < HEAD
            for source in range(4):
                share = jnp.where(
                    top,
                    shares[source, 2 * pair : 2 * pair + 1, :],
                    shares[source, 2 * pair + 1 : 2 * pair + 2, :],
                )
                sums = sums + parts[source, 128 * pair : 128 * pair + 128, :].astype(f32) * share
            glob_out[128 * pair : 128 * pair + 128, :] = sums.astype(bf16)
            mixed[ROWS:, 128 * pair : 128 * pair + 128] = sums.T.astype(bf16)
        attn_copy(first_mine).wait()
        middle = dot_nn(mixed[...], wa[...])
        middle = middle + jnp.concatenate(
            [rows[128:640].astype(f32), rows[768:].astype(f32)], 0
        )
        total[...] = middle
        base, scale = normalise(middle)
        normal[...] = base
        factor[...] = scale
        acts[...] = (base * norms[1:2] + norms[3:4]).astype(bf16)
        for p in range(4):
            pltpu.make_async_copy(in_mine.at[0, :, pl.ds(0, D)], win.at[0], sems.at[p]).wait()

    @pl.when(forward)
    def _():
        inner = dot_nn(acts[...], win[chunk])
        half = 0.5 + 0.5 * lax.erf(inner * 0.7071067811865476)
        slope[chunk] = half + inner * (jnp.exp(-0.5 * inner * inner) * 0.3989422804014327)
        bits = (inner * half).astype(bf16)
        hidden[chunk] = bits
        total[...] += dot_nn(bits, wout[...])

    @pl.when(step == 3)
    def _():
        result = total[...]
        result_out[...] = result.astype(bf16)
        weight = packed[:, 2 * D : 2 * D + 1].astype(f32)
        error = result[:ROWS] - packed[:, D : 2 * D].astype(f32)
        masked = weight * error
        loss_out[...] = jnp.broadcast_to(
            jnp.sum(jnp.sum(masked * error, 0, keepdims=True), 1, keepdims=True), (8, 128)
        )
        grad = jnp.concatenate(
            [packed[:, :D].astype(f32) + coef[0] * masked, globs[:, D:].astype(f32)], 0
        )
        total[...] = grad
        grad_z[...] = grad.astype(bf16)
        grad_acts[...] = jnp.zeros_like(grad_acts)

    @pl.when(step >= 4)
    def _():
        keep_rows = owned()
        grad_inner = (dot_nt(grad_z[...], wout[...]) * slope[chunk]).astype(bf16)
        zeros = jnp.zeros_like(grad_inner)
        grad_acts[...] += dot_nt(grad_inner, win[chunk])
        part = dot_tn(acts[...], jnp.where(keep_rows, grad_inner, zeros)).astype(bf16)

        @pl.when(late < 2)
        def _():
            win_send[0] = part

        @pl.when(late >= 2)
        def _():
            win_keep[0] = part

        part = dot_tn(hidden[chunk], jnp.where(keep_rows, grad_z[...], zeros))
        part = part.reshape(2, 16, 24, D).astype(bf16)
        for i in range(2):
            wout_grad[:, i] = part[i]

    @pl.when(step == 7)
    def _():
        keep_rows = owned()
        grad = grad_acts[...]
        base = normal[...]
        mine = jnp.where(keep_rows, grad, 0.0)
        norm_grads[0:1, :] = jnp.sum(mine * base, 0, keepdims=True)
        norm_grads[1:2, :] = jnp.sum(mine, 0, keepdims=True)
        scaled = grad * norms[1:2]
        first = jnp.mean(scaled, -1, keepdims=True)
        second = jnp.mean(scaled * base, -1, keepdims=True)
        middle = total[...] + factor[...] * (scaled - first - base * second)
        middle_grad_out[...] = middle
        branch = middle.astype(bf16)
        mixed_grad_out[...] = dot_nt(branch, wa[...]).astype(bf16)
        wattn_grad[...] = dot_tn(
            mixed[...], jnp.where(keep_rows, branch, jnp.zeros_like(branch))
        ).astype(bf16)


def feed(place, coef, rows, long_out, parts, shares, packed, globs, norms, *weights):
    def chunk(t, place):
        late = jnp.maximum(t - 4, 0)
        core = place[1]
        back = jnp.where(late < 2, 2 * late + 1 - core, 2 * (late - 2) + core)
        return jnp.where(t < 4, t, back)

    def back_chunk(t, place):
        return chunk(jnp.maximum(t, 4), place)

    def fixed(shape):
        zeros = (0,) * len(shape)
        return pl.BlockSpec(shape, lambda t, place: zeros, pipeline_mode=pl.Buffered(1))

    return pl.pallas_call(
        feed_kernel,
        grid_spec=pltpu.PrefetchScalarGridSpec(
            num_scalar_prefetch=1,
            grid=(8,),
            in_specs=[
                SCALARS,
                fixed((EXT, D)),
                fixed((ROWS, D)),
                fixed((4, 816, 128)),
                fixed((4, 16, 128)),
                fixed((ROWS, 2 * D + 128)),
                fixed((128, 2 * D)),
                fixed((8, D)),
                pl.BlockSpec((D, D), lambda t, place: (chunk(t, place), 0)),
                ANY,
                ANY,
                ANY,
                ANY,
            ],
            out_specs=[
                fixed((640, D)),
                fixed((8, 128)),
                fixed((D, 128)),
                fixed((640, D)),
                fixed((640, D)),
                fixed((D, D)),
                pl.BlockSpec((1, D, D), lambda t, place: (jnp.clip(t - 4, 0, 1), 0, 0)),
                pl.BlockSpec((1, D, D), lambda t, place: (jnp.clip(t - 6, 0, 1), 0, 0)),
                pl.BlockSpec((16, 2, 24, D), lambda t, place: (0, back_chunk(t, place), 0, 0)),
                fixed((8, D)),
            ],
            scratch_shapes=[
                pltpu.VMEM((640, D), bf16),
                pltpu.VMEM((640, D), bf16),
                pltpu.VMEM((640, D), f32),
                pltpu.VMEM((640, D), f32),
                pltpu.VMEM((4, 640, D), bf16),
                pltpu.VMEM((4, 640, D), f32),
                pltpu.VMEM((640, D), bf16),
                pltpu.VMEM((640, D), f32),
                pltpu.VMEM((640, 1), f32),
                pltpu.VMEM((D, D), bf16),
                pltpu.VMEM((4, D, D), bf16),
                pltpu.SemaphoreType.DMA,
                pltpu.SemaphoreType.DMA((4,)),
            ],
        ),
        out_shape=(
            jax.ShapeDtypeStruct((640, D), bf16),
            jax.ShapeDtypeStruct((8, 128), f32),
            jax.ShapeDtypeStruct((D, 128), bf16),
            jax.ShapeDtypeStruct((640, D), f32),
            jax.ShapeDtypeStruct((640, D), bf16),
            jax.ShapeDtypeStruct((D, D), bf16),
            jax.ShapeDtypeStruct((2, D, D), bf16),
            jax.ShapeDtypeStruct((2, D, D), bf16),
            jax.ShapeDtypeStruct((16, 8, 24, D), bf16),
            jax.ShapeDtypeStruct((8, D), f32),
        ),
        compiler_params=params(60),
        cost_estimate=cost(43),
        name="feed",
    )(place, coef, rows, long_out, parts, shares, packed, globs, norms, *weights)


def input_grad_kernel(
    place, rows, grads, norms, middle_grad, rel, norm_two, loss, mine, other,
    nat, left, right, globs, totals, w, sems, grad, small,
):
    step = pl.program_id(0)
    core = place[1]

    @pl.when(step == 0)
    def _():
        load_quarters(core, mine, other, w, sems, 4)
        grad[...] = jnp.zeros_like(grad)
        small[2:4, :] = norm_two[0:2, :]
        for n in range(HEADS):
            low = 256 * (n % 3)
            small[4 + n // 3 : 5 + n // 3, low : low + 256] = rel[n // 2, n % 2 : n % 2 + 1, :256]
        lane = lax.broadcasted_iota(jnp.int32, (1, 128), 1)
        line = jnp.where(lane == 24, loss[0:1, :], small[4:5, :128])
        for n in range(2 * HEADS):
            head, row = n % HEADS, 2 + 2 * (n // HEADS)
            part = rel[head // 2, row + head % 2 : row + head % 2 + 1, :128]
            line = jnp.where(lane == n, jnp.sum(part, 1, keepdims=True), line)
        small[4:5, :128] = line

    quarter_copy(step, core, mine, w, sems).wait()
    grad[...] += dot_nt(grads[0], w[step])

    @pl.when(step == 2)
    def _():
        quarter_copy(step + 1, core, mine, w, sems).wait()
        base, factor = normalise(rows[...].astype(f32))
        total = grad[...]
        small[0:1, :] = jnp.sum(total * base, 0, keepdims=True)
        small[1:2, :] = jnp.sum(total, 0, keepdims=True)
        high, low = encode(small[...])
        totals[0, :8] = high
        totals[0, 8:16] = low
        totals[0, 16:] = jnp.zeros((8, D), bf16)
        scaled = total * norms[0:1]
        first = jnp.mean(scaled, -1, keepdims=True)
        second = jnp.mean(scaled * base, -1, keepdims=True)
        back = factor * (scaled - first - base * second)
        nat[...] = back[128:640] + middle_grad[:ROWS]
        left[...] = back[:128].astype(bf16)
        right[...] = back[640:768].astype(bf16)
        globs[...] = back[768:]


def input_grad(*operands):
    return pl.pallas_call(
        input_grad_kernel,
        grid=(3,),
        in_specs=[
            SCALARS,
            whole((EXT, D)),
            pl.BlockSpec((1, EXT, D), lambda i: (i, 0, 0)),
            whole((8, D)),
            whole((640, D)),
            whole((6, 8, 512)),
            whole((8, D)),
            whole((8, 128)),
            ANY,
            ANY,
        ],
        out_specs=[
            whole((ROWS, D)),
            whole((128, D)),
            whole((128, D)),
            whole((128, D)),
            whole((1, 24, D)),
        ],
        scratch_shapes=[
            pltpu.VMEM((4, D, D), bf16),
            pltpu.SemaphoreType.DMA((4,)),
            pltpu.VMEM((EXT, D), f32),
            pltpu.VMEM((8, D), f32),
        ],
        out_shape=(
            jax.ShapeDtypeStruct((ROWS, D), f32),
            jax.ShapeDtypeStruct((128, D), bf16),
            jax.ShapeDtypeStruct((128, D), bf16),
            jax.ShapeDtypeStruct((128, D), f32),
            jax.ShapeDtypeStruct((1, 24, D), bf16),
        ),
        compiler_params=params(56),
        cost_estimate=cost(60),
        name="input_grad",
    )(*operands)


def weight_grad_kernel(place, acts, grads, wattn_grad, totals, send, keep):
    step = pl.program_id(0)
    ours = step % 2 == place[1]
    part = dot_tn(acts[...], grads[0]).reshape(32, 24, D).astype(bf16)
    chunks = pl.ds(32 * (step // 2), 32)

    @pl.when(ours)
    def _():
        keep[chunks] = part

    @pl.when(jnp.logical_not(ours))
    def _():
        send[chunks] = part

    @pl.when(step == 2)
    def _():
        send[64] = totals[0]
        keep[64] = totals[0]
        rest = wattn_grad[...].astype(f32).reshape(32, 24, D).astype(bf16)

        @pl.when(ours)
        def _():
            send[32:64] = rest

        @pl.when(jnp.logical_not(ours))
        def _():
            keep[32:64] = rest


def weight_grad(*operands):
    return pl.pallas_call(
        weight_grad_kernel,
        grid=(3,),
        in_specs=[
            SCALARS,
            whole((EXT, D)),
            pl.BlockSpec((1, EXT, D), lambda i: (i, 0, 0)),
            whole((D, D)),
            whole((1, 24, D)),
        ],
        out_specs=[whole((65, 24, D))] * 2,
        out_shape=[jax.ShapeDtypeStruct((65, 24, D), bf16)] * 2,
        compiler_params=params(48),
        cost_estimate=cost(0.1),
        name="weight_grad",
    )(*operands)


def shards(
    long_in,
    glob_in,
    cot_long,
    cot_glob,
    teacher,
    w_qkv,
    w_attn,
    w_in,
    w_out,
    norm_gains,
    norm_biases,
    rel_bias,
    lengths,
    block_order,
    global_pos,
    rel_labels,
    loss_mask,
):
    member = lax.axis_index("fsdp")
    core = member % 2
    quarter = member % 4
    seq = member // 4
    order = block_order[0]
    slots = jnp.arange(64)
    inverse = jnp.sum(jnp.where(order[None, :] == slots[:, None], slots[None, :], 0), 1)
    length = jnp.sum(jnp.where(jnp.arange(4) == seq, lengths, 0))
    anchors = lax.dynamic_slice_in_dim(global_pos, seq * GSEQ, GSEQ)

    my_ids = lax.dynamic_slice_in_dim(order, member * 4, 4)
    my_lens = jnp.sum(
        jnp.where(my_ids[:, None] // SEQ_BLOCKS == jnp.arange(4)[None, :], lengths[None, :], 0), 1
    )
    slot_pos = (my_ids % SEQ_BLOCKS)[:, None] * BLOCK + jnp.arange(BLOCK)[None, :]
    slot_weight = ((slot_pos < my_lens[:, None]).reshape(ROWS) & (loss_mask == 1)).astype(jnp.int32)
    my_count = jnp.sum(slot_weight)

    device = lax.axis_index("dp") * 16 + member
    spot = {
        "x": ((device >> 4) & 3)[None],
        "y": ((device >> 1) & 3)[None],
        "z": (((device >> 6) & 1) * 2 + ((device >> 3) & 1))[None],
    }
    counted = jnp.stack([my_count // 16, my_count % 16]).astype(bf16)
    extra = jnp.concatenate([norm_gains, norm_biases, jnp.broadcast_to(counted, (6, 2))], 1)
    extra = jnp.broadcast_to(jnp.pad(extra, ((0, 6), (0, D - 6))), (4, 12, D))
    opening = jnp.concatenate(
        [
            jnp.concatenate([w_qkv, w_attn], 1).reshape(6, 4, D).transpose(1, 0, 2),
            w_in.reshape(6, 4, D).transpose(1, 0, 2),
            extra,
            jnp.broadcast_to(jnp.concatenate([glob_in, cot_glob])[None], (4, 64, D)),
        ],
        1,
    )
    opening = exchange(opening, "fsdp", QUADS)
    spread_long = exchange(pieces(after(long_in, opening)), "fsdp")
    first = jnp.concatenate([opening[:, :6].reshape(24, D), opening[:, 12:18, :128].reshape(24, 128)], 1)
    globs = jnp.concatenate([opening[:, 24:56], opening[:, 56:]], 2).reshape(GSEQ, 2 * D)
    wout = jnp.concatenate([w_out, jnp.zeros((24, D), bf16)], 0)
    wout = lax.all_gather(wout, "fsdp", axis=0, tiled=True)
    wout = wout.reshape(16, 48, D)[:, :24].reshape(384, D)
    natural = unpieces(exchange(spread_long[inverse], "fsdp"))
    every = slice(None)
    start = quarter * ROWS
    place = jnp.stack([quarter, core]).astype(jnp.int32)
    key_pos = start - BLOCK + jnp.arange(768)
    key_ok = (key_pos >= 0) & (key_pos < length)
    glob_ok = anchors < length
    own_glob = jnp.arange(GSEQ) // 32 == quarter
    key_mask = jnp.broadcast_to(
        jnp.where(jnp.concatenate([key_ok, glob_ok]), 0.0, MASKED)[:, None], (EXT, 256)
    )
    self_mask = jnp.broadcast_to(jnp.where(glob_ok & own_glob, 0.0, MASKED)[:, None], (GSEQ, 256))
    picker = (rel_labels[:, None] == jnp.arange(LABELS)[None, :]).astype(f32)
    label_table = jnp.dot(picker, rel_bias[:LABELS], precision=HIGHEST)
    line = jnp.full((HEADS, 512), MASKED, f32)
    line = lax.dynamic_update_slice(line, label_table.T, (0, 44)).reshape(6, 2, 512)
    table = rel_bias[LABELS:]
    second = opening[:, 6:12].reshape(24, D)
    (first,) = gather_axis(
        spot["y"], first, "y", [(2, 2, 24, EXT)], lambda s: [(..., 0, (s & 1, s >> 1))], "first_y"
    )
    (second,) = gather_axis(
        spot["z"], second, "z", [(2, 2, 24, D)], lambda s: [(..., 0, (s >> 1, s & 1))], "second_z"
    )
    first, second = lax.optimization_barrier((first, second))
    (first,) = gather_axis(
        spot["z"],
        first,
        "z",
        [(2, 2, 2, 2, 24, EXT)],
        lambda s: [(..., 0, (every, s >> 1, s & 1))],
        "first_z",
    )
    (second,) = gather_axis(
        spot["x"],
        second,
        "x",
        [(2, 4, 2, 24, D)],
        lambda s: [(..., 0, (every, s))],
        "second_x",
    )
    first, second, natural, key_mask, self_mask, line = lax.optimization_barrier(
        (first, second, natural, key_mask, self_mask, line)
    )
    wout = lax.all_gather(after(wout, natural), "dp", axis=0, tiled=True)
    left = lax.ppermute(natural[ROWS - BLOCK :], "fsdp", TO_RIGHT)
    right = lax.ppermute(natural[:BLOCK], "fsdp", TO_LEFT)
    first = first.reshape(2, 2, 4, 24, EXT)
    parts = [first] + relay([first] * 3, "x")
    packed = jnp.concatenate(
        [
            cot_long,
            teacher,
            jnp.broadcast_to(slot_weight[:, None], (ROWS, 128)).astype(bf16),
        ],
        1,
    )
    packed = exchange(pieces(after(packed, natural)), "fsdp")
    *parts, left, right, packed = lax.optimization_barrier((*parts, left, right, packed))
    (first,) = place_parts(
        spot["x"],
        parts,
        [(2, 2, 4, 4, 24, EXT)],
        lambda s: [(..., 0, (every, every, s))],
        "first_x",
    )
    first = first.reshape(2, D, EXT)
    first_other = swap(first)
    second = after(second.reshape(16, 24, D), first_other)
    second_parts = [second] + relay([second] * 3, "y")
    side = first[0, :, D:].astype(f32)
    whole_count = side[:, 4] * 16.0 + side[:, 5]
    count = jnp.sum(jnp.where(jnp.arange(D) % 6 == 0, whole_count, 0.0))
    norms = jnp.pad(side[:, :4].T, ((0, 4), (0, 0)))

    packed = exchange(packed[inverse], "fsdp")
    rows, acts, proj = project(place, left, natural, right, globs, norms, first, first_other)
    long_out, long_lse, part_out, part_lse = attend(place, table, line, key_mask, self_mask, proj)

    sent = jnp.concatenate(
        [part_out, split3(part_lse.reshape(HEADS, 128)), jnp.zeros((12, 128), bf16)], 0
    )
    packed = after(packed, long_out)
    sent = jnp.broadcast_to(after(sent, packed)[None], (4, 816, 128))
    second_parts = lax.optimization_barrier((*second_parts, sent))[:-1]
    got = exchange(sent, "fsdp", QUADS)
    (second,) = place_parts(
        spot["y"],
        second_parts,
        [(2, 16, 2, 24, D)],
        lambda s: [(..., 0, (s & 1, every, s >> 1))],
        "second_y",
    )
    second = second.reshape(2, D, D)
    second_other = swap(second)

    packed = unpieces(packed)
    lses = join3(got[:, D:])
    high = jnp.max(lses, 0)
    glob_lse = high + jnp.log(jnp.sum(jnp.exp(lses - high), 0))
    shares = jnp.pad(jnp.exp(lses - glob_lse), ((0, 0), (0, 4), (0, 0)))
    glob_lse = glob_lse.reshape(6, 1, 256)

    (
        result,
        loss_sum,
        glob_out,
        grad_middle,
        grad_mixed,
        wattn_grad,
        win_send,
        win_keep,
        wout_grad,
        norm_two,
    ) = feed(
        place,
        (2.0 / count)[None],
        rows,
        long_out,
        got,
        shares,
        packed,
        globs,
        norms,
        wout,
        first,
        first_other,
        second,
        second_other,
    )
    (two,) = add_pairs([(win_keep, swap(win_send))], "add_cores")
    grads, rel = attend_back(
        place, table, line, key_mask, self_mask, proj, grad_mixed, long_lse, glob_out, glob_lse
    )
    grads, two = lax.optimization_barrier((grads, two))
    two = exchange(two.reshape(64, 24, D), BOTH, SAME_CORE)
    grad_nat, back_left, back_right, back_glob, totals = input_grad(
        place, rows, grads, norms, grad_middle, rel, norm_two, loss_sum, first, first_other
    )
    from_left = lax.ppermute(back_right, "fsdp", TO_RIGHT)
    from_right = lax.ppermute(back_left, "fsdp", TO_LEFT)
    both = pack_rows(result, grad_nat, from_left, from_right)
    one_send, one_keep = weight_grad(place, acts, grads, wattn_grad, totals)
    one_send, one_keep, two, both = lax.optimization_barrier((one_send, one_keep, two, both))
    out_grad = lax.psum_scatter(
        wout_grad.reshape(4 * D, D), "fsdp", scatter_dimension=0, tiled=True
    )
    one = scatter_axis(
        spot["x"],
        [one_keep, swap(one_send)],
        "x",
        lambda s: [(g * 4 + s) * 4 for g in range(4)],
        4,
        "one_x",
    )
    both = exchange(both, "fsdp")[order]
    out_grad = after(out_grad, both).reshape(2, 4, 24, D)
    cut = [
        lax.dynamic_index_in_dim(out_grad, spot["x"][0] ^ k, 1, keepdims=False) for k in range(4)
    ]
    out_grad = total_of([cut[0]] + relay(cut[1:], "x"))
    z_hi = spot["z"][0] >> 1
    far = lax.dynamic_index_in_dim(out_grad, 1 - z_hi, 0, keepdims=False).astype(bf16)
    near = lax.dynamic_index_in_dim(out_grad, z_hi, 0, keepdims=False)
    out_grad = near + lax.ppermute(far, BOTH, PARTNERS["z"][1]).astype(f32)
    *one, both = lax.optimization_barrier((*one, both))
    out_long, grad_long = unpack_rows(exchange(both, "fsdp"))
    two = jnp.sum(two.astype(f32), 0)
    out_glob = lax.dynamic_slice_in_dim(result, ROWS + quarter * 32, 32, 0)
    one = scatter_axis(
        spot["z"], one, "z", lambda s: [s * 2, (4 + s) * 2], 2, "one_z"
    )
    one = scatter_axis(spot["y"], one, "y", lambda s: [(s & 1) * 2 + (s >> 1)], 1, "one_y")
    one = lax.optimization_barrier((*one, out_long, out_grad))[:4]
    small = [part[1, :8].astype(f32) + part[1, 8:16].astype(f32) for part in one]
    small = (small[0] + small[1]) + (small[2] + small[3])
    one = [part[0] for part in one]
    closing = jnp.concatenate(
        [
            back_glob.reshape(4, 32, D),
            total_of(one).reshape(4, 6, D),
            two.reshape(4, 6, D),
            jnp.zeros((4, 4, D), f32),
        ],
        1,
    )
    closing = exchange(after(closing, out_long), "fsdp", QUADS)
    grad_glob = lax.dynamic_slice_in_dim(grad_middle, ROWS + quarter * 32, 32, 0) + jnp.sum(
        closing[:, :32], 0
    )
    one, two = closing[:, 32:38], closing[:, 38:44]
    qkv_grad = one[:3].transpose(1, 0, 2).reshape(6, 3 * D)
    attn_grad = one[3]
    in_grad = two.transpose(1, 0, 2).reshape(6, 4 * D)
    bands = small[4:].reshape(HEADS, 256)[:, 44 : 44 + LABELS]
    label_grad = jnp.dot(picker.T, bands.T, precision=HIGHEST)
    rel_total = jnp.concatenate([label_grad, small[4:5, :HEADS], small[4:5, HEADS : 2 * HEADS]], 0)
    loss_total = small[4, 24]
    mine_norm = lax.dynamic_slice_in_dim(small[:4], device * 6, 6, 1).T
    return (
        out_long,
        out_glob,
        loss_total / count,
        grad_long,
        grad_glob,
        qkv_grad,
        attn_grad,
        in_grad,
        out_grad,
        mine_norm[:, 0::2],
        mine_norm[:, 1::2],
        rel_total,
    )


def solution(mesh):
    rows = P(BOTH, None)
    in_specs = (rows,) * 11 + (P(), P("dp"), P("dp", None), P("dp"), P(), P(BOTH))
    out_specs = (rows, rows, P(), rows, rows, rows, rows, rows, rows, rows, rows, P())
    return jax.shard_map(shards, mesh=mesh, in_specs=in_specs, out_specs=out_specs, check_vma=False)
```

```python
import jax
import jax.numpy as jnp
from jax import lax
from jax.experimental import pallas as pl
from jax.experimental.pallas import tpu as pltpu
from jax.sharding import PartitionSpec as P

D = 768
HEADS = 12
HEAD = 64
RADIUS = 84
LABELS = 169
BLOCK = 128
SEQ_BLOCKS = 16
GLOBAL_EVERY = 16
GSEQ = 128
ROWS = 512
EXT = 896
EPS = 1e-05
MASKED = -1e30
HIGHEST = lax.Precision.HIGHEST
BOTH = ("dp", "fsdp")
f32 = jnp.float32
bf16 = jnp.bfloat16

QUADS = [[4 * i + j for j in range(4)] for i in range(4)]
SAME_CORE = [[4 * g + 2 * p + c for p in range(2) for g in range(32)] for c in range(2)]
SWAP = [(i, i ^ 1) for i in range(16)]
TO_RIGHT = [(i, i + 1) for i in range(16) if i % 4 < 3]
TO_LEFT = [(i, i - 1) for i in range(16) if i % 4 > 0]


def flip(device, axis, step):
    if axis == "x":
        return device ^ (step << 4)
    if axis == "y":
        return device ^ (step << 1)
    return device ^ ((step >> 1) << 6) ^ ((step & 1) << 3)


PARTNERS = {
    axis: [[(i, flip(i, axis, step)) for i in range(128)] for step in (1, 2, 3)] for axis in "xyz"
}


def exchange(value, axis, groups=None):
    return lax.all_to_all(value, axis, 0, 0, axis_index_groups=groups, tiled=True)


def swap(value):
    return lax.ppermute(value, "fsdp", SWAP)


def relay(values, axis):
    return [lax.ppermute(value, BOTH, pairs) for value, pairs in zip(values, PARTNERS[axis])]


def after(value, *others):
    return lax.optimization_barrier((value,) + others)[0]


ANY = pl.BlockSpec(memory_space=pl.ANY)
SCALARS = pl.BlockSpec(memory_space=pltpu.SMEM)


def cost(microseconds):
    return pl.CostEstimate(
        flops=int(microseconds * 1.1e9),
        bytes_accessed=int(microseconds * 3.6e6),
        transcendentals=0,
    )


def place_parts(spot, parts, shapes, moves, name):
    def kernel(spot_ref, *refs):
        ins, outs = refs[:4], refs[4:]
        for k in range(4):
            for source, which, target in moves(spot_ref[0] ^ k):
                outs[which][target] = ins[k][source]

    vm = pl.BlockSpec(memory_space=pltpu.VMEM)
    return pl.pallas_call(
        kernel,
        in_specs=[SCALARS] + [vm] * 4,
        out_specs=[vm] * len(shapes),
        out_shape=[jax.ShapeDtypeStruct(shape, bf16) for shape in shapes],
        compiler_params=params(32),
        cost_estimate=cost(2),
        name=name,
    )(spot, *parts)


def gather_axis(spot, value, axis, shapes, moves, name):
    return place_parts(spot, [value] + relay([value] * 3, axis), shapes, moves, name)


def encode(value):
    high = value.astype(bf16)
    return high, (value - high.astype(f32)).astype(bf16)


def fold_parts(spot, parts, starts, length, name):
    count = parts[0].shape[0] // 4 * 4
    extra = parts[0].shape[0] - count
    size = count // 4

    def kernel(spot_ref, *refs):
        ins, outs = refs[: len(parts)], refs[len(parts) :]
        for k in range(4):
            for i, start in enumerate(starts(spot_ref[0] ^ k)):
                total = ins[0][pl.ds(start, length)].astype(f32)
                for other in ins[1:]:
                    total = total + other[pl.ds(start, length)].astype(f32)
                outs[k][i * length : (i + 1) * length] = total.astype(bf16)
        if extra:
            small = [ref[count, :8].astype(f32) + ref[count, 8:16].astype(f32) for ref in ins]
            small = [small[i] + small[i + 1] for i in range(0, len(ins), 2)]
            high, low = encode(small[0] if len(small) == 1 else small[0] + small[1])
            for out in outs:
                out[size, :8] = high
                out[size, 8:16] = low
                out[size, 16:] = jnp.zeros((8, D), bf16)

    vm = pl.BlockSpec(memory_space=pltpu.VMEM)
    return pl.pallas_call(
        kernel,
        in_specs=[SCALARS] + [vm] * len(parts),
        out_specs=[vm] * 4,
        out_shape=[jax.ShapeDtypeStruct((size + extra, 24, D), bf16)] * 4,
        compiler_params=params(32),
        cost_estimate=cost(2),
        name=name,
    )(spot, *parts)


def add_pairs(pairs, name):
    def kernel(*refs):
        for i in range(len(pairs)):
            ours, theirs = refs[2 * i][...].astype(f32), refs[2 * i + 1][...].astype(f32)
            refs[2 * len(pairs) + i][...] = (ours + theirs).astype(bf16)

    block = pl.BlockSpec((384, D), lambda i: (i, 0))
    return pl.pallas_call(
        kernel,
        grid=(4,),
        in_specs=[block] * (2 * len(pairs)),
        out_specs=[block] * len(pairs),
        out_shape=[jax.ShapeDtypeStruct((2 * D, D), bf16)] * len(pairs),
        compiler_params=params(32),
        cost_estimate=cost(4),
        name=name,
    )(*[part.reshape(2 * D, D) for pair in pairs for part in pair])


def scatter_axis(spot, parts, axis, starts, length, name):
    cut = fold_parts(spot, parts, starts, length, name)
    return [cut[0]] + relay(cut[1:], axis)


def pack_rows(result, nat, from_left, from_right):
    def kernel(result_ref, nat_ref, left_ref, right_ref, out):
        for block in range(4):
            rows = slice(128 * block, 128 * block + 128)
            grad = nat_ref[rows]
            if block == 0:
                grad = grad + left_ref[...].astype(f32)
            if block == 3:
                grad = grad + right_ref[...].astype(f32)
            for piece in range(16):
                low = 8 * piece
                out[4 * piece + block, :, D:] = grad[low : low + 8].astype(bf16)
                out[4 * piece + block, :, :D] = result_ref[
                    128 * block + low : 128 * block + low + 8
                ]

    vm = pl.BlockSpec(memory_space=pltpu.VMEM)
    return pl.pallas_call(
        kernel,
        in_specs=[vm] * 4,
        out_specs=vm,
        out_shape=jax.ShapeDtypeStruct((64, 8, 2 * D), bf16),
        compiler_params=params(32),
        cost_estimate=cost(3),
        name="pack_rows",
    )(result, nat, from_left, from_right)


def unpack_rows(value):
    def kernel(value_ref, long_ref, grad_ref):
        for block in range(4):
            for piece in range(16):
                low = 128 * block + 8 * piece
                long_ref[low : low + 8] = value_ref[4 * piece + block, :, :D]
                grad_ref[low : low + 8] = value_ref[4 * piece + block, :, D:].astype(f32)

    vm = pl.BlockSpec(memory_space=pltpu.VMEM)
    return pl.pallas_call(
        kernel,
        in_specs=[vm],
        out_specs=[vm] * 2,
        out_shape=[jax.ShapeDtypeStruct((ROWS, D), bf16), jax.ShapeDtypeStruct((ROWS, D), f32)],
        compiler_params=params(32),
        cost_estimate=cost(3),
        name="unpack_rows",
    )(value)


def total_of(parts):
    total = parts[0].astype(f32)
    for part in parts[1:]:
        total = total + part.astype(f32)
    return total


def pieces(rows):
    width = rows.shape[-1]
    return rows.reshape(4, 16, 8, width).transpose(1, 0, 2, 3).reshape(64, 8, width)


def unpieces(value):
    width = value.shape[-1]
    return value.reshape(16, 4, 8, width).transpose(1, 0, 2, 3).reshape(ROWS, width)


def reorder(rows, index):
    spread = exchange(pieces(rows), "fsdp")
    return unpieces(exchange(spread[index], "fsdp"))


def split3(value):
    high = value.astype(bf16)
    rest = value - high.astype(f32)
    mid = rest.astype(bf16)
    low = (rest - mid.astype(f32)).astype(bf16)
    return jnp.concatenate([high, mid, low], 0)


def join3(value):
    value = value.astype(f32)
    return value[:, :HEADS] + value[:, HEADS : 2 * HEADS] + value[:, 2 * HEADS : 3 * HEADS]


def dot_nn(a, b):
    return lax.dot_general(a, b, (((1,), (0,)), ((), ())), preferred_element_type=f32)


def dot_nt(a, b):
    return lax.dot_general(a, b, (((1,), (1,)), ((), ())), preferred_element_type=f32)


def dot_tn(a, b):
    return lax.dot_general(a, b, (((0,), (0,)), ((), ())), preferred_element_type=f32)


def whole(shape):
    zeros = (0,) * len(shape)
    return pl.BlockSpec(shape, lambda *_: zeros, pipeline_mode=pl.Buffered(1))


def params(megabytes):
    return pltpu.CompilerParams(vmem_limit_bytes=megabytes << 20)


def normalise(values):
    centre = jnp.mean(values, -1, keepdims=True)
    centred = values - centre
    spread = jnp.mean(centred * centred, -1, keepdims=True)
    factor = lax.rsqrt(spread + EPS)
    return centred * factor, factor


def load_quarters(core, mine, other, target, sems, count):
    copies = []
    for p in range(2):
        copies.append(pltpu.make_async_copy(mine.at[p, :, pl.ds(0, D)], target.at[2 * p + core], sems.at[2 * p]))
        copies.append(
            pltpu.make_async_copy(
                other.at[p, :, pl.ds(0, D)], target.at[2 * p + 1 - core], sems.at[2 * p + 1]
            )
        )
    for copy in copies:
        copy.start()
    return copies


def quarter_copy(step, core, mine, target, sems):
    slot = 2 * (step // 2) + jnp.where(step % 2 == core, 0, 1)
    return pltpu.make_async_copy(mine.at[0, :, pl.ds(0, D)], target.at[step], sems.at[slot])


def project_kernel(
    place, left, nat, right, globs, norms, mine, other, rows_out, acts_out, proj_out, w, sems
):
    step = pl.program_id(0)
    core = place[1]

    @pl.when(step == 0)
    def _():
        load_quarters(core, mine, other, w, sems, 4)
        rows_out[:128] = left[...]
        rows_out[128:640] = nat[...]
        rows_out[640:768] = right[...]
        rows_out[768:] = globs[:, :D]
        normal, _ = normalise(rows_out[...].astype(f32))
        acts_out[...] = (normal * norms[0:1] + norms[2:3]).astype(bf16)

    quarter_copy(step, core, mine, w, sems).wait()
    proj_out[...] = dot_nn(acts_out[...], w[step]).astype(bf16)

    @pl.when(step == 2)
    def _():
        quarter_copy(step + 1, core, mine, w, sems).wait()


def project(place, left, nat, right, globs, norms, mine, other):
    return pl.pallas_call(
        project_kernel,
        grid=(3,),
        in_specs=[
            SCALARS,
            whole((128, D)),
            whole((ROWS, D)),
            whole((128, D)),
            whole((128, 2 * D)),
            whole((8, D)),
            ANY,
            ANY,
        ],
        out_specs=[
            whole((EXT, D)),
            whole((EXT, D)),
            pl.BlockSpec((EXT, D), lambda i: (0, i)),
        ],
        scratch_shapes=[pltpu.VMEM((4, D, D), bf16), pltpu.SemaphoreType.DMA((4,))],
        out_shape=(
            jax.ShapeDtypeStruct((EXT, D), bf16),
            jax.ShapeDtypeStruct((EXT, D), bf16),
            jax.ShapeDtypeStruct((EXT, 3 * D), bf16),
        ),
        compiler_params=params(50),
        cost_estimate=cost(9),
        name="project",
    )(place, left, nat, right, globs, norms, mine, other)


def stack_heads(rows):
    first = lax.broadcasted_iota(jnp.int32, rows.shape, 1) < HEAD
    zero = jnp.zeros_like(rows)
    return jnp.concatenate([jnp.where(first, rows, zero), jnp.where(first, zero, rows)], 0)


def merge_heads(value):
    first = lax.broadcasted_iota(jnp.int32, (128, 128), 0) < HEAD
    return jnp.where(first, value[:, :128], value[:, 128:]).T


def band_tile(line):
    tiles = []
    for head in range(2):
        spread = jnp.broadcast_to(line[head : head + 1], (BLOCK, 512))
        rolled = pltpu.roll(spread, 0, 1, stride=1, stride_axis=0)
        tiles.append(
            jnp.concatenate([rolled[:, 128 * i : 128 * i + 128].T for i in range(3)], 0)
        )
    return jnp.concatenate(tiles, 1)


def pair_row(first, second):
    lane = lax.broadcasted_iota(jnp.int32, (1, 256), 1)
    return jnp.where(lane < 128, first, second)


def long_owned(run):
    key = lax.broadcasted_iota(jnp.int32, (128, 256), 0)
    lane = lax.broadcasted_iota(jnp.int32, (128, 256), 1)
    return key == run + lax.shift_right_logical(lane & 127, 4)


def cross_owned(run):
    key = lax.broadcasted_iota(jnp.int32, (ROWS, 256), 0)
    lane = lax.broadcasted_iota(jnp.int32, (ROWS, 256), 1)
    return run + lax.shift_right_logical(key, 4) == (lane & 127)


def attend_kernel(
    place, table, line, key_mask, self_mask, q, k, v, out, lse, glob_out, glob_lse, band
):
    pair = pl.program_id(0)
    run = place[0] * 32
    own = pair_row(table[0, 2 * pair], table[0, 2 * pair + 1])
    other = pair_row(table[1, 2 * pair], table[1, 2 * pair + 1])
    band[...] = band_tile(line[0])
    values = v[...].T
    for j in range(4):
        low = 128 * j
        query = stack_heads(q[128 + low : 256 + low, :] * 0.125)
        near = dot_nt(k[low : low + 384, :], query) + (band[...] + key_mask[low : low + 384, :])
        far = dot_nt(k[768:, :], query) + (
            jnp.where(long_owned(run + 8 * j), own, other) + key_mask[768:, :]
        )
        top = jnp.maximum(jnp.max(near, 0, keepdims=True), jnp.max(far, 0, keepdims=True))
        near = jnp.exp(near - top)
        far = jnp.exp(far - top)
        total = jnp.sum(near, 0, keepdims=True) + jnp.sum(far, 0, keepdims=True)
        share = 1.0 / total
        got = dot_nn(values[:, low : low + 384], (near * share).astype(bf16)) + dot_nn(
            values[:, 768:], (far * share).astype(bf16)
        )
        out[low : low + 128, :] = merge_heads(got).astype(bf16)
        lse[0, j : j + 1, :] = top + jnp.log(total)
    query = stack_heads(q[768:, :] * 0.125)
    near = dot_nt(k[128:640, :], query) + (
        jnp.where(cross_owned(run), own, other) + key_mask[128:640, :]
    )
    far = dot_nt(k[768:, :], query) + self_mask[...]
    top = jnp.maximum(jnp.max(near, 0, keepdims=True), jnp.max(far, 0, keepdims=True))
    near = jnp.exp(near - top)
    far = jnp.exp(far - top)
    total = jnp.sum(near, 0, keepdims=True) + jnp.sum(far, 0, keepdims=True)
    share = 1.0 / total
    got = dot_nn(values[:, 128:640], (near * share).astype(bf16)) + dot_nn(
        values[:, 768:], (far * share).astype(bf16)
    )
    first = lax.broadcasted_iota(jnp.int32, (128, 128), 0) < HEAD
    glob_out[...] = jnp.where(first, got[:, :128], got[:, 128:]).astype(bf16)
    glob_lse[0] = top + jnp.log(total)


def column(width, offset):
    return pl.BlockSpec((width, 128), lambda h: (0, h + offset))


def attend(place, table, line, key_mask, self_mask, proj):
    return pl.pallas_call(
        attend_kernel,
        grid=(6,),
        in_specs=[
            SCALARS,
            SCALARS,
            pl.BlockSpec((1, 2, 512), lambda h: (h, 0, 0)),
            whole((EXT, 256)),
            whole((128, 256)),
            column(EXT, 0),
            column(EXT, 6),
            column(EXT, 12),
        ],
        out_specs=[
            column(ROWS, 0),
            pl.BlockSpec((1, 4, 256), lambda h: (h, 0, 0)),
            pl.BlockSpec((128, 128), lambda h: (h, 0)),
            pl.BlockSpec((1, 1, 256), lambda h: (h, 0, 0)),
        ],
        out_shape=(
            jax.ShapeDtypeStruct((ROWS, D), bf16),
            jax.ShapeDtypeStruct((6, 4, 256), f32),
            jax.ShapeDtypeStruct((D, 128), bf16),
            jax.ShapeDtypeStruct((6, 1, 256), f32),
        ),
        scratch_shapes=[pltpu.VMEM((384, 256), f32)],
        compiler_params=params(40),
        cost_estimate=cost(15),
        name="attend",
    )(place, table, line, key_mask, self_mask, proj, proj, proj)


def fold_band(tile):
    rows = jnp.concatenate([tile[128 * i : 128 * i + 128].T for i in range(3)], 1)
    rows = jnp.concatenate([rows, jnp.zeros((BLOCK, 128), f32)], 1)
    total = rows[:8]
    for a in range(1, 16):
        total = total + pltpu.roll(rows[8 * a : 8 * a + 8], 512 - 8 * a, 1)
    row = lax.broadcasted_iota(jnp.int32, (8, 512), 0)
    for bit in (1, 2, 4):
        total = jnp.where((row & bit) != 0, pltpu.roll(total, 512 - bit, 1), total)
    return jnp.sum(total, 0, keepdims=True)


def attend_back_kernel(
    place,
    table,
    line,
    key_mask,
    self_mask,
    q,
    k,
    v,
    grad,
    lse,
    glob_out,
    glob_lse,
    grads,
    rel,
    band,
    band_sum,
    key_sum,
    value_sum,
):
    pair = pl.program_id(0)
    run = place[0] * 32
    own = pair_row(table[0, 2 * pair], table[0, 2 * pair + 1])
    other = pair_row(table[1, 2 * pair], table[1, 2 * pair + 1])
    band[...] = band_tile(line[0])
    keys = k[...].T
    band_sum[...] = jnp.zeros_like(band_sum)
    key_sum[...] = jnp.zeros_like(key_sum)
    value_sum[...] = jnp.zeros_like(value_sum)
    owned_sum = jnp.zeros((1, 256), f32)
    other_sum = jnp.zeros((1, 256), f32)
    grads[0, :128] = jnp.zeros((128, 128), bf16)
    grads[0, 640:768] = jnp.zeros((128, 128), bf16)
    for j in range(4):
        low = 128 * j
        query = stack_heads(q[128 + low : 256 + low, :] * 0.125)
        back = stack_heads(grad[low : low + 128, :])
        near = dot_nt(k[low : low + 384, :], query) + (band[...] + key_mask[low : low + 384, :])
        owned = long_owned(run + 8 * j)
        far = dot_nt(k[768:, :], query) + (jnp.where(owned, own, other) + key_mask[768:, :])
        top = lse[0, j : j + 1, :]
        near = jnp.exp(near - top)
        far = jnp.exp(far - top)
        near_d = dot_nt(v[low : low + 384, :], back)
        far_d = dot_nt(v[768:, :], back)
        delta = jnp.sum(near * near_d, 0, keepdims=True) + jnp.sum(far * far_d, 0, keepdims=True)
        near_d = (near * (near_d - delta)).astype(bf16)
        far_d = (far * (far_d - delta)).astype(bf16)
        key_sum[low : low + 384, :] += dot_nn(near_d, query)
        value_sum[low : low + 384, :] += dot_nn(near.astype(bf16), back)
        key_sum[768:, :] += dot_nn(far_d, query)
        value_sum[768:, :] += dot_nn(far.astype(bf16), back)
        got = dot_nn(keys[:, low : low + 384], near_d) + dot_nn(keys[:, 768:], far_d)
        grads[0, 128 + low : 256 + low, :] = (merge_heads(got) * 0.125).astype(bf16)
        band_sum[...] += near_d.astype(f32)
        far_d = far_d.astype(f32)
        owned_sum += jnp.sum(jnp.where(owned, far_d, 0.0), 0, keepdims=True)
        other_sum += jnp.sum(jnp.where(owned, 0.0, far_d), 0, keepdims=True)
    query = stack_heads(q[768:, :] * 0.125)
    back = stack_heads(grad[ROWS:, :])
    owned = cross_owned(run)
    near = dot_nt(k[128:640, :], query) + (jnp.where(owned, own, other) + key_mask[128:640, :])
    far = dot_nt(k[768:, :], query) + self_mask[...]
    top = glob_lse[0]
    near = jnp.exp(near - top)
    far = jnp.exp(far - top)
    near_d = dot_nt(v[128:640, :], back)
    far_d = dot_nt(v[768:, :], back)
    product = grad[ROWS:, :].astype(f32).T * glob_out[...].astype(f32)
    delta = jnp.concatenate(
        [
            jnp.sum(product[:HEAD], 0, keepdims=True),
            jnp.sum(product[HEAD:], 0, keepdims=True),
        ],
        1,
    )
    near_d = (near * (near_d - delta)).astype(bf16)
    far_d = (far * (far_d - delta)).astype(bf16)
    key_sum[128:640, :] += dot_nn(near_d, query)
    value_sum[128:640, :] += dot_nn(near.astype(bf16), back)
    key_sum[768:, :] += dot_nn(far_d, query)
    value_sum[768:, :] += dot_nn(far.astype(bf16), back)
    got = dot_nn(keys[:, 128:640], near_d) + dot_nn(keys[:, 768:], far_d)
    grads[0, 768:, :] = (merge_heads(got) * 0.125).astype(bf16)
    near_d = near_d.astype(f32)
    owned_sum += jnp.sum(jnp.where(owned, near_d, 0.0), 0, keepdims=True)
    other_sum += jnp.sum(jnp.where(owned, 0.0, near_d), 0, keepdims=True)
    grads[1] = key_sum[...].astype(bf16)
    grads[2] = value_sum[...].astype(bf16)
    rel[0] = jnp.zeros((8, 512), f32)
    for head in range(2):
        lanes = slice(128 * head, 128 * head + 128)
        rel[0, head : head + 1, :] = fold_band(band_sum[:, lanes])
        rel[0, 2 + head : 3 + head, :128] = owned_sum[:, lanes]
        rel[0, 4 + head : 5 + head, :128] = other_sum[:, lanes]


def attend_back(place, table, line, key_mask, self_mask, proj, grad, lse, glob_out, glob_lse):
    return pl.pallas_call(
        attend_back_kernel,
        grid=(6,),
        in_specs=[
            SCALARS,
            SCALARS,
            pl.BlockSpec((1, 2, 512), lambda h: (h, 0, 0)),
            whole((EXT, 256)),
            whole((128, 256)),
            column(EXT, 0),
            column(EXT, 6),
            column(EXT, 12),
            column(640, 0),
            pl.BlockSpec((1, 4, 256), lambda h: (h, 0, 0)),
            pl.BlockSpec((128, 128), lambda h: (h, 0)),
            pl.BlockSpec((1, 1, 256), lambda h: (h, 0, 0)),
        ],
        out_specs=[
            pl.BlockSpec((3, EXT, 128), lambda h: (0, 0, h)),
            pl.BlockSpec((1, 8, 512), lambda h: (h, 0, 0)),
        ],
        out_shape=(
            jax.ShapeDtypeStruct((3, EXT, D), bf16),
            jax.ShapeDtypeStruct((6, 8, 512), f32),
        ),
        scratch_shapes=[
            pltpu.VMEM((384, 256), f32),
            pltpu.VMEM((384, 256), f32),
            pltpu.VMEM((EXT, 128), f32),
            pltpu.VMEM((EXT, 128), f32),
        ],
        compiler_params=params(48),
        cost_estimate=cost(21),
        name="attend_back",
    )(place, table, line, key_mask, self_mask, proj, proj, proj, grad, lse, glob_out, glob_lse)


def feed_kernel(
    place,
    coef,
    rows,
    long_out,
    parts,
    shares,
    packed,
    globs,
    norms,
    wout,
    first_mine,
    first_other,
    in_mine,
    in_other,
    result_out,
    loss_out,
    glob_out,
    middle_grad_out,
    mixed_grad_out,
    wattn_grad,
    win_send,
    win_keep,
    wout_grad,
    norm_grads,
    mixed,
    acts,
    normal,
    total,
    hidden,
    slope,
    grad_z,
    grad_acts,
    factor,
    wa,
    win,
    sem,
    sems,
):
    step = pl.program_id(0)
    core = place[1]


    def attn_copy(source):
        return pltpu.make_async_copy(source.at[1, :, pl.ds(0, D)], wa, sem)

    quarter = place[0]
    forward = step < 4
    late = jnp.maximum(step - 4, 0)
    chunk = jnp.where(
        forward, step, jnp.where(late < 2, 2 * late + 1 - core, 2 * (late - 2) + core)
    )

    def owned():
        row = lax.broadcasted_iota(jnp.int32, (640, 1), 0)
        first = ROWS + quarter * 32
        return (row < ROWS) | ((row >= first) & (row < first + 32))

    @pl.when(step == 0)
    def _():
        @pl.when(core == 1)
        def _():
            attn_copy(first_mine).start()

        @pl.when(core == 0)
        def _():
            attn_copy(first_other).start()

        load_quarters(core, in_mine, in_other, win, sems, 4)
        mixed[:ROWS] = long_out[...]
        for pair in range(6):
            sums = jnp.zeros((128, 128), f32)
            top = lax.broadcasted_iota(jnp.int32, (128, 128), 0) < HEAD
            for source in range(4):
                share = jnp.where(
                    top,
                    shares[source, 2 * pair : 2 * pair + 1, :],
                    shares[source, 2 * pair + 1 : 2 * pair + 2, :],
                )
                sums = sums + parts[source, 128 * pair : 128 * pair + 128, :].astype(f32) * share
            glob_out[128 * pair : 128 * pair + 128, :] = sums.astype(bf16)
            mixed[ROWS:, 128 * pair : 128 * pair + 128] = sums.T.astype(bf16)
        attn_copy(first_mine).wait()
        middle = dot_nn(mixed[...], wa[...])
        middle = middle + jnp.concatenate(
            [rows[128:640].astype(f32), rows[768:].astype(f32)], 0
        )
        total[...] = middle
        base, scale = normalise(middle)
        normal[...] = base
        factor[...] = scale
        acts[...] = (base * norms[1:2] + norms[3:4]).astype(bf16)
        for p in range(4):
            pltpu.make_async_copy(in_mine.at[0, :, pl.ds(0, D)], win.at[0], sems.at[p]).wait()

    @pl.when(forward)
    def _():
        inner = dot_nn(acts[...], win[chunk])
        half = 0.5 + 0.5 * lax.erf(inner * 0.7071067811865476)
        slope[chunk] = half + inner * (jnp.exp(-0.5 * inner * inner) * 0.3989422804014327)
        bits = (inner * half).astype(bf16)
        hidden[chunk] = bits
        total[...] += dot_nn(bits, wout[...])

    @pl.when(step == 3)
    def _():
        result = total[...]
        result_out[...] = result.astype(bf16)
        weight = packed[:, 2 * D : 2 * D + 1].astype(f32)
        error = result[:ROWS] - packed[:, D : 2 * D].astype(f32)
        masked = weight * error
        loss_out[...] = jnp.broadcast_to(
            jnp.sum(jnp.sum(masked * error, 0, keepdims=True), 1, keepdims=True), (8, 128)
        )
        grad = jnp.concatenate(
            [packed[:, :D].astype(f32) + coef[0] * masked, globs[:, D:].astype(f32)], 0
        )
        total[...] = grad
        grad_z[...] = grad.astype(bf16)
        grad_acts[...] = jnp.zeros_like(grad_acts)

    @pl.when(step >= 4)
    def _():
        keep_rows = owned()
        grad_inner = (dot_nt(grad_z[...], wout[...]) * slope[chunk]).astype(bf16)
        zeros = jnp.zeros_like(grad_inner)
        grad_acts[...] += dot_nt(grad_inner, win[chunk])
        part = dot_tn(acts[...], jnp.where(keep_rows, grad_inner, zeros)).astype(bf16)

        @pl.when(late < 2)
        def _():
            win_send[0] = part

        @pl.when(late >= 2)
        def _():
            win_keep[0] = part

        part = dot_tn(hidden[chunk], jnp.where(keep_rows, grad_z[...], zeros))
        part = part.reshape(2, 16, 24, D).astype(bf16)
        for i in range(2):
            wout_grad[:, i] = part[i]

    @pl.when(step == 7)
    def _():
        keep_rows = owned()
        grad = grad_acts[...]
        base = normal[...]
        mine = jnp.where(keep_rows, grad, 0.0)
        norm_grads[0:1, :] = jnp.sum(mine * base, 0, keepdims=True)
        norm_grads[1:2, :] = jnp.sum(mine, 0, keepdims=True)
        scaled = grad * norms[1:2]
        first = jnp.mean(scaled, -1, keepdims=True)
        second = jnp.mean(scaled * base, -1, keepdims=True)
        middle = total[...] + factor[...] * (scaled - first - base * second)
        middle_grad_out[...] = middle
        branch = middle.astype(bf16)
        mixed_grad_out[...] = dot_nt(branch, wa[...]).astype(bf16)
        wattn_grad[...] = dot_tn(
            mixed[...], jnp.where(keep_rows, branch, jnp.zeros_like(branch))
        ).astype(bf16)


def feed(place, coef, rows, long_out, parts, shares, packed, globs, norms, *weights):
    def chunk(t, place):
        late = jnp.maximum(t - 4, 0)
        core = place[1]
        back = jnp.where(late < 2, 2 * late + 1 - core, 2 * (late - 2) + core)
        return jnp.where(t < 4, t, back)

    def back_chunk(t, place):
        return chunk(jnp.maximum(t, 4), place)

    def fixed(shape):
        zeros = (0,) * len(shape)
        return pl.BlockSpec(shape, lambda t, place: zeros, pipeline_mode=pl.Buffered(1))

    return pl.pallas_call(
        feed_kernel,
        grid_spec=pltpu.PrefetchScalarGridSpec(
            num_scalar_prefetch=1,
            grid=(8,),
            in_specs=[
                SCALARS,
                fixed((EXT, D)),
                fixed((ROWS, D)),
                fixed((4, 816, 128)),
                fixed((4, 16, 128)),
                fixed((ROWS, 2 * D + 128)),
                fixed((128, 2 * D)),
                fixed((8, D)),
                pl.BlockSpec((D, D), lambda t, place: (chunk(t, place), 0)),
                ANY,
                ANY,
                ANY,
                ANY,
            ],
            out_specs=[
                fixed((640, D)),
                fixed((8, 128)),
                fixed((D, 128)),
                fixed((640, D)),
                fixed((640, D)),
                fixed((D, D)),
                pl.BlockSpec((1, D, D), lambda t, place: (jnp.clip(t - 4, 0, 1), 0, 0)),
                pl.BlockSpec((1, D, D), lambda t, place: (jnp.clip(t - 6, 0, 1), 0, 0)),
                pl.BlockSpec((16, 2, 24, D), lambda t, place: (0, back_chunk(t, place), 0, 0)),
                fixed((8, D)),
            ],
            scratch_shapes=[
                pltpu.VMEM((640, D), bf16),
                pltpu.VMEM((640, D), bf16),
                pltpu.VMEM((640, D), f32),
                pltpu.VMEM((640, D), f32),
                pltpu.VMEM((4, 640, D), bf16),
                pltpu.VMEM((4, 640, D), f32),
                pltpu.VMEM((640, D), bf16),
                pltpu.VMEM((640, D), f32),
                pltpu.VMEM((640, 1), f32),
                pltpu.VMEM((D, D), bf16),
                pltpu.VMEM((4, D, D), bf16),
                pltpu.SemaphoreType.DMA,
                pltpu.SemaphoreType.DMA((4,)),
            ],
        ),
        out_shape=(
            jax.ShapeDtypeStruct((640, D), bf16),
            jax.ShapeDtypeStruct((8, 128), f32),
            jax.ShapeDtypeStruct((D, 128), bf16),
            jax.ShapeDtypeStruct((640, D), f32),
            jax.ShapeDtypeStruct((640, D), bf16),
            jax.ShapeDtypeStruct((D, D), bf16),
            jax.ShapeDtypeStruct((2, D, D), bf16),
            jax.ShapeDtypeStruct((2, D, D), bf16),
            jax.ShapeDtypeStruct((16, 8, 24, D), bf16),
            jax.ShapeDtypeStruct((8, D), f32),
        ),
        compiler_params=params(60),
        cost_estimate=cost(43),
        name="feed",
    )(place, coef, rows, long_out, parts, shares, packed, globs, norms, *weights)


def input_grad_kernel(
    place, rows, grads, norms, middle_grad, rel, norm_two, loss, mine, other,
    nat, left, right, globs, totals, w, sems, grad, small,
):
    step = pl.program_id(0)
    core = place[1]

    @pl.when(step == 0)
    def _():
        load_quarters(core, mine, other, w, sems, 4)
        grad[...] = jnp.zeros_like(grad)
        small[2:4, :] = norm_two[0:2, :]
        for n in range(HEADS):
            low = 256 * (n % 3)
            small[4 + n // 3 : 5 + n // 3, low : low + 256] = rel[n // 2, n % 2 : n % 2 + 1, :256]
        lane = lax.broadcasted_iota(jnp.int32, (1, 128), 1)
        line = jnp.where(lane == 24, loss[0:1, :], small[4:5, :128])
        for n in range(2 * HEADS):
            head, row = n % HEADS, 2 + 2 * (n // HEADS)
            part = rel[head // 2, row + head % 2 : row + head % 2 + 1, :128]
            line = jnp.where(lane == n, jnp.sum(part, 1, keepdims=True), line)
        small[4:5, :128] = line

    quarter_copy(step, core, mine, w, sems).wait()
    grad[...] += dot_nt(grads[0], w[step])

    @pl.when(step == 2)
    def _():
        quarter_copy(step + 1, core, mine, w, sems).wait()
        base, factor = normalise(rows[...].astype(f32))
        total = grad[...]
        small[0:1, :] = jnp.sum(total * base, 0, keepdims=True)
        small[1:2, :] = jnp.sum(total, 0, keepdims=True)
        high, low = encode(small[...])
        totals[0, :8] = high
        totals[0, 8:16] = low
        totals[0, 16:] = jnp.zeros((8, D), bf16)
        scaled = total * norms[0:1]
        first = jnp.mean(scaled, -1, keepdims=True)
        second = jnp.mean(scaled * base, -1, keepdims=True)
        back = factor * (scaled - first - base * second)
        nat[...] = back[128:640] + middle_grad[:ROWS]
        left[...] = back[:128].astype(bf16)
        right[...] = back[640:768].astype(bf16)
        globs[...] = back[768:]


def input_grad(*operands):
    return pl.pallas_call(
        input_grad_kernel,
        grid=(3,),
        in_specs=[
            SCALARS,
            whole((EXT, D)),
            pl.BlockSpec((1, EXT, D), lambda i: (i, 0, 0)),
            whole((8, D)),
            whole((640, D)),
            whole((6, 8, 512)),
            whole((8, D)),
            whole((8, 128)),
            ANY,
            ANY,
        ],
        out_specs=[
            whole((ROWS, D)),
            whole((128, D)),
            whole((128, D)),
            whole((128, D)),
            whole((1, 24, D)),
        ],
        scratch_shapes=[
            pltpu.VMEM((4, D, D), bf16),
            pltpu.SemaphoreType.DMA((4,)),
            pltpu.VMEM((EXT, D), f32),
            pltpu.VMEM((8, D), f32),
        ],
        out_shape=(
            jax.ShapeDtypeStruct((ROWS, D), f32),
            jax.ShapeDtypeStruct((128, D), bf16),
            jax.ShapeDtypeStruct((128, D), bf16),
            jax.ShapeDtypeStruct((128, D), f32),
            jax.ShapeDtypeStruct((1, 24, D), bf16),
        ),
        compiler_params=params(56),
        cost_estimate=cost(60),
        name="input_grad",
    )(*operands)


def weight_grad_kernel(place, acts, grads, wattn_grad, totals, send, keep):
    step = pl.program_id(0)
    ours = step % 2 == place[1]
    part = dot_tn(acts[...], grads[0]).reshape(32, 24, D).astype(bf16)
    chunks = pl.ds(32 * (step // 2), 32)

    @pl.when(ours)
    def _():
        keep[chunks] = part

    @pl.when(jnp.logical_not(ours))
    def _():
        send[chunks] = part

    @pl.when(step == 2)
    def _():
        send[64] = totals[0]
        keep[64] = totals[0]
        rest = wattn_grad[...].astype(f32).reshape(32, 24, D).astype(bf16)

        @pl.when(ours)
        def _():
            send[32:64] = rest

        @pl.when(jnp.logical_not(ours))
        def _():
            keep[32:64] = rest


def weight_grad(*operands):
    return pl.pallas_call(
        weight_grad_kernel,
        grid=(3,),
        in_specs=[
            SCALARS,
            whole((EXT, D)),
            pl.BlockSpec((1, EXT, D), lambda i: (i, 0, 0)),
            whole((D, D)),
            whole((1, 24, D)),
        ],
        out_specs=[whole((65, 24, D))] * 2,
        out_shape=[jax.ShapeDtypeStruct((65, 24, D), bf16)] * 2,
        compiler_params=params(48),
        cost_estimate=cost(0.1),
        name="weight_grad",
    )(*operands)


def shards(
    long_in,
    glob_in,
    cot_long,
    cot_glob,
    teacher,
    w_qkv,
    w_attn,
    w_in,
    w_out,
    norm_gains,
    norm_biases,
    rel_bias,
    lengths,
    block_order,
    global_pos,
    rel_labels,
    loss_mask,
):
    member = lax.axis_index("fsdp")
    core = member % 2
    quarter = member % 4
    seq = member // 4
    order = block_order[0]
    slots = jnp.arange(64)
    inverse = jnp.sum(jnp.where(order[None, :] == slots[:, None], slots[None, :], 0), 1)
    length = jnp.sum(jnp.where(jnp.arange(4) == seq, lengths, 0))
    anchors = lax.dynamic_slice_in_dim(global_pos, seq * GSEQ, GSEQ)

    my_ids = lax.dynamic_slice_in_dim(order, member * 4, 4)
    my_lens = jnp.sum(
        jnp.where(my_ids[:, None] // SEQ_BLOCKS == jnp.arange(4)[None, :], lengths[None, :], 0), 1
    )
    slot_pos = (my_ids % SEQ_BLOCKS)[:, None] * BLOCK + jnp.arange(BLOCK)[None, :]
    slot_weight = ((slot_pos < my_lens[:, None]).reshape(ROWS) & (loss_mask == 1)).astype(jnp.int32)
    my_count = jnp.sum(slot_weight)

    device = lax.axis_index("dp") * 16 + member
    spot = {
        "x": ((device >> 4) & 3)[None],
        "y": ((device >> 1) & 3)[None],
        "z": (((device >> 6) & 1) * 2 + ((device >> 3) & 1))[None],
    }
    counted = jnp.stack([my_count // 16, my_count % 16]).astype(bf16)
    extra = jnp.concatenate([norm_gains, norm_biases, jnp.broadcast_to(counted, (6, 2))], 1)
    extra = jnp.broadcast_to(jnp.pad(extra, ((0, 6), (0, D - 6))), (4, 12, D))
    opening = jnp.concatenate(
        [
            jnp.concatenate([w_qkv, w_attn], 1).reshape(6, 4, D).transpose(1, 0, 2),
            w_in.reshape(6, 4, D).transpose(1, 0, 2),
            extra,
            jnp.broadcast_to(jnp.concatenate([glob_in, cot_glob])[None], (4, 64, D)),
        ],
        1,
    )
    opening = exchange(opening, "fsdp", QUADS)
    spread_long = exchange(pieces(after(long_in, opening)), "fsdp")
    first = jnp.concatenate([opening[:, :6].reshape(24, D), opening[:, 12:18, :128].reshape(24, 128)], 1)
    globs = jnp.concatenate([opening[:, 24:56], opening[:, 56:]], 2).reshape(GSEQ, 2 * D)
    wout = jnp.concatenate([w_out, jnp.zeros((24, D), bf16)], 0)
    wout = lax.all_gather(wout, "fsdp", axis=0, tiled=True)
    wout = wout.reshape(16, 48, D)[:, :24].reshape(384, D)
    natural = unpieces(exchange(spread_long[inverse], "fsdp"))
    every = slice(None)
    start = quarter * ROWS
    place = jnp.stack([quarter, core]).astype(jnp.int32)
    key_pos = start - BLOCK + jnp.arange(768)
    key_ok = (key_pos >= 0) & (key_pos < length)
    glob_ok = anchors < length
    own_glob = jnp.arange(GSEQ) // 32 == quarter
    key_mask = jnp.broadcast_to(
        jnp.where(jnp.concatenate([key_ok, glob_ok]), 0.0, MASKED)[:, None], (EXT, 256)
    )
    self_mask = jnp.broadcast_to(jnp.where(glob_ok & own_glob, 0.0, MASKED)[:, None], (GSEQ, 256))
    picker = (rel_labels[:, None] == jnp.arange(LABELS)[None, :]).astype(f32)
    label_table = jnp.dot(picker, rel_bias[:LABELS], precision=HIGHEST)
    line = jnp.full((HEADS, 512), MASKED, f32)
    line = lax.dynamic_update_slice(line, label_table.T, (0, 44)).reshape(6, 2, 512)
    table = rel_bias[LABELS:]
    second = opening[:, 6:12].reshape(24, D)
    (first,) = gather_axis(
        spot["y"], first, "y", [(2, 2, 24, EXT)], lambda s: [(..., 0, (s & 1, s >> 1))], "first_y"
    )
    (second,) = gather_axis(
        spot["z"], second, "z", [(2, 2, 24, D)], lambda s: [(..., 0, (s >> 1, s & 1))], "second_z"
    )
    first, second = lax.optimization_barrier((first, second))
    (first,) = gather_axis(
        spot["z"],
        first,
        "z",
        [(2, 2, 2, 2, 24, EXT)],
        lambda s: [(..., 0, (every, s >> 1, s & 1))],
        "first_z",
    )
    (second,) = gather_axis(
        spot["y"],
        second,
        "y",
        [(2, 2, 2, 2, 24, D)],
        lambda s: [(..., 0, (s & 1, every, every, s >> 1))],
        "second_y",
    )
    first, second, natural, key_mask, self_mask, line = lax.optimization_barrier(
        (first, second, natural, key_mask, self_mask, line)
    )
    wout = lax.all_gather(after(wout, natural), "dp", axis=0, tiled=True)
    left = lax.ppermute(natural[ROWS - BLOCK :], "fsdp", TO_RIGHT)
    right = lax.ppermute(natural[:BLOCK], "fsdp", TO_LEFT)
    first = first.reshape(2, 2, 4, 24, EXT)
    parts = [first] + relay([first] * 3, "x")
    packed = jnp.concatenate(
        [
            cot_long,
            teacher,
            jnp.broadcast_to(slot_weight[:, None], (ROWS, 128)).astype(bf16),
        ],
        1,
    )
    packed = exchange(pieces(after(packed, natural)), "fsdp")
    *parts, left, right, packed = lax.optimization_barrier((*parts, left, right, packed))
    (first,) = place_parts(
        spot["x"],
        parts,
        [(2, 2, 4, 4, 24, EXT)],
        lambda s: [(..., 0, (every, every, s))],
        "first_x",
    )
    first = first.reshape(2, D, EXT)
    first_other = swap(first)
    second = after(second.reshape(2, 2, 4, 24, D), first_other)
    second_parts = [second] + relay([second] * 3, "x")
    side = first[0, :, D:].astype(f32)
    whole_count = side[:, 4] * 16.0 + side[:, 5]
    count = jnp.sum(jnp.where(jnp.arange(D) % 6 == 0, whole_count, 0.0))
    norms = jnp.pad(side[:, :4].T, ((0, 4), (0, 0)))

    packed = exchange(packed[inverse], "fsdp")
    rows, acts, proj = project(place, left, natural, right, globs, norms, first, first_other)
    long_out, long_lse, part_out, part_lse = attend(place, table, line, key_mask, self_mask, proj)

    sent = jnp.concatenate(
        [part_out, split3(part_lse.reshape(HEADS, 128)), jnp.zeros((12, 128), bf16)], 0
    )
    packed = after(packed, long_out)
    sent = jnp.broadcast_to(after(sent, packed)[None], (4, 816, 128))
    second_parts = lax.optimization_barrier((*second_parts, sent))[:-1]
    got = exchange(sent, "fsdp", QUADS)
    (second,) = place_parts(
        spot["x"],
        second_parts,
        [(2, 2, 4, 4, 24, D)],
        lambda s: [(..., 0, (every, every, s))],
        "second_x",
    )
    second = second.reshape(2, D, D)
    second_other = swap(second)

    packed = unpieces(packed)
    lses = join3(got[:, D:])
    high = jnp.max(lses, 0)
    glob_lse = high + jnp.log(jnp.sum(jnp.exp(lses - high), 0))
    shares = jnp.pad(jnp.exp(lses - glob_lse), ((0, 0), (0, 4), (0, 0)))
    glob_lse = glob_lse.reshape(6, 1, 256)

    (
        result,
        loss_sum,
        glob_out,
        grad_middle,
        grad_mixed,
        wattn_grad,
        win_send,
        win_keep,
        wout_grad,
        norm_two,
    ) = feed(
        place,
        (2.0 / count)[None],
        rows,
        long_out,
        got,
        shares,
        packed,
        globs,
        norms,
        wout,
        first,
        first_other,
        second,
        second_other,
    )
    (two,) = add_pairs([(win_keep, swap(win_send))], "add_cores")
    grads, rel = attend_back(
        place, table, line, key_mask, self_mask, proj, grad_mixed, long_lse, glob_out, glob_lse
    )
    grads, two = lax.optimization_barrier((grads, two))
    two = exchange(two.reshape(64, 24, D), BOTH, SAME_CORE)
    grad_nat, back_left, back_right, back_glob, totals = input_grad(
        place, rows, grads, norms, grad_middle, rel, norm_two, loss_sum, first, first_other
    )
    from_left = lax.ppermute(back_right, "fsdp", TO_RIGHT)
    from_right = lax.ppermute(back_left, "fsdp", TO_LEFT)
    both = pack_rows(result, grad_nat, from_left, from_right)
    one_send, one_keep = weight_grad(place, acts, grads, wattn_grad, totals)
    one_send, one_keep, two, both = lax.optimization_barrier((one_send, one_keep, two, both))
    out_grad = lax.psum_scatter(
        wout_grad.reshape(4 * D, D), "fsdp", scatter_dimension=0, tiled=True
    )
    one = scatter_axis(
        spot["x"],
        [one_keep, swap(one_send)],
        "x",
        lambda s: [(g * 4 + s) * 4 for g in range(4)],
        4,
        "one_x",
    )
    both = exchange(both, "fsdp")[order]
    out_grad = after(out_grad, both).reshape(2, 4, 24, D)
    cut = [
        lax.dynamic_index_in_dim(out_grad, spot["x"][0] ^ k, 1, keepdims=False) for k in range(4)
    ]
    out_grad = total_of([cut[0]] + relay(cut[1:], "x"))
    z_hi = spot["z"][0] >> 1
    far = lax.dynamic_index_in_dim(out_grad, 1 - z_hi, 0, keepdims=False).astype(bf16)
    near = lax.dynamic_index_in_dim(out_grad, z_hi, 0, keepdims=False)
    out_grad = near + lax.ppermute(far, BOTH, PARTNERS["z"][1]).astype(f32)
    *one, both = lax.optimization_barrier((*one, both))
    out_long, grad_long = unpack_rows(exchange(both, "fsdp"))
    two = jnp.sum(two.astype(f32), 0)
    out_glob = lax.dynamic_slice_in_dim(result, ROWS + quarter * 32, 32, 0)
    one = scatter_axis(
        spot["z"], one, "z", lambda s: [s * 2, (4 + s) * 2], 2, "one_z"
    )
    one = scatter_axis(spot["y"], one, "y", lambda s: [(s & 1) * 2 + (s >> 1)], 1, "one_y")
    one = lax.optimization_barrier((*one, out_long, out_grad))[:4]
    small = [part[1, :8].astype(f32) + part[1, 8:16].astype(f32) for part in one]
    small = (small[0] + small[1]) + (small[2] + small[3])
    one = [part[0] for part in one]
    closing = jnp.concatenate(
        [
            back_glob.reshape(4, 32, D),
            total_of(one).reshape(4, 6, D),
            two.reshape(4, 6, D),
            jnp.zeros((4, 4, D), f32),
        ],
        1,
    )
    closing = exchange(after(closing, out_long), "fsdp", QUADS)
    grad_glob = lax.dynamic_slice_in_dim(grad_middle, ROWS + quarter * 32, 32, 0) + jnp.sum(
        closing[:, :32], 0
    )
    one, two = closing[:, 32:38], closing[:, 38:44]
    qkv_grad = one[:3].transpose(1, 0, 2).reshape(6, 3 * D)
    attn_grad = one[3]
    in_grad = two.transpose(1, 0, 2).reshape(6, 4 * D)
    bands = small[4:].reshape(HEADS, 256)[:, 44 : 44 + LABELS]
    label_grad = jnp.dot(picker.T, bands.T, precision=HIGHEST)
    rel_total = jnp.concatenate([label_grad, small[4:5, :HEADS], small[4:5, HEADS : 2 * HEADS]], 0)
    loss_total = small[4, 24]
    mine_norm = lax.dynamic_slice_in_dim(small[:4], device * 6, 6, 1).T
    return (
        out_long,
        out_glob,
        loss_total / count,
        grad_long,
        grad_glob,
        qkv_grad,
        attn_grad,
        in_grad,
        out_grad,
        mine_norm[:, 0::2],
        mine_norm[:, 1::2],
        rel_total,
    )


def solution(mesh):
    rows = P(BOTH, None)
    in_specs = (rows,) * 11 + (P(), P("dp"), P("dp", None), P("dp"), P(), P(BOTH))
    out_specs = (rows, rows, P(), rows, rows, rows, rows, rows, rows, rows, rows, P())
    return jax.shard_map(shards, mesh=mesh, in_specs=in_specs, out_specs=out_specs, check_vma=False)
```

```python
import jax
import jax.numpy as jnp
from jax import lax
from jax.experimental import pallas as pl
from jax.experimental.pallas import tpu as pltpu
from jax.sharding import PartitionSpec as P

D = 768
HEADS = 12
HEAD = 64
RADIUS = 84
LABELS = 169
BLOCK = 128
SEQ_BLOCKS = 16
GLOBAL_EVERY = 16
GSEQ = 128
ROWS = 512
EXT = 896
EPS = 1e-05
MASKED = -1e30
HIGHEST = lax.Precision.HIGHEST
BOTH = ("dp", "fsdp")
f32 = jnp.float32
bf16 = jnp.bfloat16

QUADS = [[4 * i + j for j in range(4)] for i in range(4)]
SAME_CORE = [[4 * g + 2 * p + c for p in range(2) for g in range(32)] for c in range(2)]
SWAP = [(i, i ^ 1) for i in range(16)]
TO_RIGHT = [(i, i + 1) for i in range(16) if i % 4 < 3]
TO_LEFT = [(i, i - 1) for i in range(16) if i % 4 > 0]


def flip(device, axis, step):
    if axis == "x":
        return device ^ (step << 4)
    if axis == "y":
        return device ^ (step << 1)
    return device ^ ((step >> 1) << 6) ^ ((step & 1) << 3)


PARTNERS = {
    axis: [[(i, flip(i, axis, step)) for i in range(128)] for step in (1, 2, 3)] for axis in "xyz"
}


def exchange(value, axis, groups=None):
    return lax.all_to_all(value, axis, 0, 0, axis_index_groups=groups, tiled=True)


def swap(value):
    return lax.ppermute(value, "fsdp", SWAP)


def relay(values, axis):
    return [lax.ppermute(value, BOTH, pairs) for value, pairs in zip(values, PARTNERS[axis])]


def after(value, *others):
    return lax.optimization_barrier((value,) + others)[0]


ANY = pl.BlockSpec(memory_space=pl.ANY)
SCALARS = pl.BlockSpec(memory_space=pltpu.SMEM)


def cost(microseconds):
    return pl.CostEstimate(
        flops=int(microseconds * 1.1e9),
        bytes_accessed=int(microseconds * 3.6e6),
        transcendentals=0,
    )


def place_parts(spot, parts, shapes, moves, name):
    def kernel(spot_ref, *refs):
        ins, outs = refs[:4], refs[4:]
        for k in range(4):
            for source, which, target in moves(spot_ref[0] ^ k):
                outs[which][target] = ins[k][source]

    vm = pl.BlockSpec(memory_space=pltpu.VMEM)
    return pl.pallas_call(
        kernel,
        in_specs=[SCALARS] + [vm] * 4,
        out_specs=[vm] * len(shapes),
        out_shape=[jax.ShapeDtypeStruct(shape, bf16) for shape in shapes],
        compiler_params=params(32),
        cost_estimate=cost(2),
        name=name,
    )(spot, *parts)


def gather_axis(spot, value, axis, shapes, moves, name):
    return place_parts(spot, [value] + relay([value] * 3, axis), shapes, moves, name)


def encode(value):
    high = value.astype(bf16)
    return high, (value - high.astype(f32)).astype(bf16)


def fold_parts(spot, parts, starts, length, name):
    count = parts[0].shape[0] // 4 * 4
    extra = parts[0].shape[0] - count
    size = count // 4

    def kernel(spot_ref, *refs):
        ins, outs = refs[: len(parts)], refs[len(parts) :]
        for k in range(4):
            for i, start in enumerate(starts(spot_ref[0] ^ k)):
                total = ins[0][pl.ds(start, length)].astype(f32)
                for other in ins[1:]:
                    total = total + other[pl.ds(start, length)].astype(f32)
                outs[k][i * length : (i + 1) * length] = total.astype(bf16)
        if extra:
            small = [ref[count, :8].astype(f32) + ref[count, 8:16].astype(f32) for ref in ins]
            small = [small[i] + small[i + 1] for i in range(0, len(ins), 2)]
            high, low = encode(small[0] if len(small) == 1 else small[0] + small[1])
            for out in outs:
                out[size, :8] = high
                out[size, 8:16] = low
                out[size, 16:] = jnp.zeros((8, D), bf16)

    vm = pl.BlockSpec(memory_space=pltpu.VMEM)
    return pl.pallas_call(
        kernel,
        in_specs=[SCALARS] + [vm] * len(parts),
        out_specs=[vm] * 4,
        out_shape=[jax.ShapeDtypeStruct((size + extra, 24, D), bf16)] * 4,
        compiler_params=params(32),
        cost_estimate=cost(2),
        name=name,
    )(spot, *parts)


def add_pairs(pairs, name):
    def kernel(*refs):
        for i in range(len(pairs)):
            ours, theirs = refs[2 * i][...].astype(f32), refs[2 * i + 1][...].astype(f32)
            refs[2 * len(pairs) + i][...] = (ours + theirs).astype(bf16)

    block = pl.BlockSpec((384, D), lambda i: (i, 0))
    return pl.pallas_call(
        kernel,
        grid=(4,),
        in_specs=[block] * (2 * len(pairs)),
        out_specs=[block] * len(pairs),
        out_shape=[jax.ShapeDtypeStruct((2 * D, D), bf16)] * len(pairs),
        compiler_params=params(32),
        cost_estimate=cost(4),
        name=name,
    )(*[part.reshape(2 * D, D) for pair in pairs for part in pair])


def scatter_axis(spot, parts, axis, starts, length, name):
    cut = fold_parts(spot, parts, starts, length, name)
    return [cut[0]] + relay(cut[1:], axis)


def pack_rows(result, nat, from_left, from_right):
    def kernel(result_ref, nat_ref, left_ref, right_ref, out):
        for block in range(4):
            rows = slice(128 * block, 128 * block + 128)
            grad = nat_ref[rows]
            if block == 0:
                grad = grad + left_ref[...].astype(f32)
            if block == 3:
                grad = grad + right_ref[...].astype(f32)
            for piece in range(16):
                low = 8 * piece
                out[4 * piece + block, :, D:] = grad[low : low + 8].astype(bf16)
                out[4 * piece + block, :, :D] = result_ref[
                    128 * block + low : 128 * block + low + 8
                ]

    vm = pl.BlockSpec(memory_space=pltpu.VMEM)
    return pl.pallas_call(
        kernel,
        in_specs=[vm] * 4,
        out_specs=vm,
        out_shape=jax.ShapeDtypeStruct((64, 8, 2 * D), bf16),
        compiler_params=params(32),
        cost_estimate=cost(3),
        name="pack_rows",
    )(result, nat, from_left, from_right)


def unpack_rows(value):
    def kernel(value_ref, long_ref, grad_ref):
        for block in range(4):
            for piece in range(16):
                low = 128 * block + 8 * piece
                long_ref[low : low + 8] = value_ref[4 * piece + block, :, :D]
                grad_ref[low : low + 8] = value_ref[4 * piece + block, :, D:].astype(f32)

    vm = pl.BlockSpec(memory_space=pltpu.VMEM)
    return pl.pallas_call(
        kernel,
        in_specs=[vm],
        out_specs=[vm] * 2,
        out_shape=[jax.ShapeDtypeStruct((ROWS, D), bf16), jax.ShapeDtypeStruct((ROWS, D), f32)],
        compiler_params=params(32),
        cost_estimate=cost(3),
        name="unpack_rows",
    )(value)


def total_of(parts):
    total = parts[0].astype(f32)
    for part in parts[1:]:
        total = total + part.astype(f32)
    return total


def pieces(rows):
    width = rows.shape[-1]
    return rows.reshape(4, 16, 8, width).transpose(1, 0, 2, 3).reshape(64, 8, width)


def unpieces(value):
    width = value.shape[-1]
    return value.reshape(16, 4, 8, width).transpose(1, 0, 2, 3).reshape(ROWS, width)


def reorder(rows, index):
    spread = exchange(pieces(rows), "fsdp")
    return unpieces(exchange(spread[index], "fsdp"))


def split3(value):
    high = value.astype(bf16)
    rest = value - high.astype(f32)
    mid = rest.astype(bf16)
    low = (rest - mid.astype(f32)).astype(bf16)
    return jnp.concatenate([high, mid, low], 0)


def join3(value):
    value = value.astype(f32)
    return value[:, :HEADS] + value[:, HEADS : 2 * HEADS] + value[:, 2 * HEADS : 3 * HEADS]


def dot_nn(a, b):
    return lax.dot_general(a, b, (((1,), (0,)), ((), ())), preferred_element_type=f32)


def dot_nt(a, b):
    return lax.dot_general(a, b, (((1,), (1,)), ((), ())), preferred_element_type=f32)


def dot_tn(a, b):
    return lax.dot_general(a, b, (((0,), (0,)), ((), ())), preferred_element_type=f32)


def whole(shape):
    zeros = (0,) * len(shape)
    return pl.BlockSpec(shape, lambda *_: zeros, pipeline_mode=pl.Buffered(1))


def params(megabytes):
    return pltpu.CompilerParams(vmem_limit_bytes=megabytes << 20)


def normalise(values):
    centre = jnp.mean(values, -1, keepdims=True)
    centred = values - centre
    spread = jnp.mean(centred * centred, -1, keepdims=True)
    factor = lax.rsqrt(spread + EPS)
    return centred * factor, factor


def load_quarters(core, mine, other, target, sems, count):
    copies = []
    for p in range(2):
        copies.append(pltpu.make_async_copy(mine.at[p, :, pl.ds(0, D)], target.at[2 * p + core], sems.at[2 * p]))
        copies.append(
            pltpu.make_async_copy(
                other.at[p, :, pl.ds(0, D)], target.at[2 * p + 1 - core], sems.at[2 * p + 1]
            )
        )
    for copy in copies:
        copy.start()
    return copies


def quarter_copy(step, core, mine, target, sems):
    slot = 2 * (step // 2) + jnp.where(step % 2 == core, 0, 1)
    return pltpu.make_async_copy(mine.at[0, :, pl.ds(0, D)], target.at[step], sems.at[slot])


def project_kernel(
    place, left, nat, right, globs, norms, mine, other, rows_out, acts_out, proj_out, w, sems
):
    step = pl.program_id(0)
    core = place[1]

    @pl.when(step == 0)
    def _():
        load_quarters(core, mine, other, w, sems, 4)
        rows_out[:128] = left[...]
        rows_out[128:640] = nat[...]
        rows_out[640:768] = right[...]
        rows_out[768:] = globs[:, :D]
        normal, _ = normalise(rows_out[...].astype(f32))
        acts_out[...] = (normal * norms[0:1] + norms[2:3]).astype(bf16)

    quarter_copy(step, core, mine, w, sems).wait()
    proj_out[...] = dot_nn(acts_out[...], w[step]).astype(bf16)

    @pl.when(step == 2)
    def _():
        quarter_copy(step + 1, core, mine, w, sems).wait()


def project(place, left, nat, right, globs, norms, mine, other):
    return pl.pallas_call(
        project_kernel,
        grid=(3,),
        in_specs=[
            SCALARS,
            whole((128, D)),
            whole((ROWS, D)),
            whole((128, D)),
            whole((128, 2 * D)),
            whole((8, D)),
            ANY,
            ANY,
        ],
        out_specs=[
            whole((EXT, D)),
            whole((EXT, D)),
            pl.BlockSpec((EXT, D), lambda i: (0, i)),
        ],
        scratch_shapes=[pltpu.VMEM((4, D, D), bf16), pltpu.SemaphoreType.DMA((4,))],
        out_shape=(
            jax.ShapeDtypeStruct((EXT, D), bf16),
            jax.ShapeDtypeStruct((EXT, D), bf16),
            jax.ShapeDtypeStruct((EXT, 3 * D), bf16),
        ),
        compiler_params=params(50),
        cost_estimate=cost(9),
        name="project",
    )(place, left, nat, right, globs, norms, mine, other)


def stack_heads(rows):
    first = lax.broadcasted_iota(jnp.int32, rows.shape, 1) < HEAD
    zero = jnp.zeros_like(rows)
    return jnp.concatenate([jnp.where(first, rows, zero), jnp.where(first, zero, rows)], 0)


def merge_heads(value):
    first = lax.broadcasted_iota(jnp.int32, (128, 128), 0) < HEAD
    return jnp.where(first, value[:, :128], value[:, 128:]).T


def band_tile(line):
    tiles = []
    for head in range(2):
        spread = jnp.broadcast_to(line[head : head + 1], (BLOCK, 512))
        rolled = pltpu.roll(spread, 0, 1, stride=1, stride_axis=0)
        tiles.append(
            jnp.concatenate([rolled[:, 128 * i : 128 * i + 128].T for i in range(3)], 0)
        )
    return jnp.concatenate(tiles, 1)


def pair_row(first, second):
    lane = lax.broadcasted_iota(jnp.int32, (1, 256), 1)
    return jnp.where(lane < 128, first, second)


def long_owned(run):
    key = lax.broadcasted_iota(jnp.int32, (128, 256), 0)
    lane = lax.broadcasted_iota(jnp.int32, (128, 256), 1)
    return key == run + lax.shift_right_logical(lane & 127, 4)


def cross_owned(run):
    key = lax.broadcasted_iota(jnp.int32, (ROWS, 256), 0)
    lane = lax.broadcasted_iota(jnp.int32, (ROWS, 256), 1)
    return run + lax.shift_right_logical(key, 4) == (lane & 127)


def attend_kernel(
    place, table, line, key_mask, self_mask, q, k, v, out, lse, glob_out, glob_lse, band
):
    pair = pl.program_id(0)
    run = place[0] * 32
    own = pair_row(table[0, 2 * pair], table[0, 2 * pair + 1])
    other = pair_row(table[1, 2 * pair], table[1, 2 * pair + 1])
    band[...] = band_tile(line[0])
    values = v[...].T
    for j in range(4):
        low = 128 * j
        query = stack_heads(q[128 + low : 256 + low, :] * 0.125)
        near = dot_nt(k[low : low + 384, :], query) + (band[...] + key_mask[low : low + 384, :])
        far = dot_nt(k[768:, :], query) + (
            jnp.where(long_owned(run + 8 * j), own, other) + key_mask[768:, :]
        )
        top = jnp.maximum(jnp.max(near, 0, keepdims=True), jnp.max(far, 0, keepdims=True))
        near = jnp.exp(near - top)
        far = jnp.exp(far - top)
        total = jnp.sum(near, 0, keepdims=True) + jnp.sum(far, 0, keepdims=True)
        share = 1.0 / total
        got = dot_nn(values[:, low : low + 384], (near * share).astype(bf16)) + dot_nn(
            values[:, 768:], (far * share).astype(bf16)
        )
        out[low : low + 128, :] = merge_heads(got).astype(bf16)
        lse[0, j : j + 1, :] = top + jnp.log(total)
    query = stack_heads(q[768:, :] * 0.125)
    near = dot_nt(k[128:640, :], query) + (
        jnp.where(cross_owned(run), own, other) + key_mask[128:640, :]
    )
    far = dot_nt(k[768:, :], query) + self_mask[...]
    top = jnp.maximum(jnp.max(near, 0, keepdims=True), jnp.max(far, 0, keepdims=True))
    near = jnp.exp(near - top)
    far = jnp.exp(far - top)
    total = jnp.sum(near, 0, keepdims=True) + jnp.sum(far, 0, keepdims=True)
    share = 1.0 / total
    got = dot_nn(values[:, 128:640], (near * share).astype(bf16)) + dot_nn(
        values[:, 768:], (far * share).astype(bf16)
    )
    first = lax.broadcasted_iota(jnp.int32, (128, 128), 0) < HEAD
    glob_out[...] = jnp.where(first, got[:, :128], got[:, 128:]).astype(bf16)
    glob_lse[0] = top + jnp.log(total)


def column(width, offset):
    return pl.BlockSpec((width, 128), lambda h: (0, h + offset))


def attend(place, table, line, key_mask, self_mask, proj):
    return pl.pallas_call(
        attend_kernel,
        grid=(6,),
        in_specs=[
            SCALARS,
            SCALARS,
            pl.BlockSpec((1, 2, 512), lambda h: (h, 0, 0)),
            whole((EXT, 256)),
            whole((128, 256)),
            column(EXT, 0),
            column(EXT, 6),
            column(EXT, 12),
        ],
        out_specs=[
            column(ROWS, 0),
            pl.BlockSpec((1, 4, 256), lambda h: (h, 0, 0)),
            pl.BlockSpec((128, 128), lambda h: (h, 0)),
            pl.BlockSpec((1, 1, 256), lambda h: (h, 0, 0)),
        ],
        out_shape=(
            jax.ShapeDtypeStruct((ROWS, D), bf16),
            jax.ShapeDtypeStruct((6, 4, 256), f32),
            jax.ShapeDtypeStruct((D, 128), bf16),
            jax.ShapeDtypeStruct((6, 1, 256), f32),
        ),
        scratch_shapes=[pltpu.VMEM((384, 256), f32)],
        compiler_params=params(40),
        cost_estimate=cost(15),
        name="attend",
    )(place, table, line, key_mask, self_mask, proj, proj, proj)


def fold_band(tile):
    rows = jnp.concatenate([tile[128 * i : 128 * i + 128].T for i in range(3)], 1)
    rows = jnp.concatenate([rows, jnp.zeros((BLOCK, 128), f32)], 1)
    total = rows[:8]
    for a in range(1, 16):
        total = total + pltpu.roll(rows[8 * a : 8 * a + 8], 512 - 8 * a, 1)
    row = lax.broadcasted_iota(jnp.int32, (8, 512), 0)
    for bit in (1, 2, 4):
        total = jnp.where((row & bit) != 0, pltpu.roll(total, 512 - bit, 1), total)
    return jnp.sum(total, 0, keepdims=True)


def attend_back_kernel(
    place,
    table,
    line,
    key_mask,
    self_mask,
    q,
    k,
    v,
    grad,
    lse,
    glob_out,
    glob_lse,
    grads,
    rel,
    band,
    band_sum,
    key_sum,
    value_sum,
):
    pair = pl.program_id(0)
    run = place[0] * 32
    own = pair_row(table[0, 2 * pair], table[0, 2 * pair + 1])
    other = pair_row(table[1, 2 * pair], table[1, 2 * pair + 1])
    band[...] = band_tile(line[0])
    keys = k[...].T
    band_sum[...] = jnp.zeros_like(band_sum)
    key_sum[...] = jnp.zeros_like(key_sum)
    value_sum[...] = jnp.zeros_like(value_sum)
    owned_sum = jnp.zeros((1, 256), f32)
    other_sum = jnp.zeros((1, 256), f32)
    grads[0, :128] = jnp.zeros((128, 128), bf16)
    grads[0, 640:768] = jnp.zeros((128, 128), bf16)
    for j in range(4):
        low = 128 * j
        query = stack_heads(q[128 + low : 256 + low, :] * 0.125)
        back = stack_heads(grad[low : low + 128, :])
        near = dot_nt(k[low : low + 384, :], query) + (band[...] + key_mask[low : low + 384, :])
        owned = long_owned(run + 8 * j)
        far = dot_nt(k[768:, :], query) + (jnp.where(owned, own, other) + key_mask[768:, :])
        top = lse[0, j : j + 1, :]
        near = jnp.exp(near - top)
        far = jnp.exp(far - top)
        near_d = dot_nt(v[low : low + 384, :], back)
        far_d = dot_nt(v[768:, :], back)
        delta = jnp.sum(near * near_d, 0, keepdims=True) + jnp.sum(far * far_d, 0, keepdims=True)
        near_d = (near * (near_d - delta)).astype(bf16)
        far_d = (far * (far_d - delta)).astype(bf16)
        key_sum[low : low + 384, :] += dot_nn(near_d, query)
        value_sum[low : low + 384, :] += dot_nn(near.astype(bf16), back)
        key_sum[768:, :] += dot_nn(far_d, query)
        value_sum[768:, :] += dot_nn(far.astype(bf16), back)
        got = dot_nn(keys[:, low : low + 384], near_d) + dot_nn(keys[:, 768:], far_d)
        grads[0, 128 + low : 256 + low, :] = (merge_heads(got) * 0.125).astype(bf16)
        band_sum[...] += near_d.astype(f32)
        far_d = far_d.astype(f32)
        owned_sum += jnp.sum(jnp.where(owned, far_d, 0.0), 0, keepdims=True)
        other_sum += jnp.sum(jnp.where(owned, 0.0, far_d), 0, keepdims=True)
    query = stack_heads(q[768:, :] * 0.125)
    back = stack_heads(grad[ROWS:, :])
    owned = cross_owned(run)
    near = dot_nt(k[128:640, :], query) + (jnp.where(owned, own, other) + key_mask[128:640, :])
    far = dot_nt(k[768:, :], query) + self_mask[...]
    top = glob_lse[0]
    near = jnp.exp(near - top)
    far = jnp.exp(far - top)
    near_d = dot_nt(v[128:640, :], back)
    far_d = dot_nt(v[768:, :], back)
    product = grad[ROWS:, :].astype(f32).T * glob_out[...].astype(f32)
    delta = jnp.concatenate(
        [
            jnp.sum(product[:HEAD], 0, keepdims=True),
            jnp.sum(product[HEAD:], 0, keepdims=True),
        ],
        1,
    )
    near_d = (near * (near_d - delta)).astype(bf16)
    far_d = (far * (far_d - delta)).astype(bf16)
    key_sum[128:640, :] += dot_nn(near_d, query)
    value_sum[128:640, :] += dot_nn(near.astype(bf16), back)
    key_sum[768:, :] += dot_nn(far_d, query)
    value_sum[768:, :] += dot_nn(far.astype(bf16), back)
    got = dot_nn(keys[:, 128:640], near_d) + dot_nn(keys[:, 768:], far_d)
    grads[0, 768:, :] = (merge_heads(got) * 0.125).astype(bf16)
    near_d = near_d.astype(f32)
    owned_sum += jnp.sum(jnp.where(owned, near_d, 0.0), 0, keepdims=True)
    other_sum += jnp.sum(jnp.where(owned, 0.0, near_d), 0, keepdims=True)
    grads[1] = key_sum[...].astype(bf16)
    grads[2] = value_sum[...].astype(bf16)
    rel[0] = jnp.zeros((8, 512), f32)
    for head in range(2):
        lanes = slice(128 * head, 128 * head + 128)
        rel[0, head : head + 1, :] = fold_band(band_sum[:, lanes])
        rel[0, 2 + head : 3 + head, :128] = owned_sum[:, lanes]
        rel[0, 4 + head : 5 + head, :128] = other_sum[:, lanes]


def attend_back(place, table, line, key_mask, self_mask, proj, grad, lse, glob_out, glob_lse):
    return pl.pallas_call(
        attend_back_kernel,
        grid=(6,),
        in_specs=[
            SCALARS,
            SCALARS,
            pl.BlockSpec((1, 2, 512), lambda h: (h, 0, 0)),
            whole((EXT, 256)),
            whole((128, 256)),
            column(EXT, 0),
            column(EXT, 6),
            column(EXT, 12),
            column(640, 0),
            pl.BlockSpec((1, 4, 256), lambda h: (h, 0, 0)),
            pl.BlockSpec((128, 128), lambda h: (h, 0)),
            pl.BlockSpec((1, 1, 256), lambda h: (h, 0, 0)),
        ],
        out_specs=[
            pl.BlockSpec((3, EXT, 128), lambda h: (0, 0, h)),
            pl.BlockSpec((1, 8, 512), lambda h: (h, 0, 0)),
        ],
        out_shape=(
            jax.ShapeDtypeStruct((3, EXT, D), bf16),
            jax.ShapeDtypeStruct((6, 8, 512), f32),
        ),
        scratch_shapes=[
            pltpu.VMEM((384, 256), f32),
            pltpu.VMEM((384, 256), f32),
            pltpu.VMEM((EXT, 128), f32),
            pltpu.VMEM((EXT, 128), f32),
        ],
        compiler_params=params(48),
        cost_estimate=cost(21),
        name="attend_back",
    )(place, table, line, key_mask, self_mask, proj, proj, proj, grad, lse, glob_out, glob_lse)


def feed_kernel(
    place,
    coef,
    rows,
    long_out,
    parts,
    shares,
    packed,
    globs,
    norms,
    wout,
    first_mine,
    first_other,
    in_mine,
    in_other,
    result_out,
    loss_out,
    glob_out,
    middle_grad_out,
    mixed_grad_out,
    wattn_grad,
    win_send,
    win_keep,
    wout_grad,
    norm_grads,
    mixed,
    acts,
    normal,
    total,
    hidden,
    slope,
    grad_z,
    grad_acts,
    factor,
    wa,
    win,
    sem,
    sems,
):
    step = pl.program_id(0)
    core = place[1]


    def attn_copy(source):
        return pltpu.make_async_copy(source.at[1, :, pl.ds(0, D)], wa, sem)

    quarter = place[0]
    forward = step < 4
    late = jnp.maximum(step - 4, 0)
    chunk = jnp.where(
        forward, step, jnp.where(late < 2, 2 * late + 1 - core, 2 * (late - 2) + core)
    )

    def owned():
        row = lax.broadcasted_iota(jnp.int32, (640, 1), 0)
        first = ROWS + quarter * 32
        return (row < ROWS) | ((row >= first) & (row < first + 32))

    @pl.when(step == 0)
    def _():
        @pl.when(core == 1)
        def _():
            attn_copy(first_mine).start()

        @pl.when(core == 0)
        def _():
            attn_copy(first_other).start()

        load_quarters(core, in_mine, in_other, win, sems, 4)
        mixed[:ROWS] = long_out[...]
        for pair in range(6):
            sums = jnp.zeros((128, 128), f32)
            top = lax.broadcasted_iota(jnp.int32, (128, 128), 0) < HEAD
            for source in range(4):
                share = jnp.where(
                    top,
                    shares[source, 2 * pair : 2 * pair + 1, :],
                    shares[source, 2 * pair + 1 : 2 * pair + 2, :],
                )
                sums = sums + parts[source, 128 * pair : 128 * pair + 128, :].astype(f32) * share
            glob_out[128 * pair : 128 * pair + 128, :] = sums.astype(bf16)
            mixed[ROWS:, 128 * pair : 128 * pair + 128] = sums.T.astype(bf16)
        attn_copy(first_mine).wait()
        middle = dot_nn(mixed[...], wa[...])
        middle = middle + jnp.concatenate(
            [rows[128:640].astype(f32), rows[768:].astype(f32)], 0
        )
        total[...] = middle
        base, scale = normalise(middle)
        normal[...] = base
        factor[...] = scale
        acts[...] = (base * norms[1:2] + norms[3:4]).astype(bf16)
        for p in range(4):
            pltpu.make_async_copy(in_mine.at[0, :, pl.ds(0, D)], win.at[0], sems.at[p]).wait()

    @pl.when(forward)
    def _():
        inner = dot_nn(acts[...], win[chunk])
        half = 0.5 + 0.5 * lax.erf(inner * 0.7071067811865476)
        slope[chunk] = half + inner * (jnp.exp(-0.5 * inner * inner) * 0.3989422804014327)
        bits = (inner * half).astype(bf16)
        hidden[chunk] = bits
        total[...] += dot_nn(bits, wout[...])

    @pl.when(step == 3)
    def _():
        result = total[...]
        result_out[...] = result.astype(bf16)
        weight = packed[:, 2 * D : 2 * D + 1].astype(f32)
        error = result[:ROWS] - packed[:, D : 2 * D].astype(f32)
        masked = weight * error
        loss_out[...] = jnp.broadcast_to(
            jnp.sum(jnp.sum(masked * error, 0, keepdims=True), 1, keepdims=True), (8, 128)
        )
        grad = jnp.concatenate(
            [packed[:, :D].astype(f32) + coef[0] * masked, globs[:, D:].astype(f32)], 0
        )
        total[...] = grad
        grad_z[...] = grad.astype(bf16)
        grad_acts[...] = jnp.zeros_like(grad_acts)

    @pl.when(step >= 4)
    def _():
        keep_rows = owned()
        grad_inner = (dot_nt(grad_z[...], wout[...]) * slope[chunk]).astype(bf16)
        zeros = jnp.zeros_like(grad_inner)
        grad_acts[...] += dot_nt(grad_inner, win[chunk])
        part = dot_tn(acts[...], jnp.where(keep_rows, grad_inner, zeros)).astype(bf16)

        @pl.when(late < 2)
        def _():
            win_send[0] = part

        @pl.when(late >= 2)
        def _():
            win_keep[0] = part

        part = dot_tn(hidden[chunk], jnp.where(keep_rows, grad_z[...], zeros))
        part = part.reshape(2, 16, 24, D).astype(bf16)
        for i in range(2):
            wout_grad[:, i] = part[i]

    @pl.when(step == 7)
    def _():
        keep_rows = owned()
        grad = grad_acts[...]
        base = normal[...]
        mine = jnp.where(keep_rows, grad, 0.0)
        norm_grads[0:1, :] = jnp.sum(mine * base, 0, keepdims=True)
        norm_grads[1:2, :] = jnp.sum(mine, 0, keepdims=True)
        scaled = grad * norms[1:2]
        first = jnp.mean(scaled, -1, keepdims=True)
        second = jnp.mean(scaled * base, -1, keepdims=True)
        middle = total[...] + factor[...] * (scaled - first - base * second)
        middle_grad_out[...] = middle
        branch = middle.astype(bf16)
        mixed_grad_out[...] = dot_nt(branch, wa[...]).astype(bf16)
        wattn_grad[...] = dot_tn(
            mixed[...], jnp.where(keep_rows, branch, jnp.zeros_like(branch))
        ).astype(bf16)


def feed(place, coef, rows, long_out, parts, shares, packed, globs, norms, *weights):
    def chunk(t, place):
        late = jnp.maximum(t - 4, 0)
        core = place[1]
        back = jnp.where(late < 2, 2 * late + 1 - core, 2 * (late - 2) + core)
        return jnp.where(t < 4, t, back)

    def back_chunk(t, place):
        return chunk(jnp.maximum(t, 4), place)

    def fixed(shape):
        zeros = (0,) * len(shape)
        return pl.BlockSpec(shape, lambda t, place: zeros, pipeline_mode=pl.Buffered(1))

    return pl.pallas_call(
        feed_kernel,
        grid_spec=pltpu.PrefetchScalarGridSpec(
            num_scalar_prefetch=1,
            grid=(8,),
            in_specs=[
                SCALARS,
                fixed((EXT, D)),
                fixed((ROWS, D)),
                fixed((4, 816, 128)),
                fixed((4, 16, 128)),
                fixed((ROWS, 2 * D + 128)),
                fixed((128, 2 * D)),
                fixed((8, D)),
                pl.BlockSpec((D, D), lambda t, place: (chunk(t, place), 0)),
                ANY,
                ANY,
                ANY,
                ANY,
            ],
            out_specs=[
                fixed((640, D)),
                fixed((8, 128)),
                fixed((D, 128)),
                fixed((640, D)),
                fixed((640, D)),
                fixed((D, D)),
                pl.BlockSpec((1, D, D), lambda t, place: (jnp.clip(t - 4, 0, 1), 0, 0)),
                pl.BlockSpec((1, D, D), lambda t, place: (jnp.clip(t - 6, 0, 1), 0, 0)),
                pl.BlockSpec((16, 2, 24, D), lambda t, place: (0, back_chunk(t, place), 0, 0)),
                fixed((8, D)),
            ],
            scratch_shapes=[
                pltpu.VMEM((640, D), bf16),
                pltpu.VMEM((640, D), bf16),
                pltpu.VMEM((640, D), f32),
                pltpu.VMEM((640, D), f32),
                pltpu.VMEM((4, 640, D), bf16),
                pltpu.VMEM((4, 640, D), f32),
                pltpu.VMEM((640, D), bf16),
                pltpu.VMEM((640, D), f32),
                pltpu.VMEM((640, 1), f32),
                pltpu.VMEM((D, D), bf16),
                pltpu.VMEM((4, D, D), bf16),
                pltpu.SemaphoreType.DMA,
                pltpu.SemaphoreType.DMA((4,)),
            ],
        ),
        out_shape=(
            jax.ShapeDtypeStruct((640, D), bf16),
            jax.ShapeDtypeStruct((8, 128), f32),
            jax.ShapeDtypeStruct((D, 128), bf16),
            jax.ShapeDtypeStruct((640, D), f32),
            jax.ShapeDtypeStruct((640, D), bf16),
            jax.ShapeDtypeStruct((D, D), bf16),
            jax.ShapeDtypeStruct((2, D, D), bf16),
            jax.ShapeDtypeStruct((2, D, D), bf16),
            jax.ShapeDtypeStruct((16, 8, 24, D), bf16),
            jax.ShapeDtypeStruct((8, D), f32),
        ),
        compiler_params=params(60),
        cost_estimate=cost(43),
        name="feed",
    )(place, coef, rows, long_out, parts, shares, packed, globs, norms, *weights)


def input_grad_kernel(
    place, rows, grads, norms, middle_grad, rel, norm_two, loss, mine, other,
    nat, left, right, globs, totals, w, sems, grad, small,
):
    step = pl.program_id(0)
    core = place[1]

    @pl.when(step == 0)
    def _():
        load_quarters(core, mine, other, w, sems, 4)
        grad[...] = jnp.zeros_like(grad)
        small[2:4, :] = norm_two[0:2, :]
        for n in range(HEADS):
            low = 256 * (n % 3)
            small[4 + n // 3 : 5 + n // 3, low : low + 256] = rel[n // 2, n % 2 : n % 2 + 1, :256]
        lane = lax.broadcasted_iota(jnp.int32, (1, 128), 1)
        line = jnp.where(lane == 24, loss[0:1, :], small[4:5, :128])
        for n in range(2 * HEADS):
            head, row = n % HEADS, 2 + 2 * (n // HEADS)
            part = rel[head // 2, row + head % 2 : row + head % 2 + 1, :128]
            line = jnp.where(lane == n, jnp.sum(part, 1, keepdims=True), line)
        small[4:5, :128] = line

    quarter_copy(step, core, mine, w, sems).wait()
    grad[...] += dot_nt(grads[0], w[step])

    @pl.when(step == 2)
    def _():
        quarter_copy(step + 1, core, mine, w, sems).wait()
        base, factor = normalise(rows[...].astype(f32))
        total = grad[...]
        small[0:1, :] = jnp.sum(total * base, 0, keepdims=True)
        small[1:2, :] = jnp.sum(total, 0, keepdims=True)
        high, low = encode(small[...])
        totals[0, :8] = high
        totals[0, 8:16] = low
        totals[0, 16:] = jnp.zeros((8, D), bf16)
        scaled = total * norms[0:1]
        first = jnp.mean(scaled, -1, keepdims=True)
        second = jnp.mean(scaled * base, -1, keepdims=True)
        back = factor * (scaled - first - base * second)
        nat[...] = back[128:640] + middle_grad[:ROWS]
        left[...] = back[:128].astype(bf16)
        right[...] = back[640:768].astype(bf16)
        globs[...] = back[768:]


def input_grad(*operands):
    return pl.pallas_call(
        input_grad_kernel,
        grid=(3,),
        in_specs=[
            SCALARS,
            whole((EXT, D)),
            pl.BlockSpec((1, EXT, D), lambda i: (i, 0, 0)),
            whole((8, D)),
            whole((640, D)),
            whole((6, 8, 512)),
            whole((8, D)),
            whole((8, 128)),
            ANY,
            ANY,
        ],
        out_specs=[
            whole((ROWS, D)),
            whole((128, D)),
            whole((128, D)),
            whole((128, D)),
            whole((1, 24, D)),
        ],
        scratch_shapes=[
            pltpu.VMEM((4, D, D), bf16),
            pltpu.SemaphoreType.DMA((4,)),
            pltpu.VMEM((EXT, D), f32),
            pltpu.VMEM((8, D), f32),
        ],
        out_shape=(
            jax.ShapeDtypeStruct((ROWS, D), f32),
            jax.ShapeDtypeStruct((128, D), bf16),
            jax.ShapeDtypeStruct((128, D), bf16),
            jax.ShapeDtypeStruct((128, D), f32),
            jax.ShapeDtypeStruct((1, 24, D), bf16),
        ),
        compiler_params=params(56),
        cost_estimate=cost(60),
        name="input_grad",
    )(*operands)


def weight_grad_kernel(place, acts, grads, wattn_grad, totals, send, keep):
    step = pl.program_id(0)
    ours = step % 2 == place[1]
    part = dot_tn(acts[...], grads[0]).reshape(32, 24, D).astype(bf16)
    chunks = pl.ds(32 * (step // 2), 32)

    @pl.when(ours)
    def _():
        keep[chunks] = part

    @pl.when(jnp.logical_not(ours))
    def _():
        send[chunks] = part

    @pl.when(step == 2)
    def _():
        send[64] = totals[0]
        keep[64] = totals[0]
        rest = wattn_grad[...].astype(f32).reshape(32, 24, D).astype(bf16)

        @pl.when(ours)
        def _():
            send[32:64] = rest

        @pl.when(jnp.logical_not(ours))
        def _():
            keep[32:64] = rest


def weight_grad(*operands):
    return pl.pallas_call(
        weight_grad_kernel,
        grid=(3,),
        in_specs=[
            SCALARS,
            whole((EXT, D)),
            pl.BlockSpec((1, EXT, D), lambda i: (i, 0, 0)),
            whole((D, D)),
            whole((1, 24, D)),
        ],
        out_specs=[whole((65, 24, D))] * 2,
        out_shape=[jax.ShapeDtypeStruct((65, 24, D), bf16)] * 2,
        compiler_params=params(48),
        cost_estimate=cost(0.1),
        name="weight_grad",
    )(*operands)


def shards(
    long_in,
    glob_in,
    cot_long,
    cot_glob,
    teacher,
    w_qkv,
    w_attn,
    w_in,
    w_out,
    norm_gains,
    norm_biases,
    rel_bias,
    lengths,
    block_order,
    global_pos,
    rel_labels,
    loss_mask,
):
    member = lax.axis_index("fsdp")
    core = member % 2
    quarter = member % 4
    seq = member // 4
    order = block_order[0]
    slots = jnp.arange(64)
    inverse = jnp.sum(jnp.where(order[None, :] == slots[:, None], slots[None, :], 0), 1)
    length = jnp.sum(jnp.where(jnp.arange(4) == seq, lengths, 0))
    anchors = lax.dynamic_slice_in_dim(global_pos, seq * GSEQ, GSEQ)

    my_ids = lax.dynamic_slice_in_dim(order, member * 4, 4)
    my_lens = jnp.sum(
        jnp.where(my_ids[:, None] // SEQ_BLOCKS == jnp.arange(4)[None, :], lengths[None, :], 0), 1
    )
    slot_pos = (my_ids % SEQ_BLOCKS)[:, None] * BLOCK + jnp.arange(BLOCK)[None, :]
    slot_weight = ((slot_pos < my_lens[:, None]).reshape(ROWS) & (loss_mask == 1)).astype(jnp.int32)
    my_count = jnp.sum(slot_weight)

    device = lax.axis_index("dp") * 16 + member
    spot = {
        "x": ((device >> 4) & 3)[None],
        "y": ((device >> 1) & 3)[None],
        "z": (((device >> 6) & 1) * 2 + ((device >> 3) & 1))[None],
    }
    counted = jnp.stack([my_count // 16, my_count % 16]).astype(bf16)
    extra = jnp.concatenate([norm_gains, norm_biases, jnp.broadcast_to(counted, (6, 2))], 1)
    extra = jnp.broadcast_to(jnp.pad(extra, ((0, 6), (0, D - 6))), (4, 12, D))
    opening = jnp.concatenate(
        [
            jnp.concatenate([w_qkv, w_attn], 1).reshape(6, 4, D).transpose(1, 0, 2),
            w_in.reshape(6, 4, D).transpose(1, 0, 2),
            extra,
            jnp.broadcast_to(jnp.concatenate([glob_in, cot_glob])[None], (4, 64, D)),
        ],
        1,
    )
    opening = exchange(opening, "fsdp", QUADS)
    spread_long = exchange(pieces(after(long_in, opening)), "fsdp")
    first = jnp.concatenate([opening[:, :6].reshape(24, D), opening[:, 12:18, :128].reshape(24, 128)], 1)
    globs = jnp.concatenate([opening[:, 24:56], opening[:, 56:]], 2).reshape(GSEQ, 2 * D)
    wout = jnp.concatenate([w_out, jnp.zeros((24, D), bf16)], 0)
    wout = lax.all_gather(wout, "fsdp", axis=0, tiled=True)
    wout = wout.reshape(16, 48, D)[:, :24].reshape(384, D)
    natural = unpieces(exchange(spread_long[inverse], "fsdp"))
    every = slice(None)
    start = quarter * ROWS
    place = jnp.stack([quarter, core]).astype(jnp.int32)
    key_pos = start - BLOCK + jnp.arange(768)
    key_ok = (key_pos >= 0) & (key_pos < length)
    glob_ok = anchors < length
    own_glob = jnp.arange(GSEQ) // 32 == quarter
    key_mask = jnp.broadcast_to(
        jnp.where(jnp.concatenate([key_ok, glob_ok]), 0.0, MASKED)[:, None], (EXT, 256)
    )
    self_mask = jnp.broadcast_to(jnp.where(glob_ok & own_glob, 0.0, MASKED)[:, None], (GSEQ, 256))
    picker = (rel_labels[:, None] == jnp.arange(LABELS)[None, :]).astype(f32)
    label_table = jnp.dot(picker, rel_bias[:LABELS], precision=HIGHEST)
    line = jnp.full((HEADS, 512), MASKED, f32)
    line = lax.dynamic_update_slice(line, label_table.T, (0, 44)).reshape(6, 2, 512)
    table = rel_bias[LABELS:]
    second = opening[:, 6:12].reshape(24, D)
    (first,) = gather_axis(
        spot["y"], first, "y", [(2, 2, 24, EXT)], lambda s: [(..., 0, (s & 1, s >> 1))], "first_y"
    )
    (second,) = gather_axis(
        spot["z"], second, "z", [(2, 2, 24, D)], lambda s: [(..., 0, (s >> 1, s & 1))], "second_z"
    )
    first, second = lax.optimization_barrier((first, second))
    (first,) = gather_axis(
        spot["z"],
        first,
        "z",
        [(2, 2, 2, 2, 24, EXT)],
        lambda s: [(..., 0, (every, s >> 1, s & 1))],
        "first_z",
    )
    (second,) = gather_axis(
        spot["y"],
        second,
        "y",
        [(2, 2, 2, 2, 24, D)],
        lambda s: [(..., 0, (s & 1, every, every, s >> 1))],
        "second_y",
    )
    first, second, natural, key_mask, self_mask, line = lax.optimization_barrier(
        (first, second, natural, key_mask, self_mask, line)
    )
    wout = lax.all_gather(after(wout, natural), "dp", axis=0, tiled=True)
    left = lax.ppermute(natural[ROWS - BLOCK :], "fsdp", TO_RIGHT)
    right = lax.ppermute(natural[:BLOCK], "fsdp", TO_LEFT)
    first = first.reshape(2, 2, 4, 24, EXT)
    parts = [first] + relay([first] * 3, "x")
    packed = jnp.concatenate(
        [
            cot_long,
            teacher,
            jnp.broadcast_to(slot_weight[:, None], (ROWS, 128)).astype(bf16),
        ],
        1,
    )
    packed = exchange(pieces(after(packed, natural)), "fsdp")
    *parts, left, right, packed = lax.optimization_barrier((*parts, left, right, packed))
    (first,) = place_parts(
        spot["x"],
        parts,
        [(2, 2, 4, 4, 24, EXT)],
        lambda s: [(..., 0, (every, every, s))],
        "first_x",
    )
    first = first.reshape(2, D, EXT)
    first_other = swap(first)
    second = after(second.reshape(2, 2, 4, 24, D), first_other)
    second_parts = [second] + relay([second] * 3, "x")
    side = first[0, :, D:].astype(f32)
    whole_count = side[:, 4] * 16.0 + side[:, 5]
    count = jnp.sum(jnp.where(jnp.arange(D) % 6 == 0, whole_count, 0.0))
    norms = jnp.pad(side[:, :4].T, ((0, 4), (0, 0)))

    packed = exchange(packed[inverse], "fsdp")
    rows, acts, proj = project(place, left, natural, right, globs, norms, first, first_other)
    long_out, long_lse, part_out, part_lse = attend(place, table, line, key_mask, self_mask, proj)

    sent = jnp.concatenate(
        [part_out, split3(part_lse.reshape(HEADS, 128)), jnp.zeros((12, 128), bf16)], 0
    )
    packed = after(packed, long_out)
    sent = jnp.broadcast_to(after(sent, packed)[None], (4, 816, 128))
    second_parts = lax.optimization_barrier((*second_parts, sent))[:-1]
    got = exchange(sent, "fsdp", QUADS)
    (second,) = place_parts(
        spot["x"],
        second_parts,
        [(2, 2, 4, 4, 24, D)],
        lambda s: [(..., 0, (every, every, s))],
        "second_x",
    )
    second = second.reshape(2, D, D)
    second_other = swap(second)

    packed = unpieces(packed)
    lses = join3(got[:, D:])
    high = jnp.max(lses, 0)
    glob_lse = high + jnp.log(jnp.sum(jnp.exp(lses - high), 0))
    shares = jnp.pad(jnp.exp(lses - glob_lse), ((0, 0), (0, 4), (0, 0)))
    glob_lse = glob_lse.reshape(6, 1, 256)

    (
        result,
        loss_sum,
        glob_out,
        grad_middle,
        grad_mixed,
        wattn_grad,
        win_send,
        win_keep,
        wout_grad,
        norm_two,
    ) = feed(
        place,
        (2.0 / count)[None],
        rows,
        long_out,
        got,
        shares,
        packed,
        globs,
        norms,
        wout,
        first,
        first_other,
        second,
        second_other,
    )
    (two,) = add_pairs([(win_keep, swap(win_send))], "add_cores")
    grads, rel = attend_back(
        place, table, line, key_mask, self_mask, proj, grad_mixed, long_lse, glob_out, glob_lse
    )
    grads, two = lax.optimization_barrier((grads, two))
    two = exchange(two.reshape(64, 24, D), BOTH, SAME_CORE)
    grad_nat, back_left, back_right, back_glob, totals = input_grad(
        place, rows, grads, norms, grad_middle, rel, norm_two, loss_sum, first, first_other
    )
    from_left = lax.ppermute(back_right, "fsdp", TO_RIGHT)
    from_right = lax.ppermute(back_left, "fsdp", TO_LEFT)
    both = pack_rows(result, grad_nat, from_left, from_right)
    one_send, one_keep = weight_grad(place, acts, grads, wattn_grad, totals)
    one_keep, two = lax.optimization_barrier((one_keep, two))
    out_grad = lax.psum_scatter(
        wout_grad.reshape(4 * D, D), "fsdp", scatter_dimension=0, tiled=True
    )
    one = scatter_axis(
        spot["x"],
        [one_keep, swap(one_send)],
        "x",
        lambda s: [(g * 4 + s) * 4 for g in range(4)],
        4,
        "one_x",
    )
    both = exchange(after(both, two), "fsdp")[order]
    out_grad = after(out_grad, both).reshape(2, 4, 24, D)
    cut = [
        lax.dynamic_index_in_dim(out_grad, spot["x"][0] ^ k, 1, keepdims=False) for k in range(4)
    ]
    out_grad = total_of([cut[0]] + relay(cut[1:], "x"))
    z_hi = spot["z"][0] >> 1
    far = lax.dynamic_index_in_dim(out_grad, 1 - z_hi, 0, keepdims=False).astype(bf16)
    near = lax.dynamic_index_in_dim(out_grad, z_hi, 0, keepdims=False)
    out_grad = near + lax.ppermute(far, BOTH, PARTNERS["z"][1]).astype(f32)
    *one, both = lax.optimization_barrier((*one, both))
    out_long, grad_long = unpack_rows(exchange(both, "fsdp"))
    two = jnp.sum(two.astype(f32), 0)
    out_glob = lax.dynamic_slice_in_dim(result, ROWS + quarter * 32, 32, 0)
    one = scatter_axis(
        spot["z"], one, "z", lambda s: [s * 2, (4 + s) * 2], 2, "one_z"
    )
    one = scatter_axis(spot["y"], one, "y", lambda s: [(s & 1) * 2 + (s >> 1)], 1, "one_y")
    one = lax.optimization_barrier((*one, out_long, out_grad))[:4]
    small = [part[1, :8].astype(f32) + part[1, 8:16].astype(f32) for part in one]
    small = (small[0] + small[1]) + (small[2] + small[3])
    one = [part[0] for part in one]
    closing = jnp.concatenate(
        [
            back_glob.reshape(4, 32, D),
            total_of(one).reshape(4, 6, D),
            two.reshape(4, 6, D),
            jnp.zeros((4, 4, D), f32),
        ],
        1,
    )
    closing = exchange(after(closing.astype(bf16), out_long), "fsdp", QUADS).astype(f32)
    grad_glob = lax.dynamic_slice_in_dim(grad_middle, ROWS + quarter * 32, 32, 0) + jnp.sum(
        closing[:, :32], 0
    )
    one, two = closing[:, 32:38], closing[:, 38:44]
    qkv_grad = one[:3].transpose(1, 0, 2).reshape(6, 3 * D)
    attn_grad = one[3]
    in_grad = two.transpose(1, 0, 2).reshape(6, 4 * D)
    bands = small[4:].reshape(HEADS, 256)[:, 44 : 44 + LABELS]
    label_grad = jnp.dot(picker.T, bands.T, precision=HIGHEST)
    rel_total = jnp.concatenate([label_grad, small[4:5, :HEADS], small[4:5, HEADS : 2 * HEADS]], 0)
    loss_total = small[4, 24]
    mine_norm = lax.dynamic_slice_in_dim(small[:4], device * 6, 6, 1).T
    return (
        out_long,
        out_glob,
        loss_total / count,
        grad_long,
        grad_glob,
        qkv_grad,
        attn_grad,
        in_grad,
        out_grad,
        mine_norm[:, 0::2],
        mine_norm[:, 1::2],
        rel_total,
    )


def solution(mesh):
    rows = P(BOTH, None)
    in_specs = (rows,) * 11 + (P(), P("dp"), P("dp", None), P("dp"), P(), P(BOTH))
    out_specs = (rows, rows, P(), rows, rows, rows, rows, rows, rows, rows, rows, P())
    return jax.shard_map(shards, mesh=mesh, in_specs=in_specs, out_specs=out_specs, check_vma=False)
```
